128 devices in a mesh: gz: 16 (over x, y), gy: 8 (over z, core).
Axes of the slice: x: 4, y: 4, z: 4, core: 2. Of those that a mesh axis runs over, the one named last changes fastest.
Arguments:
- orbitals: bfloat16 [256, 256, 1024], P(('gz', 'gy')), may hold values from -2 to 2
- points: int32 [1024], replicated, may hold values from 0 to 262143, as said below
- coulomb: float32 [256, 1024], P(None, 'gy'), may hold values from 10 to 1000
Outputs:
- potentials: bfloat16 [256, 1024, 1024], P('gz', 'gy')
The draws below stay inside these ranges and needn't reach their ends.
Inputs may be any that keep to these rules, and one draw needn't show every extreme that they name: `points`: 1024 distinct grid cells.
All inputs are finite; a program needn't handle non-finite values.
Results may differ from the reference program's by a relative error of at most 0.0025.
Values may be sent and summed in bfloat16 or wider, within the bound.
A program may use at most 192 MiB of HBM per device.

```python
import math
import jax
import jax.numpy as jnp
from jax import lax

BANDS = 256
NPTS = 1024
NZ = 256
COL_DEV = 128
COLS = 1024
N_GY = 8


def draw_orbitals(key, part):
    shared_count = 32
    repeats = BANDS // shared_count
    field_key = jax.random.fold_in(key, 11)
    sign_key = jax.random.fold_in(key, 12)
    scale_key = jax.random.fold_in(key, 13)
    noise_key = jax.random.fold_in(key, 14)
    signs = 2.0 * jax.random.bernoulli(sign_key, 0.5, (BANDS,)).astype(jnp.float32) - 1.0
    fields = 0.25 * jax.random.normal(field_key, (shared_count, NZ, COLS), jnp.float32)
    magnitude = jax.random.uniform(scale_key, (BANDS,), jnp.float32, 0.7, 1.3)
    noise = 0.025 * jax.random.normal(noise_key, (BANDS, NZ, COLS), jnp.float32)
    amplitude = (signs * magnitude)[:, None, None]
    shared = jnp.tile(fields, (repeats, 1, 1))
    values = amplitude * shared + noise
    return jnp.clip(values, -2.0, 2.0).astype(jnp.bfloat16)


def draw_points(key, part):
    cell_total = NZ * COLS
    middle_cells = jax.random.permutation(key, cell_total - 2)[:NPTS - 2] + 1
    ends = jnp.array([0, cell_total - 1], dtype=jnp.int32)
    joined = jnp.concatenate([ends, middle_cells.astype(jnp.int32)])
    shuffle = jax.random.permutation(jax.random.fold_in(key, 3), NPTS)
    return jnp.take(joined, shuffle).astype(jnp.int32)


def steps_of(rng, dims, pieces, least, top_value):
    level = 1.0
    for axis_at, blocks in pieces:
        heights = jax.random.uniform(jax.random.fold_in(jax.random.fold_in(rng, 6), axis_at), (blocks,), jnp.float32, least / len(pieces), top_value / len(pieces))
        level = level * jnp.repeat(jnp.exp(heights), dims[axis_at] // blocks).reshape((-1,) + (1,) * (len(dims) - 1 - axis_at))
    return level


def setup_inputs(seed: int = 0) -> dict:
    key_list = jax.random.split(jax.random.key(seed), 4)
    orbitals = draw_orbitals(jax.random.fold_in(key_list[3], 71), 0)
    points = draw_points(jax.random.fold_in(key_list[3], 71), 0)
    coulomb = jnp.clip(jnp.exp(math.log(1000.0) - 4.6051702 * jax.random.uniform(key_list[2], (NZ, COLS), jnp.float32) ** steps_of(key_list[2], (NZ, COLS), ((1, 8),), -0.2, 0.2)), 10.0, 1000.0)
    return dict(orbitals=orbitals, points=points, coulomb=coulomb)


def reference(orbitals, points, coulomb):
    flattened = orbitals.reshape(BANDS, NZ * COLS)
    point_values = jnp.take(flattened, points, axis=1)
    pair_base = lax.dot_general(point_values.astype(jnp.float32), point_values.astype(jnp.float32), (((0,), (0,)), ((), ())), preferred_element_type=jnp.float32)
    pair_gram = pair_base * pair_base
    factor = jnp.linalg.cholesky(pair_gram)
    inverse = jax.scipy.linalg.cho_solve((factor, True), jnp.eye(NPTS, dtype=jnp.float32))

    def one_block(block_index):
        start = (block_index * COL_DEV).astype(jnp.int32)
        column_part = lax.dynamic_slice_in_dim(orbitals, start, COL_DEV, 2)
        kernel_part = lax.dynamic_slice_in_dim(coulomb, start, COL_DEV, 1)
        column_rows = column_part.reshape(BANDS, NZ * COL_DEV)
        sums = lax.dot_general(column_rows.astype(jnp.float32), point_values.astype(jnp.float32), (((0,), (0,)), ((), ())), preferred_element_type=jnp.float32)
        products = sums * sums
        fitted = jnp.dot(products.astype(jnp.float32), inverse.astype(jnp.float32), precision=lax.Precision.HIGHEST, preferred_element_type=jnp.float32)
        fitted = fitted.reshape(NZ, COL_DEV, NPTS)
        spectrum = jnp.fft.fft(fitted, axis=0)
        weighted = spectrum * kernel_part[:, :, None]
        potential = jnp.real(jnp.fft.ifft(weighted, axis=0))
        return potential.astype(jnp.bfloat16)
    blocks = lax.map(one_block, jnp.arange(N_GY, dtype=jnp.int32))
    return jnp.transpose(blocks, (1, 0, 2, 3)).reshape(NZ, COLS, NPTS)
```

```python
import functools
import math

import jax
import jax.numpy as jnp
from jax import lax
from jax.experimental import pallas as pl
from jax.experimental.pallas import tpu as pltpu
from jax.sharding import PartitionSpec as P

FULL = lax.Precision.HIGHEST
F32 = jnp.float32


def point_kernel(orbital_ref, points_ref, out_ref):
    bands, planes, columns = orbital_ref.shape
    points = points_ref[...]
    point_planes = points // columns
    point_columns = points - point_planes * columns
    count = points.shape[1]
    column_pick = (
        lax.broadcasted_iota(jnp.int32, (columns, count), 0) == point_columns
    ).astype(jnp.bfloat16)
    plane_pick = lax.broadcasted_iota(jnp.int32, (planes, count), 0) == point_planes
    for band in range(bands):
        picked = jnp.dot(orbital_ref[band], column_pick, preferred_element_type=F32)
        out_ref[band : band + 1, :] = jnp.sum(
            jnp.where(plane_pick, picked, 0.0), axis=0, keepdims=True
        ).astype(jnp.bfloat16)


def values_at_points(orbitals, points):
    bands = orbitals.shape[0]
    count = points.shape[0]
    return pl.pallas_call(
        point_kernel,
        out_shape=jax.ShapeDtypeStruct((bands, count), jnp.bfloat16),
        compiler_params=pltpu.CompilerParams(vmem_limit_bytes=24 << 20),
        cost_estimate=pl.CostEstimate(
            flops=2 * bands * orbitals.shape[1] * orbitals.shape[2] * count,
            bytes_accessed=orbitals.size * 2,
            transcendentals=0,
        ),
    )(orbitals, points.reshape(1, count))


def small_inverse(block):
    size = block.shape[0]
    lane = lax.broadcasted_iota(jnp.int32, (1, size), 1)
    sub = lax.broadcasted_iota(jnp.int32, (size, 1), 0)
    for j in range(size):
        row = block[j : j + 1, :]
        column = block[:, j : j + 1]
        recip = 1.0 / block[j : j + 1, j : j + 1]
        scaled = jnp.where(lane == j, recip, row * recip)
        rest = jnp.where(lane == j, 0.0, block)
        block = jnp.where(sub == j, scaled, rest - column * scaled)
    return block


def inverse_kernel(width, gram_ref, out_ref):
    size = gram_ref.shape[0]
    blocks = size // width
    dot = functools.partial(jnp.dot, precision=FULL, preferred_element_type=F32)
    out_ref[...] = gram_ref[...]

    def eliminate(k, carry):
        at = pl.ds(pl.multiple_of(k * width, width), width)
        pivot = small_inverse(out_ref[at, at])
        panel = dot(pivot, out_ref[at, :])
        out_ref[at, :] = panel

        def update(i, carry):
            @pl.when(i != k)
            def _():
                rows = pl.ds(pl.multiple_of(i * width, width), width)
                left = out_ref[rows, at]
                out_ref[rows, :] = out_ref[rows, :] - dot(left, panel)
                out_ref[rows, at] = -dot(left, pivot)

            return carry

        lax.fori_loop(0, blocks, update, 0)
        out_ref[at, at] = pivot
        return carry

    lax.fori_loop(0, blocks, eliminate, 0)


def spd_inverse(gram):
    size = gram.shape[0]
    return pl.pallas_call(
        functools.partial(inverse_kernel, 128),
        out_shape=jax.ShapeDtypeStruct(gram.shape, F32),
        compiler_params=pltpu.CompilerParams(vmem_limit_bytes=24 << 20),
        cost_estimate=pl.CostEstimate(
            flops=60 * size**3, bytes_accessed=8 * size * size, transcendentals=0
        ),
    )(gram)


def circulants(kernel):
    planes = kernel.shape[0]
    positions = jnp.arange(planes, dtype=jnp.int32)
    angles = (
        2.0 * math.pi / planes
    ) * (positions[:, None] * positions[None, :] % planes).astype(F32)
    waves = jnp.concatenate([jnp.cos(angles), jnp.sin(angles)], axis=1)
    weights = jnp.concatenate([kernel, kernel], axis=0).T / planes
    return lax.dot_general(
        waves[None] * weights[:, None, :],
        jnp.broadcast_to(waves, (weights.shape[0],) + waves.shape),
        (((2,), (2,)), ((0,), (0,))),
        precision=FULL,
        preferred_element_type=F32,
    )


def per_device(orbitals, points, coulomb):
    gz_count = lax.axis_size("gz")
    col_pencil = coulomb.shape[1] // gz_count
    at_points = lax.all_gather(
        values_at_points(orbitals, points), ("gz", "gy"), axis=0, tiled=True
    )
    blocks = lax.all_to_all(orbitals, "gy", split_axis=2, concat_axis=0, tiled=True)
    pencils = lax.all_to_all(
        jnp.transpose(blocks, (2, 0, 1)), "gz", split_axis=0, concat_axis=1, tiled=True
    )
    pair_base = lax.dot_general(
        at_points, at_points, (((0,), (0,)), ((), ())), preferred_element_type=F32
    )
    inverse = spd_inverse(pair_base * pair_base)
    sums = lax.dot_general(
        pencils, at_points, (((1,), (0,)), ((), ())), preferred_element_type=F32
    )
    kernel = lax.dynamic_slice_in_dim(coulomb, lax.axis_index("gz") * col_pencil, col_pencil, 1)
    smoothed = lax.dot_general(
        circulants(kernel),
        sums * sums,
        (((2,), (1,)), ((0,), (0,))),
        precision=lax.Precision.HIGH,
        preferred_element_type=F32,
    )
    slab = lax.all_to_all(smoothed, "gz", split_axis=1, concat_axis=0, tiled=True)
    slab = jnp.transpose(slab, (1, 0, 2))
    return lax.dot_general(
        slab,
        inverse,
        (((2,), (0,)), ((), ())),
        precision=lax.Precision.HIGH,
        preferred_element_type=F32,
    ).astype(jnp.bfloat16)


def solution(mesh):
    return jax.shard_map(
        per_device,
        mesh=mesh,
        in_specs=(P(("gz", "gy"), None, None), P(), P(None, "gy")),
        out_specs=P("gz", "gy", None),
        check_vma=False,
    )
```

```python
import functools

import jax
import jax.numpy as jnp
import numpy as np
from jax import lax
from jax.experimental import pallas as pl
from jax.experimental.pallas import tpu as pltpu
from jax.sharding import PartitionSpec as P

FULL = lax.Precision.HIGHEST
F32 = jnp.float32
BF16 = jnp.bfloat16
EARLY = 8


def point_kernel(orbital_ref, points_ref, out_ref):
    bands, planes, columns = orbital_ref.shape
    points = points_ref[...]
    point_planes = points // columns
    point_columns = points - point_planes * columns
    count = points.shape[1]
    column_pick = (
        lax.broadcasted_iota(jnp.int32, (columns, count), 0) == point_columns
    ).astype(jnp.bfloat16)
    plane_pick = lax.broadcasted_iota(jnp.int32, (planes, count), 0) == point_planes
    for band in range(bands):
        picked = jnp.dot(orbital_ref[band], column_pick, preferred_element_type=F32)
        out_ref[band : band + 1, :] = jnp.sum(
            jnp.where(plane_pick, picked, 0.0), axis=0, keepdims=True
        ).astype(jnp.bfloat16)


def values_at_points(orbitals, points):
    bands = orbitals.shape[0]
    count = points.shape[0]
    return pl.pallas_call(
        point_kernel,
        out_shape=jax.ShapeDtypeStruct((bands, count), jnp.bfloat16),
        compiler_params=pltpu.CompilerParams(vmem_limit_bytes=24 << 20),
        cost_estimate=pl.CostEstimate(
            flops=2 * bands * orbitals.shape[1] * orbitals.shape[2] * count,
            bytes_accessed=orbitals.size * 2,
            transcendentals=0,
        ),
    )(orbitals, points.reshape(1, count))


def split_parts(values, count):
    parts = []
    for _ in range(count):
        part = values.astype(BF16)
        parts.append(part)
        values = values - part.astype(F32)
    return parts


def full_dot(left, right):
    high, middle, low = split_parts(left, 3)
    wide = jnp.concatenate([high, high, middle, high, low, middle], axis=1)
    return jnp.dot(wide, full_stack(right), preferred_element_type=F32)


def full_stack(right):
    high, middle, low = split_parts(right, 3)
    return jnp.concatenate([high, middle, high, low, high, middle], axis=0)


def tree_sum(terms):
    while len(terms) > 1:
        terms = [sum(terms[i : i + 2][1:], terms[i]) for i in range(0, len(terms), 2)]
    return terms[0]


def eliminate_rows(rows, first, lane, sub):
    shape = rows.shape
    columns = [jnp.broadcast_to(rows[:, first + j : first + j + 1], shape) for j in range(8)]
    cell = {
        (i, j): jnp.broadcast_to(columns[j][i : i + 1, :], shape)
        for j in range(8)
        for i in range(j + 1)
    }
    for k in range(8):
        recip = 1.0 / cell[k, k]
        side = {i: cell[min(i, k), max(i, k)] for i in range(8) if i != k}
        scaled = {i: side[i] * recip for i in side}
        swept = {}
        for i, j in cell:
            if i == k and j == k:
                swept[i, j] = -recip
            elif i == k or j == k:
                swept[i, j] = scaled[j if i == k else i]
            else:
                swept[i, j] = cell[i, j] - side[i] * scaled[j]
        cell = swept
    inside = (lane >= first) & (lane < first + 8)
    source = [
        jnp.where(
            inside,
            jnp.where(lane == first + j, -1.0, 0.0),
            -jnp.broadcast_to(rows[j : j + 1, :], shape),
        )
        for j in range(8)
    ]
    results = [
        tree_sum([cell[min(i, j), max(i, j)] * source[j] for j in range(8)]) for i in range(8)
    ]
    panel = results[0]
    for i in range(1, 8):
        panel = jnp.where(sub == i, results[i], panel)
    return results, panel, inside


def small_inverse(block):
    size = block.shape[0]
    group_rows = 32
    tiles = [block[i : i + 8, :] for i in range(0, size, 8)]
    lane = lax.broadcasted_iota(jnp.int32, (8, size), 1)
    sub = lax.broadcasted_iota(jnp.int32, (8, size), 0)
    per_group = group_rows // 8
    for start in range(0, size, group_rows):
        group = list(range(start // 8, start // 8 + per_group))
        for at in group:
            results, panel, inside = eliminate_rows(tiles[at], at * 8, lane, sub)
            for step in range(1, per_group):
                other = group[(at - group[0] + step) % per_group]
                terms = [
                    jnp.broadcast_to(tiles[other][:, at * 8 + j : at * 8 + j + 1], (8, size))
                    * results[j]
                    for j in range(8)
                ]
                tiles[other] = jnp.where(inside, 0.0, tiles[other]) - tree_sum(terms)
            tiles[at] = panel
        rest = [i for i in range(len(tiles)) if i not in group]
        panel = jnp.concatenate([tiles[i] for i in group], axis=0)
        stack = jnp.concatenate([tiles[i] for i in rest], axis=0)
        change = full_dot(stack[:, start : start + group_rows], panel)
        wide_lane = lax.broadcasted_iota(jnp.int32, stack.shape, 1)
        in_group = (wide_lane >= start) & (wide_lane < start + group_rows)
        stack = jnp.where(in_group, 0.0, stack) - change
        for place, i in enumerate(rest):
            tiles[i] = stack[place * 8 : place * 8 + 8, :]
    return jnp.concatenate(tiles, axis=0)


def inverse_kernel(width, point_ref, high_ref, low_ref, work):
    size = work.shape[0]
    row_block = 256
    for first in range(0, size, row_block):
        base = lax.dot_general(
            point_ref[:, first : first + row_block],
            point_ref[...],
            (((0,), (0,)), ((), ())),
            preferred_element_type=F32,
        )
        work[first : first + row_block, :] = base * base

    def eliminate(k, carry):
        at = pl.ds(pl.multiple_of(k * width, width), width)
        pivot = small_inverse(work[at, at])
        work[at, :] = full_dot(pivot, work[at, :])
        work[at, at] = pivot
        panel = work[at, :]
        stacked = full_stack(panel)
        for first in range(0, size, row_block):
            rows = slice(first, first + row_block)
            high, middle, low = split_parts(work[rows, at], 3)
            wide = jnp.concatenate([high, high, middle, high, low, middle], axis=1)
            change = jnp.dot(wide, stacked, preferred_element_type=F32)
            work[rows, at] = jnp.zeros((row_block, width), F32)
            work[rows, :] = work[rows, :] - change
        work[at, :] = panel
        return carry

    lax.fori_loop(0, size // width, eliminate, 0)
    for first in range(0, size, row_block):
        rows = slice(first, first + row_block)
        high, low = split_parts(work[rows, :], 2)
        high_ref[rows, :] = high
        low_ref[rows, :] = low


def gram_inverse(at_points):
    size = at_points.shape[1]
    part = jax.ShapeDtypeStruct((size, size), BF16)
    return pl.pallas_call(
        functools.partial(inverse_kernel, 128),
        out_shape=(part, part),
        scratch_shapes=[pltpu.VMEM((size, size), F32)],
        compiler_params=pltpu.CompilerParams(vmem_limit_bytes=28 << 20),
        cost_estimate=pl.CostEstimate(
            flops=60 * size**3, bytes_accessed=8 * size * size, transcendentals=0
        ),
    )(at_points)


def filter_kernel(pencil_ref, point_ref, weight_ref, wave_ref, early_ref, late_ref, circulant):
    col_count, _, planes = pencil_ref.shape
    slabs, early, _, width = early_ref.shape
    late = late_ref.shape[1]

    @pl.when(pl.program_id(0) == 0)
    def _():
        rows = jnp.dot(
            weight_ref[...], wave_ref[...], precision=FULL, preferred_element_type=F32
        ) * (1.0 / planes)
        for c in range(col_count):
            turned = pltpu.roll(
                jnp.broadcast_to(rows[c : c + 1, :], (planes, planes)),
                0,
                1,
                stride=1,
                stride_axis=0,
            )
            high, low = split_parts(turned, 2)
            circulant[c] = jnp.concatenate([high, high, low], axis=1)

    for c in range(col_count):
        sums = lax.dot_general(
            pencil_ref[c], point_ref[...], (((0,), (0,)), ((), ())), preferred_element_type=F32
        )
        high, low = split_parts(sums * sums, 2)
        smooth = jnp.dot(
            circulant[c], jnp.concatenate([high, low, high], axis=0), preferred_element_type=F32
        ).reshape(slabs, early + late, width)
        early_ref[:, :, c, :] = smooth[:, :early]
        late_ref[:, :, c, :] = smooth[:, early:]


def filtered_products(pencils, at_points, weights, slabs, early):
    col_count, bands, planes = pencils.shape
    count = at_points.shape[1]
    late = planes // slabs - early
    angles = 2.0 * np.pi / planes * (np.arange(planes)[:, None] * np.arange(planes) % planes)
    waves = jnp.asarray(np.cos(angles), F32)
    chunk = 256
    return pl.pallas_call(
        filter_kernel,
        grid=(count // chunk,),
        in_specs=[
            pl.BlockSpec(pencils.shape, lambda i: (0, 0, 0)),
            pl.BlockSpec((bands, chunk), lambda i: (0, i)),
            pl.BlockSpec(weights.shape, lambda i: (0, 0)),
            pl.BlockSpec(waves.shape, lambda i: (0, 0)),
        ],
        out_specs=[
            pl.BlockSpec((slabs, early, col_count, chunk), lambda i: (0, 0, 0, i)),
            pl.BlockSpec((slabs, late, col_count, chunk), lambda i: (0, 0, 0, i)),
        ],
        out_shape=[
            jax.ShapeDtypeStruct((slabs, early, col_count, count), F32),
            jax.ShapeDtypeStruct((slabs, late, col_count, count), F32),
        ],
        scratch_shapes=[pltpu.VMEM((col_count, planes, 3 * planes), BF16)],
        compiler_params=pltpu.CompilerParams(vmem_limit_bytes=28 << 20),
        cost_estimate=pl.CostEstimate(
            flops=8 * col_count * planes * bands * count, bytes_accessed=10 << 20, transcendentals=0
        ),
    )(pencils, at_points, weights, waves)


def fit_rows(rows, high_ref, low_ref):
    high, low = split_parts(rows, 2)
    dot = functools.partial(jnp.dot, preferred_element_type=F32)
    return (
        dot(high, high_ref[...]) + (dot(low, high_ref[...]) + dot(high, low_ref[...]))
    ).astype(BF16)


def late_fit_kernel(rows_ref, high_ref, low_ref, out_ref):
    out_ref[...] = fit_rows(rows_ref[...], high_ref, low_ref)


def late_fit(rows, high, low):
    total, count = rows.shape
    block = 256
    whole = pl.BlockSpec((count, count), lambda i: (0, 0))
    return pl.pallas_call(
        late_fit_kernel,
        grid=(total // block,),
        in_specs=[pl.BlockSpec((block, count), lambda i: (i, 0)), whole, whole],
        out_specs=pl.BlockSpec((block, count), lambda i: (i, 0)),
        out_shape=jax.ShapeDtypeStruct(rows.shape, BF16),
        compiler_params=pltpu.CompilerParams(vmem_limit_bytes=24 << 20),
        cost_estimate=pl.CostEstimate(
            flops=6 * total * count * count, bytes_accessed=10 << 20, transcendentals=0
        ),
    )(rows, high, low)


def early_fit_kernel(rows_ref, high_ref, low_ref, out_ref):
    planes, cols, count = out_ref.shape
    rows = jnp.concatenate(
        [rows_ref[:, z].reshape(cols, count) for z in range(planes)], axis=0
    )
    out_ref[...] = fit_rows(rows, high_ref, low_ref).reshape(planes, cols, count)


def early_fit(slab, high, low, total_planes):
    sources, early, col_count, count = slab.shape
    block = 2
    whole = pl.BlockSpec((count, count), lambda i: (0, 0))
    return pl.pallas_call(
        early_fit_kernel,
        grid=(early // block,),
        in_specs=[
            pl.BlockSpec((sources, block, col_count, count), lambda i: (0, i, 0, 0)),
            whole,
            whole,
        ],
        out_specs=pl.BlockSpec((block, sources * col_count, count), lambda i: (i, 0, 0)),
        out_shape=jax.ShapeDtypeStruct((total_planes, sources * col_count, count), BF16),
        compiler_params=pltpu.CompilerParams(vmem_limit_bytes=24 << 20),
        cost_estimate=pl.CostEstimate(
            flops=6 * slab.size * count, bytes_accessed=10 << 20, transcendentals=0
        ),
    )(slab, high, low)


def place_late_kernel(late_ref, _, out_ref):
    planes, cols, count = out_ref.shape
    for z in range(planes):
        out_ref[z] = late_ref[:, z].astype(F32).reshape(cols, count).astype(BF16)


def place_late(late, fitted):
    sources, planes, col_count, count = late.shape
    block = 2
    first = (fitted.shape[0] - planes) // block
    return pl.pallas_call(
        place_late_kernel,
        grid=(planes // block,),
        in_specs=[
            pl.BlockSpec((sources, block, col_count, count), lambda i: (0, i, 0, 0)),
            pl.BlockSpec(memory_space=pl.ANY),
        ],
        out_specs=pl.BlockSpec((block, sources * col_count, count), lambda i: (first + i, 0, 0)),
        out_shape=jax.ShapeDtypeStruct(fitted.shape, BF16),
        input_output_aliases={1: 0},
        compiler_params=pltpu.CompilerParams(vmem_limit_bytes=12 << 20),
        cost_estimate=pl.CostEstimate(flops=0, bytes_accessed=2 * late.size * 2, transcendentals=0),
    )(late, fitted)


def per_device(orbitals, points, coulomb):
    gz_count = lax.axis_size("gz")
    planes, columns = coulomb.shape
    col_pencil = columns // gz_count
    count = points.shape[0]
    slab_planes = planes // gz_count
    early = EARLY
    blocks = lax.all_to_all(orbitals, "gy", split_axis=2, concat_axis=0, tiled=True)
    pencils = lax.all_to_all(
        jnp.transpose(blocks, (2, 0, 1)), "gz", split_axis=0, concat_axis=1, tiled=True
    )
    at_points = lax.all_gather(
        values_at_points(orbitals, points), ("gz", "gy"), axis=0, tiled=True
    )
    weights = lax.dynamic_slice_in_dim(
        coulomb, lax.axis_index("gz") * col_pencil, col_pencil, 1
    ).T
    first, second = filtered_products(pencils, at_points, weights, gz_count, early)
    swap = functools.partial(
        lax.all_to_all, axis_name="gz", split_axis=0, concat_axis=0, tiled=True
    )
    slab = swap(first)
    high, low = gram_inverse(at_points)
    late = late_fit(second.reshape(-1, count), high, low)
    late = swap(late.reshape(gz_count, slab_planes - early, col_pencil, count))
    return place_late(late, early_fit(slab, high, low, slab_planes))


def solution(mesh):
    return jax.shard_map(
        per_device,
        mesh=mesh,
        in_specs=(P(("gz", "gy"), None, None), P(), P(None, "gy")),
        out_specs=P("gz", "gy", None),
        check_vma=False,
    )
```

```python
import functools

import jax
import jax.numpy as jnp
import numpy as np
from jax import lax
from jax.experimental import pallas as pl
from jax.experimental.pallas import tpu as pltpu
from jax.sharding import PartitionSpec as P

FULL = lax.Precision.HIGHEST
F32 = jnp.float32
BF16 = jnp.bfloat16
EARLY = 8


def pick_points(orbital_ref, points_ref, out_ref):
    bands, planes, columns = orbital_ref.shape
    points = points_ref[...]
    point_planes = points // columns
    point_columns = points - point_planes * columns
    count = points.shape[1]
    column_pick = (
        lax.broadcasted_iota(jnp.int32, (columns, count), 0) == point_columns
    ).astype(BF16)
    plane_pick = lax.broadcasted_iota(jnp.int32, (planes, count), 0) == point_planes
    for band in range(bands):
        picked = jnp.dot(orbital_ref[band], column_pick, preferred_element_type=F32)
        out_ref[band : band + 1, :] = jnp.sum(
            jnp.where(plane_pick, picked, 0.0), axis=0, keepdims=True
        ).astype(BF16)


def send(source, target, send_sem, recv_sem, device):
    copy = pltpu.make_async_remote_copy(
        src_ref=source,
        dst_ref=target,
        send_sem=send_sem,
        recv_sem=recv_sem,
        device_id=device,
        device_id_type=pl.DeviceIdType.MESH,
    )
    copy.start()
    return copy


def exchange_kernel(
    gz_count,
    gy_count,
    orbital_ref,
    points_ref,
    pencil_ref,
    value_ref,
    own_blocks,
    row_blocks,
    own_values,
    gy_value_sems,
    gz_value_sems,
    gy_block_sems,
    gz_block_sems,
    local_sems,
):
    gz, gy = lax.axis_index("gz"), lax.axis_index("gy")
    gy_peers = [lax.rem(gy + d, gy_count) for d in range(1, gy_count)]
    gz_peers = [lax.rem(gz + d, gz_count) for d in range(1, gz_count)]
    barrier = pltpu.get_barrier_semaphore()
    for device in [(gz, peer) for peer in gy_peers] + [(peer, gy) for peer in gz_peers]:
        pl.semaphore_signal(
            barrier, inc=1, device_id=device, device_id_type=pl.DeviceIdType.MESH
        )
    pick_points(orbital_ref, points_ref, own_values)
    pl.semaphore_wait(barrier, gy_count + gz_count - 2)

    own_value_copy = pltpu.make_async_copy(own_values, value_ref.at[gz, gy], local_sems.at[0])
    own_value_copy.start()
    gy_values = [
        send(
            own_values, value_ref.at[gz, gy], gy_value_sems.at[0, i], gy_value_sems.at[1, i], (gz, peer)
        )
        for i, peer in enumerate(gy_peers)
    ]

    bands, planes, columns = orbital_ref.shape
    _, _, cols, _ = own_blocks.shape
    width = 256
    for band in range(bands):
        for first in range(0, columns, width):
            turned = orbital_ref[band, :, first : first + width].astype(F32).T
            own_blocks[first // cols : (first + width) // cols, band] = turned.reshape(
                width // cols, cols, planes
            ).astype(BF16)
    own_rows = pltpu.make_async_copy(
        own_blocks.at[pl.ds(gy * gz_count, gz_count)], row_blocks.at[gy], local_sems.at[1]
    )
    own_rows.start()
    gy_blocks = [
        send(
            own_blocks.at[pl.ds(peer * gz_count, gz_count)],
            row_blocks.at[gy],
            gy_block_sems.at[0, i],
            gy_block_sems.at[1, i],
            (gz, peer),
        )
        for i, peer in enumerate(gy_peers)
    ]

    own_value_copy.wait()
    for copy in gy_values:
        copy.wait_recv()
    gz_values = [
        send(
            value_ref.at[gz], value_ref.at[gz], gz_value_sems.at[0, i], gz_value_sems.at[1, i], (peer, gy)
        )
        for i, peer in enumerate(gz_peers)
    ]
    own_rows.wait()
    for copy in gy_blocks:
        copy.wait_recv()
    gz_blocks = [
        send(
            row_blocks.at[:, peer],
            pencil_ref.at[gz],
            gz_block_sems.at[0, i],
            gz_block_sems.at[1, i],
            (peer, gy),
        )
        for i, peer in enumerate(gz_peers)
    ]
    own_pencil = pltpu.make_async_copy(row_blocks.at[:, gz], pencil_ref.at[gz], local_sems.at[2])
    own_pencil.start()
    own_pencil.wait()
    for copy in gy_values + gy_blocks:
        copy.wait_send()
    for copy in gz_values + gz_blocks:
        copy.wait()


def exchange(orbitals, points, gz_count, gy_count, cols):
    bands, planes, columns = orbitals.shape
    count = points.shape[0]
    vmem = pl.BlockSpec(memory_space=pltpu.VMEM)
    dma = pltpu.SemaphoreType.DMA
    return pl.pallas_call(
        functools.partial(exchange_kernel, gz_count, gy_count),
        in_specs=[vmem, vmem],
        out_specs=(vmem, vmem),
        out_shape=(
            jax.ShapeDtypeStruct((gz_count, gy_count, bands, cols, planes), BF16),
            jax.ShapeDtypeStruct((gz_count, gy_count, bands, count), BF16),
        ),
        scratch_shapes=[
            pltpu.VMEM((columns // cols, bands, cols, planes), BF16),
            pltpu.VMEM((gy_count, gz_count, bands, cols, planes), BF16),
            pltpu.VMEM((bands, count), BF16),
            dma((2, gy_count - 1)),
            dma((2, gz_count - 1)),
            dma((2, gy_count - 1)),
            dma((2, gz_count - 1)),
            dma((3,)),
        ],
        compiler_params=pltpu.CompilerParams(
            collective_id=0, has_side_effects=True, vmem_limit_bytes=24 << 20
        ),
    )(orbitals, points.reshape(1, count))


def split_parts(values, count):
    parts = []
    for _ in range(count):
        part = values.astype(BF16)
        parts.append(part)
        values = values - part.astype(F32)
    return parts


def full_dot(left, right):
    high, middle, low = split_parts(left, 3)
    wide = jnp.concatenate([high, high, middle, high, low, middle], axis=1)
    return jnp.dot(wide, full_stack(right), preferred_element_type=F32)


def full_stack(right):
    high, middle, low = split_parts(right, 3)
    return jnp.concatenate([high, middle, high, low, high, middle], axis=0)


def tree_sum(terms):
    while len(terms) > 1:
        terms = [sum(terms[i : i + 2][1:], terms[i]) for i in range(0, len(terms), 2)]
    return terms[0]


def eliminate_rows(rows, first, lane, sub):
    shape = rows.shape
    columns = [jnp.broadcast_to(rows[:, first + j : first + j + 1], shape) for j in range(8)]
    cell = {
        (i, j): jnp.broadcast_to(columns[j][i : i + 1, :], shape)
        for j in range(8)
        for i in range(j + 1)
    }
    for k in range(8):
        recip = 1.0 / cell[k, k]
        side = {i: cell[min(i, k), max(i, k)] for i in range(8) if i != k}
        scaled = {i: side[i] * recip for i in side}
        swept = {}
        for i, j in cell:
            if i == k and j == k:
                swept[i, j] = -recip
            elif i == k or j == k:
                swept[i, j] = scaled[j if i == k else i]
            else:
                swept[i, j] = cell[i, j] - side[i] * scaled[j]
        cell = swept
    inside = (lane >= first) & (lane < first + 8)
    source = [
        jnp.where(
            inside,
            jnp.where(lane == first + j, -1.0, 0.0),
            -jnp.broadcast_to(rows[j : j + 1, :], shape),
        )
        for j in range(8)
    ]
    results = [
        tree_sum([cell[min(i, j), max(i, j)] * source[j] for j in range(8)]) for i in range(8)
    ]
    panel = results[0]
    for i in range(1, 8):
        panel = jnp.where(sub == i, results[i], panel)
    return results, panel, inside


def small_inverse(block):
    size = block.shape[0]
    group_rows = 32
    tiles = [block[i : i + 8, :] for i in range(0, size, 8)]
    lane = lax.broadcasted_iota(jnp.int32, (8, size), 1)
    sub = lax.broadcasted_iota(jnp.int32, (8, size), 0)
    per_group = group_rows // 8
    for start in range(0, size, group_rows):
        group = list(range(start // 8, start // 8 + per_group))
        for at in group:
            results, panel, inside = eliminate_rows(tiles[at], at * 8, lane, sub)
            for step in range(1, per_group):
                other = group[(at - group[0] + step) % per_group]
                terms = [
                    jnp.broadcast_to(tiles[other][:, at * 8 + j : at * 8 + j + 1], (8, size))
                    * results[j]
                    for j in range(8)
                ]
                tiles[other] = jnp.where(inside, 0.0, tiles[other]) - tree_sum(terms)
            tiles[at] = panel
        rest = [i for i in range(len(tiles)) if i not in group]
        panel = jnp.concatenate([tiles[i] for i in group], axis=0)
        stack = jnp.concatenate([tiles[i] for i in rest], axis=0)
        change = full_dot(stack[:, start : start + group_rows], panel)
        wide_lane = lax.broadcasted_iota(jnp.int32, stack.shape, 1)
        in_group = (wide_lane >= start) & (wide_lane < start + group_rows)
        stack = jnp.where(in_group, 0.0, stack) - change
        for place, i in enumerate(rest):
            tiles[i] = stack[place * 8 : place * 8 + 8, :]
    return jnp.concatenate(tiles, axis=0)


def inverse_kernel(width, point_ref, high_ref, low_ref, work):
    size = work.shape[0]
    row_block = 256
    for first in range(0, size, row_block):
        base = lax.dot_general(
            point_ref[:, first : first + row_block],
            point_ref[...],
            (((0,), (0,)), ((), ())),
            preferred_element_type=F32,
        )
        work[first : first + row_block, :] = base * base

    def eliminate(k, carry):
        at = pl.ds(pl.multiple_of(k * width, width), width)
        pivot = small_inverse(work[at, at])
        work[at, :] = full_dot(pivot, work[at, :])
        work[at, at] = pivot
        panel = work[at, :]
        stacked = full_stack(panel)
        for first in range(0, size, row_block):
            rows = slice(first, first + row_block)
            high, middle, low = split_parts(work[rows, at], 3)
            wide = jnp.concatenate([high, high, middle, high, low, middle], axis=1)
            change = jnp.dot(wide, stacked, preferred_element_type=F32)
            work[rows, at] = jnp.zeros((row_block, width), F32)
            work[rows, :] = work[rows, :] - change
        work[at, :] = panel
        return carry

    lax.fori_loop(0, size // width, eliminate, 0)
    for first in range(0, size, row_block):
        rows = slice(first, first + row_block)
        high, low = split_parts(work[rows, :], 2)
        high_ref[rows, :] = high
        low_ref[rows, :] = low


def gram_inverse(at_points):
    size = at_points.shape[1]
    part = jax.ShapeDtypeStruct((size, size), BF16)
    return pl.pallas_call(
        functools.partial(inverse_kernel, 128),
        out_shape=(part, part),
        scratch_shapes=[pltpu.VMEM((size, size), F32)],
        compiler_params=pltpu.CompilerParams(vmem_limit_bytes=28 << 20),
        cost_estimate=pl.CostEstimate(
            flops=60 * size**3, bytes_accessed=8 * size * size, transcendentals=0
        ),
    )(at_points)


def filter_kernel(pencil_ref, point_ref, weight_ref, wave_ref, early_ref, late_ref, circulant):
    col_count, _, planes = pencil_ref.shape
    slabs, early, _, width = early_ref.shape
    late = late_ref.shape[1]

    @pl.when(pl.program_id(0) == 0)
    def _():
        rows = jnp.dot(
            weight_ref[...], wave_ref[...], precision=FULL, preferred_element_type=F32
        ) * (1.0 / planes)
        for c in range(col_count):
            turned = pltpu.roll(
                jnp.broadcast_to(rows[c : c + 1, :], (planes, planes)),
                0,
                1,
                stride=1,
                stride_axis=0,
            )
            high, low = split_parts(turned, 2)
            circulant[c] = jnp.concatenate([high, high, low], axis=1)

    for c in range(col_count):
        sums = lax.dot_general(
            pencil_ref[c], point_ref[...], (((0,), (0,)), ((), ())), preferred_element_type=F32
        )
        high, low = split_parts(sums * sums, 2)
        smooth = jnp.dot(
            circulant[c], jnp.concatenate([high, low, high], axis=0), preferred_element_type=F32
        ).reshape(slabs, early + late, width)
        early_ref[:, :, c, :] = smooth[:, :early]
        late_ref[:, :, c, :] = smooth[:, early:]


def filtered_products(pencils, at_points, weights, slabs, early):
    col_count, bands, planes = pencils.shape
    count = at_points.shape[1]
    late = planes // slabs - early
    angles = 2.0 * np.pi / planes * (np.arange(planes)[:, None] * np.arange(planes) % planes)
    waves = jnp.asarray(np.cos(angles), F32)
    chunk = 256
    return pl.pallas_call(
        filter_kernel,
        grid=(count // chunk,),
        in_specs=[
            pl.BlockSpec(pencils.shape, lambda i: (0, 0, 0)),
            pl.BlockSpec((bands, chunk), lambda i: (0, i)),
            pl.BlockSpec(weights.shape, lambda i: (0, 0)),
            pl.BlockSpec(waves.shape, lambda i: (0, 0)),
        ],
        out_specs=[
            pl.BlockSpec((slabs, early, col_count, chunk), lambda i: (0, 0, 0, i)),
            pl.BlockSpec((slabs, late, col_count, chunk), lambda i: (0, 0, 0, i)),
        ],
        out_shape=[
            jax.ShapeDtypeStruct((slabs, early, col_count, count), F32),
            jax.ShapeDtypeStruct((slabs, late, col_count, count), F32),
        ],
        scratch_shapes=[pltpu.VMEM((col_count, planes, 3 * planes), BF16)],
        compiler_params=pltpu.CompilerParams(vmem_limit_bytes=28 << 20),
        cost_estimate=pl.CostEstimate(
            flops=8 * col_count * planes * bands * count, bytes_accessed=10 << 20, transcendentals=0
        ),
    )(pencils, at_points, weights, waves)


def fit_rows(rows, high_ref, low_ref):
    high, low = split_parts(rows, 2)
    dot = functools.partial(jnp.dot, preferred_element_type=F32)
    return (
        dot(high, high_ref[...]) + (dot(low, high_ref[...]) + dot(high, low_ref[...]))
    ).astype(BF16)


def late_fit_kernel(rows_ref, high_ref, low_ref, out_ref):
    out_ref[...] = fit_rows(rows_ref[...], high_ref, low_ref)


def late_fit(rows, high, low):
    total, count = rows.shape
    block = 256
    whole = pl.BlockSpec((count, count), lambda i: (0, 0))
    return pl.pallas_call(
        late_fit_kernel,
        grid=(total // block,),
        in_specs=[pl.BlockSpec((block, count), lambda i: (i, 0)), whole, whole],
        out_specs=pl.BlockSpec((block, count), lambda i: (i, 0)),
        out_shape=jax.ShapeDtypeStruct(rows.shape, BF16),
        compiler_params=pltpu.CompilerParams(vmem_limit_bytes=24 << 20),
        cost_estimate=pl.CostEstimate(
            flops=6 * total * count * count, bytes_accessed=10 << 20, transcendentals=0
        ),
    )(rows, high, low)


def early_fit_kernel(rows_ref, high_ref, low_ref, out_ref):
    planes, cols, count = out_ref.shape
    rows = jnp.concatenate(
        [rows_ref[:, z].reshape(cols, count) for z in range(planes)], axis=0
    )
    out_ref[...] = fit_rows(rows, high_ref, low_ref).reshape(planes, cols, count)


def early_fit(slab, high, low, total_planes):
    sources, early, col_count, count = slab.shape
    block = 2
    whole = pl.BlockSpec((count, count), lambda i: (0, 0))
    return pl.pallas_call(
        early_fit_kernel,
        grid=(early // block,),
        in_specs=[
            pl.BlockSpec((sources, block, col_count, count), lambda i: (0, i, 0, 0)),
            whole,
            whole,
        ],
        out_specs=pl.BlockSpec((block, sources * col_count, count), lambda i: (i, 0, 0)),
        out_shape=jax.ShapeDtypeStruct((total_planes, sources * col_count, count), BF16),
        compiler_params=pltpu.CompilerParams(vmem_limit_bytes=24 << 20),
        cost_estimate=pl.CostEstimate(
            flops=6 * slab.size * count, bytes_accessed=10 << 20, transcendentals=0
        ),
    )(slab, high, low)


def place_late_kernel(late_ref, _, out_ref):
    planes, cols, count = out_ref.shape
    for z in range(planes):
        out_ref[z] = late_ref[:, z].astype(F32).reshape(cols, count).astype(BF16)


def place_late(late, fitted):
    sources, planes, col_count, count = late.shape
    block = 2
    first = (fitted.shape[0] - planes) // block
    return pl.pallas_call(
        place_late_kernel,
        grid=(planes // block,),
        in_specs=[
            pl.BlockSpec((sources, block, col_count, count), lambda i: (0, i, 0, 0)),
            pl.BlockSpec(memory_space=pl.ANY),
        ],
        out_specs=pl.BlockSpec((block, sources * col_count, count), lambda i: (first + i, 0, 0)),
        out_shape=jax.ShapeDtypeStruct(fitted.shape, BF16),
        input_output_aliases={1: 0},
        compiler_params=pltpu.CompilerParams(vmem_limit_bytes=12 << 20),
        cost_estimate=pl.CostEstimate(flops=0, bytes_accessed=2 * late.size * 2, transcendentals=0),
    )(late, fitted)


def per_device(orbitals, points, coulomb):
    gz_count, gy_count = lax.axis_size("gz"), lax.axis_size("gy")
    planes, columns = coulomb.shape
    col_pencil = columns // gz_count
    count = points.shape[0]
    slab_planes = planes // gz_count
    early = EARLY
    pencils, at_points = exchange(orbitals, points, gz_count, gy_count, col_pencil)
    at_points = at_points.reshape(-1, count)
    pencils = jnp.transpose(pencils.reshape(-1, col_pencil, planes), (1, 0, 2))
    weights = lax.dynamic_slice_in_dim(
        coulomb, lax.axis_index("gz") * col_pencil, col_pencil, 1
    ).T
    first, second = filtered_products(pencils, at_points, weights, gz_count, early)
    swap = functools.partial(
        lax.all_to_all, axis_name="gz", split_axis=0, concat_axis=0, tiled=True
    )
    slab = swap(first)
    high, low = gram_inverse(at_points)
    late = late_fit(second.reshape(-1, count), high, low)
    late = swap(late.reshape(gz_count, slab_planes - early, col_pencil, count))
    return place_late(late, early_fit(slab, high, low, slab_planes))


def solution(mesh):
    return jax.shard_map(
        per_device,
        mesh=mesh,
        in_specs=(P(("gz", "gy"), None, None), P(), P(None, "gy")),
        out_specs=P("gz", "gy", None),
        check_vma=False,
    )
```

```python
import functools

import jax
import jax.numpy as jnp
import numpy as np
from jax import lax
from jax.experimental import pallas as pl
from jax.experimental.pallas import tpu as pltpu
from jax.sharding import PartitionSpec as P

FULL = lax.Precision.HIGHEST
F32 = jnp.float32
BF16 = jnp.bfloat16
EARLY = 10


def pick_points(orbital_ref, points_ref, out_ref):
    bands, planes, columns = orbital_ref.shape
    points = points_ref[...]
    point_planes = points // columns
    point_columns = points - point_planes * columns
    count = points.shape[1]
    column_pick = (
        lax.broadcasted_iota(jnp.int32, (columns, count), 0) == point_columns
    ).astype(BF16)
    plane_pick = lax.broadcasted_iota(jnp.int32, (planes, count), 0) == point_planes
    for band in range(bands):
        picked = jnp.dot(orbital_ref[band], column_pick, preferred_element_type=F32)
        out_ref[band : band + 1, :] = jnp.sum(
            jnp.where(plane_pick, picked, 0.0), axis=0, keepdims=True
        ).astype(BF16)


def send(source, target, send_sem, recv_sem, device):
    copy = pltpu.make_async_remote_copy(
        src_ref=source,
        dst_ref=target,
        send_sem=send_sem,
        recv_sem=recv_sem,
        device_id=device,
        device_id_type=pl.DeviceIdType.MESH,
    )
    copy.start()
    return copy


def exchange_kernel(
    gz_count,
    gy_count,
    orbital_ref,
    points_ref,
    pencil_ref,
    value_ref,
    own_blocks,
    row_blocks,
    own_values,
    gy_value_sems,
    gz_value_sems,
    gy_block_sems,
    gz_block_sems,
    local_sems,
):
    gz, gy = lax.axis_index("gz"), lax.axis_index("gy")
    gy_peers = [lax.rem(gy + d, gy_count) for d in range(1, gy_count)]
    gz_peers = [lax.rem(gz + d, gz_count) for d in range(1, gz_count)]
    barrier = pltpu.get_barrier_semaphore()
    for device in [(gz, peer) for peer in gy_peers] + [(peer, gy) for peer in gz_peers]:
        pl.semaphore_signal(
            barrier, inc=1, device_id=device, device_id_type=pl.DeviceIdType.MESH
        )
    pick_points(orbital_ref, points_ref, own_values)
    bands, planes, columns = orbital_ref.shape
    _, _, cols, _ = own_blocks.shape
    width = 256
    for band in range(bands):
        for first in range(0, columns, width):
            turned = orbital_ref[band, :, first : first + width].astype(F32).T
            own_blocks[band, first // cols : (first + width) // cols] = turned.reshape(
                width // cols, cols, planes
            ).astype(BF16)
    pl.semaphore_wait(barrier, gy_count + gz_count - 2)

    local = [pltpu.make_async_copy(own_values, value_ref.at[gz, gy], local_sems.at[0])]
    for band in range(bands):
        local.append(
            pltpu.make_async_copy(
                own_blocks.at[band, pl.ds(gy * gz_count, gz_count)],
                row_blocks.at[band, gy],
                local_sems.at[1 + band],
            )
        )
    for copy in local:
        copy.start()
    gy_values = [
        send(
            own_values, value_ref.at[gz, gy], gy_value_sems.at[0, i], gy_value_sems.at[1, i], (gz, peer)
        )
        for i, peer in enumerate(gy_peers)
    ]
    gy_blocks = [
        [
            send(
                own_blocks.at[band, pl.ds(peer * gz_count, gz_count)],
                row_blocks.at[band, gy],
                gy_block_sems.at[0, band, i],
                gy_block_sems.at[1, band, i],
                (gz, peer),
            )
            for i, peer in enumerate(gy_peers)
        ]
        for band in range(bands)
    ]
    for copy in local:
        copy.wait()
    for copy in gy_values:
        copy.wait_recv()
    second = [
        send(
            value_ref.at[gz], value_ref.at[gz], gz_value_sems.at[0, i], gz_value_sems.at[1, i], (peer, gy)
        )
        for i, peer in enumerate(gz_peers)
    ]
    own = []
    for band in range(bands):
        for copy in gy_blocks[band]:
            copy.wait_recv()
        second += [
            send(
                row_blocks.at[band, :, peer],
                pencil_ref.at[band, gz],
                gz_block_sems.at[0, band, i],
                gz_block_sems.at[1, band, i],
                (peer, gy),
            )
            for i, peer in enumerate(gz_peers)
        ]
        own.append(
            pltpu.make_async_copy(
                row_blocks.at[band, :, gz], pencil_ref.at[band, gz], local_sems.at[1 + bands + band]
            )
        )
        own[band].start()
    for copy in own:
        copy.wait()
    for copy in gy_values + sum(gy_blocks, []):
        copy.wait_send()
    for copy in second:
        copy.wait()


def exchange(orbitals, points, gz_count, gy_count, cols):
    bands, planes, columns = orbitals.shape
    count = points.shape[0]
    vmem = pl.BlockSpec(memory_space=pltpu.VMEM)
    dma = pltpu.SemaphoreType.DMA
    return pl.pallas_call(
        functools.partial(exchange_kernel, gz_count, gy_count),
        in_specs=[vmem, vmem],
        out_specs=(vmem, vmem),
        out_shape=(
            jax.ShapeDtypeStruct((bands, gz_count, gy_count, cols, planes), BF16),
            jax.ShapeDtypeStruct((gz_count, gy_count, bands, count), BF16),
        ),
        scratch_shapes=[
            pltpu.VMEM((bands, columns // cols, cols, planes), BF16),
            pltpu.VMEM((bands, gy_count, gz_count, cols, planes), BF16),
            pltpu.VMEM((bands, count), BF16),
            dma((2, gy_count - 1)),
            dma((2, gz_count - 1)),
            dma((2, bands, gy_count - 1)),
            dma((2, bands, gz_count - 1)),
            dma((1 + 2 * bands,)),
        ],
        compiler_params=pltpu.CompilerParams(
            collective_id=0, has_side_effects=True, vmem_limit_bytes=24 << 20
        ),
    )(orbitals, points.reshape(1, count))


def split_parts(values, count):
    parts = []
    for _ in range(count):
        part = values.astype(BF16)
        parts.append(part)
        values = values - part.astype(F32)
    return parts


def full_dot(left, right):
    high, middle, low = split_parts(left, 3)
    wide = jnp.concatenate([high, high, middle, high, low, middle], axis=1)
    return jnp.dot(wide, full_stack(right), preferred_element_type=F32)


def full_stack(right):
    high, middle, low = split_parts(right, 3)
    return jnp.concatenate([high, middle, high, low, high, middle], axis=0)


def tree_sum(terms):
    while len(terms) > 1:
        terms = [sum(terms[i : i + 2][1:], terms[i]) for i in range(0, len(terms), 2)]
    return terms[0]


def eliminate_rows(rows, first, lane, sub):
    shape = rows.shape
    columns = [jnp.broadcast_to(rows[:, first + j : first + j + 1], shape) for j in range(8)]
    cell = {
        (i, j): jnp.broadcast_to(columns[j][i : i + 1, :], shape)
        for j in range(8)
        for i in range(j + 1)
    }
    for k in range(8):
        recip = 1.0 / cell[k, k]
        side = {i: cell[min(i, k), max(i, k)] for i in range(8) if i != k}
        scaled = {i: side[i] * recip for i in side}
        swept = {}
        for i, j in cell:
            if i == k and j == k:
                swept[i, j] = -recip
            elif i == k or j == k:
                swept[i, j] = scaled[j if i == k else i]
            else:
                swept[i, j] = cell[i, j] - side[i] * scaled[j]
        cell = swept
    inside = (lane >= first) & (lane < first + 8)
    source = [
        jnp.where(
            inside,
            jnp.where(lane == first + j, -1.0, 0.0),
            -jnp.broadcast_to(rows[j : j + 1, :], shape),
        )
        for j in range(8)
    ]
    results = [
        tree_sum([cell[min(i, j), max(i, j)] * source[j] for j in range(8)]) for i in range(8)
    ]
    panel = results[0]
    for i in range(1, 8):
        panel = jnp.where(sub == i, results[i], panel)
    return results, panel, inside


def small_inverse(block):
    size = block.shape[0]
    group_rows = 32
    tiles = [block[i : i + 8, :] for i in range(0, size, 8)]
    lane = lax.broadcasted_iota(jnp.int32, (8, size), 1)
    sub = lax.broadcasted_iota(jnp.int32, (8, size), 0)
    per_group = group_rows // 8
    for start in range(0, size, group_rows):
        group = list(range(start // 8, start // 8 + per_group))
        for at in group:
            results, panel, inside = eliminate_rows(tiles[at], at * 8, lane, sub)
            for step in range(1, per_group):
                other = group[(at - group[0] + step) % per_group]
                terms = [
                    jnp.broadcast_to(tiles[other][:, at * 8 + j : at * 8 + j + 1], (8, size))
                    * results[j]
                    for j in range(8)
                ]
                tiles[other] = jnp.where(inside, 0.0, tiles[other]) - tree_sum(terms)
            tiles[at] = panel
        rest = [i for i in range(len(tiles)) if i not in group]
        panel = jnp.concatenate([tiles[i] for i in group], axis=0)
        stack = jnp.concatenate([tiles[i] for i in rest], axis=0)
        change = full_dot(stack[:, start : start + group_rows], panel)
        wide_lane = lax.broadcasted_iota(jnp.int32, stack.shape, 1)
        in_group = (wide_lane >= start) & (wide_lane < start + group_rows)
        stack = jnp.where(in_group, 0.0, stack) - change
        for place, i in enumerate(rest):
            tiles[i] = stack[place * 8 : place * 8 + 8, :]
    return jnp.concatenate(tiles, axis=0)


def inverse_kernel(width, point_ref, late_ref, fitted_ref, high_ref, low_ref, work):
    size = work.shape[0]
    block = 256
    for first in range(0, size, block):
        base = lax.dot_general(
            point_ref[:, first : first + block],
            point_ref[...],
            (((0,), (0,)), ((), ())),
            preferred_element_type=F32,
        )
        work[first : first + block, :] = base * base

    def eliminate(k, carry):
        at = pl.ds(pl.multiple_of(k * width, width), width)
        pivot = small_inverse(work[at, at])
        work[at, :] = full_dot(pivot, work[at, :])
        work[at, at] = pivot
        panel = work[at, :]
        stacked = full_stack(panel)
        high, middle, low = split_parts(work[:, at], 3)
        wide = jnp.concatenate([high, high, middle, high, low, middle], axis=1)
        work[:, at] = jnp.zeros((size, width), F32)
        for first in range(0, size, block):
            columns = slice(first, first + block)
            change = jnp.dot(wide, stacked[:, columns], preferred_element_type=F32)
            work[:, columns] = work[:, columns] - change
        work[at, :] = panel
        return carry

    lax.fori_loop(0, size // width, eliminate, 0)
    for first in range(0, size, block):
        rows = slice(first, first + block)
        high, low = split_parts(work[rows, :], 2)
        high_ref[rows, :] = high
        low_ref[rows, :] = low
    for first in range(0, late_ref.shape[0], block):
        rows = slice(first, first + block)
        fitted_ref[rows, :] = fit_rows(late_ref[rows, :], high_ref, low_ref)


def inverse_and_late_fit(at_points, late):
    size = at_points.shape[1]
    whole = pl.BlockSpec((size, size), lambda i: (0, 0))
    rows = pl.BlockSpec(late.shape, lambda i: (0, 0))
    return pl.pallas_call(
        functools.partial(inverse_kernel, 128),
        grid=(1,),
        in_specs=[pl.BlockSpec(at_points.shape, lambda i: (0, 0)), rows],
        out_specs=(rows, whole, whole),
        out_shape=(
            pltpu.HBM(late.shape, BF16),
            pltpu.HBM((size, size), BF16),
            pltpu.HBM((size, size), BF16),
        ),
        scratch_shapes=[pltpu.VMEM((size, size), F32)],
        compiler_params=pltpu.CompilerParams(vmem_limit_bytes=44 << 20),
        cost_estimate=pl.CostEstimate(
            flops=60 * size**3, bytes_accessed=8 * size * size, transcendentals=0
        ),
    )(at_points, late)


def filter_kernel(
    slabs, pencil_ref, point_ref, weight_ref, wave_ref, early_ref, late_ref, circulant, natural, ordered
):
    col_count, _, planes = pencil_ref.shape
    early_rows = early_ref.shape[0]
    slab_planes, early = planes // slabs, early_rows // slabs
    late = slab_planes - early

    @pl.when(pl.program_id(0) == 0)
    def _():
        rows = jnp.dot(
            weight_ref[...], wave_ref[...], precision=FULL, preferred_element_type=F32
        ) * (1.0 / planes)
        for c in range(col_count):
            natural[...] = pltpu.roll(
                jnp.broadcast_to(rows[c : c + 1, :], (planes, planes)),
                0,
                1,
                stride=1,
                stride_axis=0,
            )
            for slab in range(slabs):
                start = slab * slab_planes
                ordered[slab * early : (slab + 1) * early, :] = natural[start : start + early, :]
                place = early_rows + slab * late
                ordered[place : place + late, :] = natural[start + early : start + slab_planes, :]
            high, low = split_parts(ordered[...], 2)
            circulant[c] = jnp.concatenate([high, high, low], axis=1)

    for c in range(col_count):
        sums = lax.dot_general(
            pencil_ref[c], point_ref[...], (((0,), (0,)), ((), ())), preferred_element_type=F32
        )
        high, low = split_parts(sums * sums, 2)
        smooth = jnp.dot(
            circulant[c], jnp.concatenate([high, low, high], axis=0), preferred_element_type=F32
        )
        early_ref[:, c, :] = smooth[:early_rows]
        late_ref[:, c, :] = smooth[early_rows:]


def filtered_products(pencils, at_points, weights, slabs, early):
    col_count, bands, planes = pencils.shape
    count = at_points.shape[1]
    late = planes // slabs - early
    early, late = slabs * early, slabs * late
    angles = 2.0 * np.pi / planes * (np.arange(planes)[:, None] * np.arange(planes) % planes)
    waves = jnp.asarray(np.cos(angles), F32)
    chunk = 256
    return pl.pallas_call(
        functools.partial(filter_kernel, slabs),
        grid=(count // chunk,),
        in_specs=[
            pl.BlockSpec(pencils.shape, lambda i: (0, 0, 0)),
            pl.BlockSpec((bands, chunk), lambda i: (0, i)),
            pl.BlockSpec(weights.shape, lambda i: (0, 0)),
            pl.BlockSpec(waves.shape, lambda i: (0, 0)),
        ],
        out_specs=[
            pl.BlockSpec((early, col_count, chunk), lambda i: (0, 0, i)),
            pl.BlockSpec((late, col_count, chunk), lambda i: (0, 0, i)),
        ],
        out_shape=[
            pltpu.HBM((early, col_count, count), F32),
            pltpu.HBM((late, col_count, count), F32),
        ],
        scratch_shapes=[
            pltpu.VMEM((col_count, planes, 3 * planes), BF16),
            pltpu.VMEM((planes, planes), F32),
            pltpu.VMEM((planes, planes), F32),
        ],
        compiler_params=pltpu.CompilerParams(vmem_limit_bytes=28 << 20),
        cost_estimate=pl.CostEstimate(
            flops=8 * col_count * planes * bands * count, bytes_accessed=10 << 20, transcendentals=0
        ),
    )(pencils, at_points, weights, waves)


def fit_rows(rows, high_ref, low_ref):
    high, low = split_parts(rows, 2)
    dot = functools.partial(jnp.dot, preferred_element_type=F32)
    return (
        dot(high, high_ref[...]) + (dot(low, high_ref[...]) + dot(high, low_ref[...]))
    ).astype(BF16)


def early_fit_kernel(rows_ref, high_ref, low_ref, out_ref):
    planes, cols, count = out_ref.shape
    rows = jnp.concatenate(
        [rows_ref[:, z].reshape(cols, count) for z in range(planes)], axis=0
    )
    out_ref[...] = fit_rows(rows, high_ref, low_ref).reshape(planes, cols, count)


def early_fit(slab, high, low, total_planes):
    sources, early, col_count, count = slab.shape
    block = 2
    whole = pl.BlockSpec((count, count), lambda i: (0, 0))
    return pl.pallas_call(
        early_fit_kernel,
        grid=(early // block,),
        in_specs=[
            pl.BlockSpec((sources, block, col_count, count), lambda i: (0, i, 0, 0)),
            whole,
            whole,
        ],
        out_specs=pl.BlockSpec((block, sources * col_count, count), lambda i: (i, 0, 0)),
        out_shape=jax.ShapeDtypeStruct((total_planes, sources * col_count, count), BF16),
        compiler_params=pltpu.CompilerParams(vmem_limit_bytes=24 << 20),
        cost_estimate=pl.CostEstimate(
            flops=6 * slab.size * count, bytes_accessed=10 << 20, transcendentals=0
        ),
    )(slab, high, low)


def place_late_kernel(late_ref, _, out_ref):
    planes, cols, count = out_ref.shape
    for z in range(planes):
        out_ref[z] = late_ref[:, z].astype(F32).reshape(cols, count).astype(BF16)


def place_late(late, fitted):
    sources, planes, col_count, count = late.shape
    block = 2
    first = (fitted.shape[0] - planes) // block
    return pl.pallas_call(
        place_late_kernel,
        grid=(planes // block,),
        in_specs=[
            pl.BlockSpec((sources, block, col_count, count), lambda i: (0, i, 0, 0)),
            pl.BlockSpec(memory_space=pl.ANY),
        ],
        out_specs=pl.BlockSpec((block, sources * col_count, count), lambda i: (first + i, 0, 0)),
        out_shape=jax.ShapeDtypeStruct(fitted.shape, BF16),
        input_output_aliases={1: 0},
        compiler_params=pltpu.CompilerParams(vmem_limit_bytes=12 << 20),
        cost_estimate=pl.CostEstimate(flops=0, bytes_accessed=2 * late.size * 2, transcendentals=0),
    )(late, fitted)


def per_device(orbitals, points, coulomb):
    gz_count, gy_count = lax.axis_size("gz"), lax.axis_size("gy")
    planes, columns = coulomb.shape
    col_pencil = columns // gz_count
    count = points.shape[0]
    slab_planes = planes // gz_count
    early = EARLY
    pencils, at_points = exchange(orbitals, points, gz_count, gy_count, col_pencil)
    at_points = jnp.transpose(at_points, (2, 0, 1, 3)).reshape(-1, count)
    pencils = jnp.transpose(pencils.reshape(-1, col_pencil, planes), (1, 0, 2))
    weights = lax.dynamic_slice_in_dim(
        coulomb, lax.axis_index("gz") * col_pencil, col_pencil, 1
    ).T
    first, second = filtered_products(pencils, at_points, weights, gz_count, early)
    swap = functools.partial(
        lax.all_to_all, axis_name="gz", split_axis=0, concat_axis=0, tiled=True
    )
    slab = swap(first.reshape(gz_count, early, col_pencil, count))
    late, high, low = inverse_and_late_fit(at_points, second.reshape(-1, count))
    late = swap(late.reshape(gz_count, slab_planes - early, col_pencil, count))
    return place_late(late, early_fit(slab, high, low, slab_planes))


def solution(mesh):
    return jax.shard_map(
        per_device,
        mesh=mesh,
        in_specs=(P(("gz", "gy"), None, None), P(), P(None, "gy")),
        out_specs=P("gz", "gy", None),
        check_vma=False,
    )
```

```python
import functools

import jax
import jax.numpy as jnp
import numpy as np
from jax import lax
from jax.experimental import pallas as pl
from jax.experimental.pallas import tpu as pltpu
from jax.sharding import PartitionSpec as P

FULL = lax.Precision.HIGHEST
F32 = jnp.float32
BF16 = jnp.bfloat16
EARLY = 8


def pick_points(orbital_ref, points_ref, out_ref):
    bands, planes, columns = orbital_ref.shape
    points = points_ref[...]
    point_planes = points // columns
    point_columns = points - point_planes * columns
    count = points.shape[1]
    column_pick = (
        lax.broadcasted_iota(jnp.int32, (columns, count), 0) == point_columns
    ).astype(BF16)
    plane_pick = lax.broadcasted_iota(jnp.int32, (planes, count), 0) == point_planes
    for band in range(bands):
        picked = jnp.dot(orbital_ref[band], column_pick, preferred_element_type=F32)
        out_ref[band : band + 1, :] = jnp.sum(
            jnp.where(plane_pick, picked, 0.0), axis=0, keepdims=True
        ).astype(BF16)


def send(source, target, send_sem, recv_sem, device):
    copy = pltpu.make_async_remote_copy(
        src_ref=source,
        dst_ref=target,
        send_sem=send_sem,
        recv_sem=recv_sem,
        device_id=device,
        device_id_type=pl.DeviceIdType.MESH,
    )
    copy.start()
    return copy


def exchange_kernel(
    gz_count,
    gy_count,
    orbital_hbm,
    points_ref,
    weight_ref,
    left_wave_hbm,
    right_wave_hbm,
    pencil_ref,
    value_ref,
    circulant_ref,
    orbital_ref,
    left_wave_ref,
    right_wave_ref,
    own_blocks,
    plane_stage,
    row_stage,
    value_stage,
    own_values,
    gz_value_sems,
    gy_value_sems,
    gy_first_sems,
    gz_first_sems,
    gz_second_sems,
    gy_second_sems,
    local_sems,
):
    gz, gy = lax.axis_index("gz"), lax.axis_index("gy")
    gy_peers = [lax.rem(gy + d, gy_count) for d in range(1, gy_count)]
    gz_peers = [lax.rem(gz + d, gz_count) for d in range(1, gz_count)]
    barrier = pltpu.get_barrier_semaphore()
    for device in [(gz, peer) for peer in gy_peers] + [(peer, gy) for peer in gz_peers]:
        pl.semaphore_signal(
            barrier, inc=1, device_id=device, device_id_type=pl.DeviceIdType.MESH
        )
    load = pltpu.make_async_copy(orbital_hbm, orbital_ref, local_sems.at[0])
    load.start()
    load_waves = [
        pltpu.make_async_copy(left_wave_hbm, left_wave_ref, local_sems.at[7]),
        pltpu.make_async_copy(right_wave_hbm, right_wave_ref, local_sems.at[8]),
    ]
    for copy in load_waves:
        copy.start()
    load.wait()
    pick_points(orbital_ref, points_ref, own_values)
    bands, planes, columns = orbital_ref.shape
    half = bands // 2
    cols = own_blocks.shape[3]
    width = 256
    for band in range(bands):
        for first in range(0, columns, width):
            turned = orbital_ref[band, :, first : first + width].astype(F32).T
            at = first // cols
            own_blocks[band, at // gz_count : (at + width // cols) // gz_count] = (
                turned.reshape(width // cols // gz_count, gz_count, cols, planes).astype(BF16)
            )
    pl.semaphore_wait(barrier, gy_count + gz_count - 2)

    own = [
        pltpu.make_async_copy(own_values, value_stage.at[gz], local_sems.at[1]),
        pltpu.make_async_copy(
            own_blocks.at[pl.ds(0, half), gy], plane_stage.at[gy], local_sems.at[2]
        ),
        pltpu.make_async_copy(
            own_blocks.at[pl.ds(half, half), :, gz], row_stage.at[gz], local_sems.at[3]
        ),
    ]
    for copy in own:
        copy.start()
    values = [
        send(own_values, value_stage.at[gz], gz_value_sems.at[0, i], gz_value_sems.at[1, i], (peer, gy))
        for i, peer in enumerate(gz_peers)
    ]
    lower = [
        send(
            own_blocks.at[pl.ds(0, half), peer],
            plane_stage.at[gy],
            gy_first_sems.at[0, i],
            gy_first_sems.at[1, i],
            (gz, peer),
        )
        for i, peer in enumerate(gy_peers)
    ]
    upper = [
        send(
            own_blocks.at[pl.ds(half, half), :, peer],
            row_stage.at[gz],
            gz_first_sems.at[0, i],
            gz_first_sems.at[1, i],
            (peer, gy),
        )
        for i, peer in enumerate(gz_peers)
    ]
    for copy in own:
        copy.wait()
    for copy in values:
        copy.wait_recv()
    values_on = [
        send(value_stage, value_ref.at[gy], gy_value_sems.at[0, i], gy_value_sems.at[1, i], (gz, peer))
        for i, peer in enumerate(gy_peers)
    ]
    for copy in lower:
        copy.wait_recv()
    lower_on = [
        send(
            plane_stage.at[:, :, peer],
            pencil_ref.at[0, gz],
            gz_second_sems.at[0, i],
            gz_second_sems.at[1, i],
            (peer, gy),
        )
        for i, peer in enumerate(gz_peers)
    ]
    for copy in upper:
        copy.wait_recv()
    upper_on = [
        send(
            row_stage.at[:, :, peer],
            pencil_ref.at[1, :, gy],
            gy_second_sems.at[0, i],
            gy_second_sems.at[1, i],
            (gz, peer),
        )
        for i, peer in enumerate(gy_peers)
    ]
    own_on = [
        pltpu.make_async_copy(value_stage, value_ref.at[gy], local_sems.at[4]),
        pltpu.make_async_copy(plane_stage.at[:, :, gz], pencil_ref.at[0, gz], local_sems.at[5]),
        pltpu.make_async_copy(row_stage.at[:, :, gy], pencil_ref.at[1, :, gy], local_sems.at[6]),
    ]
    for copy in own_on:
        copy.start()
    for copy in load_waves:
        copy.wait()
    for c in range(cols):
        high, low = split_parts(
            jnp.dot(
                left_wave_ref[...] * weight_ref[c : c + 1, :],
                right_wave_ref[...],
                precision=FULL,
                preferred_element_type=F32,
            ),
            2,
        )
        circulant_ref[c] = jnp.concatenate([high, high, low], axis=1)
    for copy in own_on:
        copy.wait()
    for copy in values + lower + upper:
        copy.wait_send()
    for copy in values_on + lower_on + upper_on:
        copy.wait()


def exchange(orbitals, points, weights, gz_count, gy_count, early):
    bands, planes, columns = orbitals.shape
    count = points.shape[0]
    cols = weights.shape[0]
    half = bands // 2
    slab = planes // gz_count
    z = np.arange(planes)
    order = z.reshape(gz_count, slab)
    order = np.concatenate([order[:, :early].ravel(), order[:, early:].ravel()])
    angles = 2.0 * np.pi / planes * (z[:, None] * z % planes)
    waves = np.concatenate([np.cos(angles), np.sin(angles)], axis=1)
    vmem, hbm = (pl.BlockSpec(memory_space=space) for space in (pltpu.VMEM, pltpu.HBM))
    dma = pltpu.SemaphoreType.DMA
    return pl.pallas_call(
        functools.partial(exchange_kernel, gz_count, gy_count),
        in_specs=[hbm, vmem, vmem, hbm, hbm],
        out_specs=(vmem, vmem, vmem),
        out_shape=(
            jax.ShapeDtypeStruct((2, gz_count, gy_count, half, cols, planes), BF16),
            jax.ShapeDtypeStruct((gy_count, gz_count, bands, count), BF16),
            jax.ShapeDtypeStruct((cols, planes, 3 * planes), BF16),
        ),
        scratch_shapes=[
            pltpu.VMEM((bands, planes, columns), BF16),
            pltpu.VMEM((planes, 2 * planes), F32),
            pltpu.VMEM((2 * planes, planes), F32),
            pltpu.VMEM((bands, gy_count, gz_count, cols, planes), BF16),
            pltpu.VMEM((gy_count, half, gz_count, cols, planes), BF16),
            pltpu.VMEM((gz_count, half, gy_count, cols, planes), BF16),
            pltpu.VMEM((gz_count, bands, count), BF16),
            pltpu.VMEM((bands, count), BF16),
            dma((2, gz_count - 1)),
            dma((2, gy_count - 1)),
            dma((2, gy_count - 1)),
            dma((2, gz_count - 1)),
            dma((2, gz_count - 1)),
            dma((2, gy_count - 1)),
            dma((9,)),
        ],
        compiler_params=pltpu.CompilerParams(
            collective_id=0, has_side_effects=True, vmem_limit_bytes=28 << 20
        ),
    )(
        orbitals,
        points.reshape(1, count),
        jnp.concatenate([weights, weights], axis=1) * (1.0 / planes),
        jnp.asarray(waves[order], F32),
        jnp.asarray(waves.T, F32),
    )


def split_parts(values, count):
    parts = []
    for _ in range(count):
        part = values.astype(BF16)
        parts.append(part)
        values = values - part.astype(F32)
    return parts


def full_dot(left, right):
    high, middle, low = split_parts(left, 3)
    wide = jnp.concatenate([high, high, middle, high, low, middle], axis=1)
    return jnp.dot(wide, full_stack(right), preferred_element_type=F32)


def full_stack(right):
    high, middle, low = split_parts(right, 3)
    return jnp.concatenate([high, middle, high, low, high, middle], axis=0)


def tree_sum(terms):
    while len(terms) > 1:
        terms = [sum(terms[i : i + 2][1:], terms[i]) for i in range(0, len(terms), 2)]
    return terms[0]


def eliminate_rows(rows, first, lane, sub):
    shape = rows.shape
    columns = [jnp.broadcast_to(rows[:, first + j : first + j + 1], shape) for j in range(8)]
    cell = {
        (i, j): jnp.broadcast_to(columns[j][i : i + 1, :], shape)
        for j in range(8)
        for i in range(j + 1)
    }
    for k in range(8):
        recip = 1.0 / cell[k, k]
        side = {i: cell[min(i, k), max(i, k)] for i in range(8) if i != k}
        scaled = {i: side[i] * recip for i in side}
        swept = {}
        for i, j in cell:
            if i == k and j == k:
                swept[i, j] = -recip
            elif i == k or j == k:
                swept[i, j] = scaled[j if i == k else i]
            else:
                swept[i, j] = cell[i, j] - side[i] * scaled[j]
        cell = swept
    inside = (lane >= first) & (lane < first + 8)
    source = [
        jnp.where(
            inside,
            jnp.where(lane == first + j, -1.0, 0.0),
            -jnp.broadcast_to(rows[j : j + 1, :], shape),
        )
        for j in range(8)
    ]
    results = [
        tree_sum([cell[min(i, j), max(i, j)] * source[j] for j in range(8)]) for i in range(8)
    ]
    panel = results[0]
    for i in range(1, 8):
        panel = jnp.where(sub == i, results[i], panel)
    return results, panel, inside


def small_inverse(block):
    size = block.shape[0]
    group_rows = 32
    tiles = [block[i : i + 8, :] for i in range(0, size, 8)]
    lane = lax.broadcasted_iota(jnp.int32, (8, size), 1)
    sub = lax.broadcasted_iota(jnp.int32, (8, size), 0)
    per_group = group_rows // 8
    for start in range(0, size, group_rows):
        group = list(range(start // 8, start // 8 + per_group))
        for at in group:
            results, panel, inside = eliminate_rows(tiles[at], at * 8, lane, sub)
            for step in range(1, per_group):
                other = group[(at - group[0] + step) % per_group]
                terms = [
                    jnp.broadcast_to(tiles[other][:, at * 8 + j : at * 8 + j + 1], (8, size))
                    * results[j]
                    for j in range(8)
                ]
                tiles[other] = jnp.where(inside, 0.0, tiles[other]) - tree_sum(terms)
            tiles[at] = panel
        rest = [i for i in range(len(tiles)) if i not in group]
        panel = jnp.concatenate([tiles[i] for i in group], axis=0)
        stack = jnp.concatenate([tiles[i] for i in rest], axis=0)
        change = full_dot(stack[:, start : start + group_rows], panel)
        wide_lane = lax.broadcasted_iota(jnp.int32, stack.shape, 1)
        in_group = (wide_lane >= start) & (wide_lane < start + group_rows)
        stack = jnp.where(in_group, 0.0, stack) - change
        for place, i in enumerate(rest):
            tiles[i] = stack[place * 8 : place * 8 + 8, :]
    return jnp.concatenate(tiles, axis=0)


def inverse_kernel(width, point_ref, late_ref, fitted_ref, high_ref, low_ref, work):
    size = work.shape[0]
    block = 256
    for first in range(0, size, block):
        base = lax.dot_general(
            point_ref[:, first : first + block],
            point_ref[...],
            (((0,), (0,)), ((), ())),
            preferred_element_type=F32,
        )
        work[first : first + block, :] = base * base

    def eliminate(k, carry):
        at = pl.ds(pl.multiple_of(k * width, width), width)
        pivot = small_inverse(work[at, at])
        work[at, :] = full_dot(pivot, work[at, :])
        work[at, at] = pivot
        panel = work[at, :]
        stacked = full_stack(panel)
        high, middle, low = split_parts(work[:, at], 3)
        wide = jnp.concatenate([high, high, middle, high, low, middle], axis=1)
        work[:, at] = jnp.zeros((size, width), F32)
        for first in range(0, size, block):
            columns = slice(first, first + block)
            change = jnp.dot(wide, stacked[:, columns], preferred_element_type=F32)
            work[:, columns] = work[:, columns] - change
        work[at, :] = panel
        return carry

    lax.fori_loop(0, size // width, eliminate, 0)
    for first in range(0, size, block):
        rows = slice(first, first + block)
        high, low = split_parts(work[rows, :], 2)
        high_ref[rows, :] = high
        low_ref[rows, :] = low
    for first in range(0, late_ref.shape[0], block):
        rows = slice(first, first + block)
        fitted_ref[rows, :] = fit_rows(late_ref[rows, :], high_ref, low_ref)


def inverse_and_late_fit(at_points, late):
    size = at_points.shape[1]
    whole = pl.BlockSpec((size, size), lambda i: (0, 0))
    rows = pl.BlockSpec(late.shape, lambda i: (0, 0))
    return pl.pallas_call(
        functools.partial(inverse_kernel, 128),
        grid=(1,),
        in_specs=[pl.BlockSpec(at_points.shape, lambda i: (0, 0)), rows],
        out_specs=(rows, whole, whole),
        out_shape=(
            pltpu.HBM(late.shape, BF16),
            pltpu.HBM((size, size), BF16),
            pltpu.HBM((size, size), BF16),
        ),
        scratch_shapes=[pltpu.VMEM((size, size), F32)],
        compiler_params=pltpu.CompilerParams(vmem_limit_bytes=44 << 20),
        cost_estimate=pl.CostEstimate(
            flops=60 * size**3, bytes_accessed=8 * size * size, transcendentals=0
        ),
    )(at_points, late)


def filter_kernel(pencil_ref, point_ref, circulant_ref, early_ref, late_ref):
    early = early_ref.shape[0]
    for c in range(pencil_ref.shape[0]):
        sums = lax.dot_general(
            pencil_ref[c], point_ref[...], (((0,), (0,)), ((), ())), preferred_element_type=F32
        )
        high, low = split_parts(sums * sums, 2)
        smooth = jnp.dot(
            circulant_ref[c],
            jnp.concatenate([high, low, high], axis=0),
            preferred_element_type=F32,
        )
        early_ref[:, c, :] = smooth[:early]
        late_ref[:, c, :] = smooth[early:]


def filtered_products(pencils, at_points, circulant, early):
    col_count, bands, planes = pencils.shape
    count = at_points.shape[1]
    late = planes - early
    chunk = 256
    return pl.pallas_call(
        filter_kernel,
        grid=(count // chunk,),
        in_specs=[
            pl.BlockSpec(pencils.shape, lambda i: (0, 0, 0)),
            pl.BlockSpec((bands, chunk), lambda i: (0, i)),
            pl.BlockSpec(circulant.shape, lambda i: (0, 0, 0)),
        ],
        out_specs=[
            pl.BlockSpec((early, col_count, chunk), lambda i: (0, 0, i)),
            pl.BlockSpec((late, col_count, chunk), lambda i: (0, 0, i)),
        ],
        out_shape=[
            pltpu.HBM((early, col_count, count), F32),
            pltpu.HBM((late, col_count, count), F32),
        ],
        compiler_params=pltpu.CompilerParams(vmem_limit_bytes=28 << 20),
        cost_estimate=pl.CostEstimate(
            flops=8 * col_count * planes * bands * count, bytes_accessed=10 << 20, transcendentals=0
        ),
    )(pencils, at_points, circulant)


def fit_rows(rows, high_ref, low_ref):
    high, low = split_parts(rows, 2)
    dot = functools.partial(jnp.dot, preferred_element_type=F32)
    return (
        dot(high, high_ref[...]) + (dot(low, high_ref[...]) + dot(high, low_ref[...]))
    ).astype(BF16)


def early_fit_kernel(rows_ref, high_ref, low_ref, out_ref):
    planes, cols, count = out_ref.shape
    rows = jnp.concatenate(
        [rows_ref[:, z].reshape(cols, count) for z in range(planes)], axis=0
    )
    out_ref[...] = fit_rows(rows, high_ref, low_ref).reshape(planes, cols, count)


def early_fit(slab, high, low, total_planes):
    sources, early, col_count, count = slab.shape
    block = 2
    whole = pl.BlockSpec((count, count), lambda i: (0, 0))
    return pl.pallas_call(
        early_fit_kernel,
        grid=(early // block,),
        in_specs=[
            pl.BlockSpec((sources, block, col_count, count), lambda i: (0, i, 0, 0)),
            whole,
            whole,
        ],
        out_specs=pl.BlockSpec((block, sources * col_count, count), lambda i: (i, 0, 0)),
        out_shape=jax.ShapeDtypeStruct((total_planes, sources * col_count, count), BF16),
        compiler_params=pltpu.CompilerParams(vmem_limit_bytes=24 << 20),
        cost_estimate=pl.CostEstimate(
            flops=6 * slab.size * count, bytes_accessed=10 << 20, transcendentals=0
        ),
    )(slab, high, low)


def place_late_kernel(late_ref, _, out_ref):
    planes, cols, count = out_ref.shape
    for z in range(planes):
        out_ref[z] = late_ref[:, z].astype(F32).reshape(cols, count).astype(BF16)


def place_late(late, fitted):
    sources, planes, col_count, count = late.shape
    block = 2
    first = (fitted.shape[0] - planes) // block
    return pl.pallas_call(
        place_late_kernel,
        grid=(planes // block,),
        in_specs=[
            pl.BlockSpec((sources, block, col_count, count), lambda i: (0, i, 0, 0)),
            pl.BlockSpec(memory_space=pl.ANY),
        ],
        out_specs=pl.BlockSpec((block, sources * col_count, count), lambda i: (first + i, 0, 0)),
        out_shape=jax.ShapeDtypeStruct(fitted.shape, BF16),
        input_output_aliases={1: 0},
        compiler_params=pltpu.CompilerParams(vmem_limit_bytes=12 << 20),
        cost_estimate=pl.CostEstimate(flops=0, bytes_accessed=2 * late.size * 2, transcendentals=0),
    )(late, fitted)


def per_device(orbitals, points, coulomb):
    gz_count, gy_count = lax.axis_size("gz"), lax.axis_size("gy")
    planes, columns = coulomb.shape
    col_pencil = columns // gz_count
    count = points.shape[0]
    slab_planes = planes // gz_count
    early = EARLY
    weights = lax.dynamic_slice_in_dim(
        coulomb, lax.axis_index("gz") * col_pencil, col_pencil, 1
    ).T
    pencils, at_points, circulant = exchange(
        orbitals, points, weights, gz_count, gy_count, early
    )
    bands = orbitals.shape[0]
    at_points = jnp.transpose(
        at_points.reshape(gy_count, gz_count, 2, bands // 2, count), (2, 1, 0, 3, 4)
    ).reshape(-1, count)
    pencils = jnp.transpose(pencils.reshape(-1, col_pencil, planes), (1, 0, 2))
    first, second = filtered_products(pencils, at_points, circulant, gz_count * early)
    swap = functools.partial(
        lax.all_to_all, axis_name="gz", split_axis=0, concat_axis=0, tiled=True
    )
    slab = swap(first.reshape(gz_count, early, col_pencil, count))
    late, high, low = inverse_and_late_fit(at_points, second.reshape(-1, count))
    late = swap(late.reshape(gz_count, slab_planes - early, col_pencil, count))
    return place_late(late, early_fit(slab, high, low, slab_planes))


def solution(mesh):
    return jax.shard_map(
        per_device,
        mesh=mesh,
        in_specs=(P(("gz", "gy"), None, None), P(), P(None, "gy")),
        out_specs=P("gz", "gy", None),
        check_vma=False,
    )
```

```python
import functools

import jax
import jax.numpy as jnp
import numpy as np
from jax import lax
from jax.experimental import pallas as pl
from jax.experimental.pallas import tpu as pltpu
from jax.sharding import PartitionSpec as P

FULL = lax.Precision.HIGHEST
F32 = jnp.float32
BF16 = jnp.bfloat16
EARLY = 8


def in_hbm(array):
    return pltpu.with_memory_space_constraint(array, pltpu.HBM)


def pick_points(orbital_ref, points_ref, out_ref):
    bands, planes, columns = orbital_ref.shape
    points = points_ref[...]
    point_planes = points // columns
    point_columns = points - point_planes * columns
    count = points.shape[1]
    column_pick = (
        lax.broadcasted_iota(jnp.int32, (columns, count), 0) == point_columns
    ).astype(BF16)
    plane_pick = lax.broadcasted_iota(jnp.int32, (planes, count), 0) == point_planes
    for band in range(bands):
        picked = jnp.dot(orbital_ref[band], column_pick, preferred_element_type=F32)
        out_ref[band : band + 1, :] = jnp.sum(
            jnp.where(plane_pick, picked, 0.0), axis=0, keepdims=True
        ).astype(BF16)


def send(source, target, send_sem, recv_sem, device):
    copy = pltpu.make_async_remote_copy(
        src_ref=source,
        dst_ref=target,
        send_sem=send_sem,
        recv_sem=recv_sem,
        device_id=device,
        device_id_type=pl.DeviceIdType.MESH,
    )
    copy.start()
    return copy


def exchange_kernel(
    gz_count,
    gy_count,
    orbital_hbm,
    points_ref,
    weight_ref,
    left_wave_hbm,
    right_wave_hbm,
    pencil_ref,
    value_ref,
    circulant_ref,
    orbital_ref,
    left_wave_ref,
    right_wave_ref,
    own_blocks,
    plane_stage,
    row_stage,
    value_stage,
    own_values,
    gz_value_sems,
    gy_value_sems,
    gy_first_sems,
    gz_first_sems,
    gz_second_sems,
    gy_second_sems,
    local_sems,
):
    gz, gy = lax.axis_index("gz"), lax.axis_index("gy")
    gy_peers = [lax.rem(gy + d, gy_count) for d in range(1, gy_count)]
    gz_peers = [lax.rem(gz + d, gz_count) for d in range(1, gz_count)]
    barrier = pltpu.get_barrier_semaphore()
    for device in [(gz, peer) for peer in gy_peers] + [(peer, gy) for peer in gz_peers]:
        pl.semaphore_signal(
            barrier, inc=1, device_id=device, device_id_type=pl.DeviceIdType.MESH
        )
    load = pltpu.make_async_copy(orbital_hbm, orbital_ref, local_sems.at[0])
    load.start()
    load_waves = [
        pltpu.make_async_copy(left_wave_hbm, left_wave_ref, local_sems.at[7]),
        pltpu.make_async_copy(right_wave_hbm, right_wave_ref, local_sems.at[8]),
    ]
    for copy in load_waves:
        copy.start()
    load.wait()
    pick_points(orbital_ref, points_ref, own_values)
    bands, planes, columns = orbital_ref.shape
    half = bands // 2
    cols = own_blocks.shape[3]
    width = 256
    for band in range(bands):
        for first in range(0, columns, width):
            turned = orbital_ref[band, :, first : first + width].astype(F32).T
            at = first // cols
            own_blocks[band, at // gz_count : (at + width // cols) // gz_count] = (
                turned.reshape(width // cols // gz_count, gz_count, cols, planes).astype(BF16)
            )
    pl.semaphore_wait(barrier, gy_count + gz_count - 2)

    own = [
        pltpu.make_async_copy(own_values, value_stage.at[gz], local_sems.at[1]),
        pltpu.make_async_copy(
            own_blocks.at[pl.ds(0, half), gy], plane_stage.at[gy], local_sems.at[2]
        ),
        pltpu.make_async_copy(
            own_blocks.at[pl.ds(half, half), :, gz], row_stage.at[gz], local_sems.at[3]
        ),
    ]
    for copy in own:
        copy.start()
    values = [
        send(own_values, value_stage.at[gz], gz_value_sems.at[0, i], gz_value_sems.at[1, i], (peer, gy))
        for i, peer in enumerate(gz_peers)
    ]
    lower = [
        send(
            own_blocks.at[pl.ds(0, half), peer],
            plane_stage.at[gy],
            gy_first_sems.at[0, i],
            gy_first_sems.at[1, i],
            (gz, peer),
        )
        for i, peer in enumerate(gy_peers)
    ]
    upper = [
        send(
            own_blocks.at[pl.ds(half, half), :, peer],
            row_stage.at[gz],
            gz_first_sems.at[0, i],
            gz_first_sems.at[1, i],
            (peer, gy),
        )
        for i, peer in enumerate(gz_peers)
    ]
    for copy in own:
        copy.wait()
    for copy in values:
        copy.wait_recv()
    values_on = [
        send(value_stage, value_ref.at[gy], gy_value_sems.at[0, i], gy_value_sems.at[1, i], (gz, peer))
        for i, peer in enumerate(gy_peers)
    ]
    for copy in lower:
        copy.wait_recv()
    lower_on = [
        send(
            plane_stage.at[:, :, peer],
            pencil_ref.at[0, gz],
            gz_second_sems.at[0, i],
            gz_second_sems.at[1, i],
            (peer, gy),
        )
        for i, peer in enumerate(gz_peers)
    ]
    for copy in upper:
        copy.wait_recv()
    upper_on = [
        send(
            row_stage.at[:, :, peer],
            pencil_ref.at[1, :, gy],
            gy_second_sems.at[0, i],
            gy_second_sems.at[1, i],
            (gz, peer),
        )
        for i, peer in enumerate(gy_peers)
    ]
    own_on = [
        pltpu.make_async_copy(value_stage, value_ref.at[gy], local_sems.at[4]),
        pltpu.make_async_copy(plane_stage.at[:, :, gz], pencil_ref.at[0, gz], local_sems.at[5]),
        pltpu.make_async_copy(row_stage.at[:, :, gy], pencil_ref.at[1, :, gy], local_sems.at[6]),
    ]
    for copy in own_on:
        copy.start()
    for copy in load_waves:
        copy.wait()
    for c in range(cols):
        high, low = split_parts(
            jnp.dot(
                left_wave_ref[...] * weight_ref[c : c + 1, :],
                right_wave_ref[...],
                precision=FULL,
                preferred_element_type=F32,
            ),
            2,
        )
        circulant_ref[c] = jnp.concatenate([high, high, low], axis=1)
    for copy in own_on:
        copy.wait()
    for copy in values + lower + upper:
        copy.wait_send()
    for copy in values_on + lower_on + upper_on:
        copy.wait()


def exchange(orbitals, points, weights, gz_count, gy_count, early):
    bands, planes, columns = orbitals.shape
    count = points.shape[0]
    cols = weights.shape[0]
    half = bands // 2
    slab = planes // gz_count
    z = np.arange(planes)
    order = z.reshape(gz_count, slab)
    order = np.concatenate([order[:, :early].ravel(), order[:, early:].ravel()])
    angles = 2.0 * np.pi / planes * (z[:, None] * z % planes)
    waves = np.concatenate([np.cos(angles), np.sin(angles)], axis=1)
    vmem, hbm = (pl.BlockSpec(memory_space=space) for space in (pltpu.VMEM, pltpu.HBM))
    dma = pltpu.SemaphoreType.DMA
    return pl.pallas_call(
        functools.partial(exchange_kernel, gz_count, gy_count),
        in_specs=[hbm, vmem, vmem, hbm, hbm],
        out_specs=(vmem, vmem, vmem),
        out_shape=(
            jax.ShapeDtypeStruct((2, gz_count, gy_count, half, cols, planes), BF16),
            jax.ShapeDtypeStruct((gy_count, gz_count, bands, count), BF16),
            jax.ShapeDtypeStruct((cols, planes, 3 * planes), BF16),
        ),
        scratch_shapes=[
            pltpu.VMEM((bands, planes, columns), BF16),
            pltpu.VMEM((planes, 2 * planes), F32),
            pltpu.VMEM((2 * planes, planes), F32),
            pltpu.VMEM((bands, gy_count, gz_count, cols, planes), BF16),
            pltpu.VMEM((gy_count, half, gz_count, cols, planes), BF16),
            pltpu.VMEM((gz_count, half, gy_count, cols, planes), BF16),
            pltpu.VMEM((gz_count, bands, count), BF16),
            pltpu.VMEM((bands, count), BF16),
            dma((2, gz_count - 1)),
            dma((2, gy_count - 1)),
            dma((2, gy_count - 1)),
            dma((2, gz_count - 1)),
            dma((2, gz_count - 1)),
            dma((2, gy_count - 1)),
            dma((9,)),
        ],
        compiler_params=pltpu.CompilerParams(
            collective_id=0, has_side_effects=True, vmem_limit_bytes=28 << 20
        ),
    )(
        in_hbm(orbitals),
        points.reshape(1, count),
        jnp.concatenate([weights, weights], axis=1) * (1.0 / planes),
        in_hbm(jnp.asarray(waves[order], F32)),
        in_hbm(jnp.asarray(waves.T, F32)),
    )


def split_parts(values, count):
    parts = []
    for _ in range(count):
        part = values.astype(BF16)
        parts.append(part)
        values = values - part.astype(F32)
    return parts


def full_dot(left, right):
    high, middle, low = split_parts(left, 3)
    wide = jnp.concatenate([high, high, middle, high, low, middle], axis=1)
    return jnp.dot(wide, full_stack(right), preferred_element_type=F32)


def full_stack(right):
    high, middle, low = split_parts(right, 3)
    return jnp.concatenate([high, middle, high, low, high, middle], axis=0)


def tree_sum(terms):
    while len(terms) > 1:
        terms = [sum(terms[i : i + 2][1:], terms[i]) for i in range(0, len(terms), 2)]
    return terms[0]


def eliminate_rows(rows, first, lane, sub):
    shape = rows.shape
    columns = [jnp.broadcast_to(rows[:, first + j : first + j + 1], shape) for j in range(8)]
    cell = {
        (i, j): jnp.broadcast_to(columns[j][i : i + 1, :], shape)
        for j in range(8)
        for i in range(j + 1)
    }
    for k in range(8):
        recip = 1.0 / cell[k, k]
        side = {i: cell[min(i, k), max(i, k)] for i in range(8) if i != k}
        scaled = {i: side[i] * recip for i in side}
        swept = {}
        for i, j in cell:
            if i == k and j == k:
                swept[i, j] = -recip
            elif i == k or j == k:
                swept[i, j] = scaled[j if i == k else i]
            else:
                swept[i, j] = cell[i, j] - side[i] * scaled[j]
        cell = swept
    inside = (lane >= first) & (lane < first + 8)
    source = [
        jnp.where(
            inside,
            jnp.where(lane == first + j, -1.0, 0.0),
            -jnp.broadcast_to(rows[j : j + 1, :], shape),
        )
        for j in range(8)
    ]
    results = [
        tree_sum([cell[min(i, j), max(i, j)] * source[j] for j in range(8)]) for i in range(8)
    ]
    panel = results[0]
    for i in range(1, 8):
        panel = jnp.where(sub == i, results[i], panel)
    return results, panel, inside


def small_inverse(block):
    size = block.shape[0]
    group_rows = 32
    tiles = [block[i : i + 8, :] for i in range(0, size, 8)]
    lane = lax.broadcasted_iota(jnp.int32, (8, size), 1)
    sub = lax.broadcasted_iota(jnp.int32, (8, size), 0)
    per_group = group_rows // 8
    for start in range(0, size, group_rows):
        group = list(range(start // 8, start // 8 + per_group))
        for at in group:
            results, panel, inside = eliminate_rows(tiles[at], at * 8, lane, sub)
            for step in range(1, per_group):
                other = group[(at - group[0] + step) % per_group]
                terms = [
                    jnp.broadcast_to(tiles[other][:, at * 8 + j : at * 8 + j + 1], (8, size))
                    * results[j]
                    for j in range(8)
                ]
                tiles[other] = jnp.where(inside, 0.0, tiles[other]) - tree_sum(terms)
            tiles[at] = panel
        rest = [i for i in range(len(tiles)) if i not in group]
        panel = jnp.concatenate([tiles[i] for i in group], axis=0)
        stack = jnp.concatenate([tiles[i] for i in rest], axis=0)
        change = full_dot(stack[:, start : start + group_rows], panel)
        wide_lane = lax.broadcasted_iota(jnp.int32, stack.shape, 1)
        in_group = (wide_lane >= start) & (wide_lane < start + group_rows)
        stack = jnp.where(in_group, 0.0, stack) - change
        for place, i in enumerate(rest):
            tiles[i] = stack[place * 8 : place * 8 + 8, :]
    return jnp.concatenate(tiles, axis=0)


def inverse_kernel(width, point_ref, late_ref, fitted_ref, high_ref, low_ref, work):
    size = work.shape[0]
    block = 256

    @pl.when(pl.program_id(0) == 0)
    def _():
        for first in range(0, size, block):
            base = lax.dot_general(
                point_ref[:, first : first + block],
                point_ref[...],
                (((0,), (0,)), ((), ())),
                preferred_element_type=F32,
            )
            work[first : first + block, :] = base * base

        def eliminate(k, carry):
            at = pl.ds(pl.multiple_of(k * width, width), width)
            pivot = small_inverse(work[at, at])
            work[at, :] = full_dot(pivot, work[at, :])
            work[at, at] = pivot
            panel = work[at, :]
            stacked = full_stack(panel)
            high, middle, low = split_parts(work[:, at], 3)
            wide = jnp.concatenate([high, high, middle, high, low, middle], axis=1)
            work[:, at] = jnp.zeros((size, width), F32)
            for first in range(0, size, block):
                columns = slice(first, first + block)
                change = jnp.dot(wide, stacked[:, columns], preferred_element_type=F32)
                work[:, columns] = work[:, columns] - change
            work[at, :] = panel
            return carry

        lax.fori_loop(0, size // width, eliminate, 0)
        for first in range(0, size, block):
            rows = slice(first, first + block)
            high, low = split_parts(work[rows, :], 2)
            high_ref[rows, :] = high
            low_ref[rows, :] = low

    @pl.when(pl.program_id(0) > 0)
    def _():
        fitted_ref[...] = fit_rows(late_ref[...], high_ref, low_ref)


def inverse_and_late_fit(at_points, late):
    size = at_points.shape[1]
    block = 256
    whole = pl.BlockSpec((size, size), lambda i: (0, 0))
    rows = pl.BlockSpec((block, size), lambda i: (jnp.maximum(i - 1, 0), 0))
    return pl.pallas_call(
        functools.partial(inverse_kernel, 128),
        grid=(1 + late.shape[0] // block,),
        in_specs=[pl.BlockSpec(at_points.shape, lambda i: (0, 0)), rows],
        out_specs=(rows, whole, whole),
        out_shape=(
            pltpu.HBM(late.shape, BF16),
            pltpu.HBM((size, size), BF16),
            pltpu.HBM((size, size), BF16),
        ),
        scratch_shapes=[pltpu.VMEM((size, size), F32)],
        compiler_params=pltpu.CompilerParams(vmem_limit_bytes=36 << 20),
        cost_estimate=pl.CostEstimate(
            flops=60 * size**3, bytes_accessed=8 * size * size, transcendentals=0
        ),
    )(at_points, in_hbm(late))


def filter_kernel(pencil_ref, point_ref, circulant_ref, early_ref, late_ref):
    early = early_ref.shape[0]
    col_count = pencil_ref.shape[0]

    def products(c):
        sums = lax.dot_general(
            pencil_ref[c], point_ref[...], (((0,), (0,)), ((), ())), preferred_element_type=F32
        )
        return split_parts(sums * sums, 2)

    following = products(0)
    for c in range(col_count):
        high, low = following
        if c + 1 < col_count:
            following = products(c + 1)
        smooth = jnp.dot(
            circulant_ref[c],
            jnp.concatenate([high, low, high], axis=0),
            preferred_element_type=F32,
        )
        early_ref[:, c, :] = smooth[:early]
        late_ref[:, c, :] = smooth[early:]


def filtered_products(pencils, at_points, circulant, early):
    col_count, bands, planes = pencils.shape
    count = at_points.shape[1]
    late = planes - early
    chunk = 256
    return pl.pallas_call(
        filter_kernel,
        grid=(count // chunk,),
        in_specs=[
            pl.BlockSpec(pencils.shape, lambda i: (0, 0, 0)),
            pl.BlockSpec((bands, chunk), lambda i: (0, i)),
            pl.BlockSpec(circulant.shape, lambda i: (0, 0, 0)),
        ],
        out_specs=[
            pl.BlockSpec((early, col_count, chunk), lambda i: (0, 0, i)),
            pl.BlockSpec((late, col_count, chunk), lambda i: (0, 0, i)),
        ],
        out_shape=[
            pltpu.HBM((early, col_count, count), F32),
            pltpu.HBM((late, col_count, count), F32),
        ],
        compiler_params=pltpu.CompilerParams(vmem_limit_bytes=28 << 20),
        cost_estimate=pl.CostEstimate(
            flops=8 * col_count * planes * bands * count, bytes_accessed=10 << 20, transcendentals=0
        ),
    )(pencils, at_points, circulant)


def fit_rows(rows, high_ref, low_ref):
    high, low = split_parts(rows, 2)
    dot = functools.partial(jnp.dot, preferred_element_type=F32)
    return (
        dot(high, high_ref[...]) + (dot(low, high_ref[...]) + dot(high, low_ref[...]))
    ).astype(BF16)


def early_fit_kernel(rows_ref, high_ref, low_ref, out_ref):
    planes, cols, count = out_ref.shape
    rows = jnp.concatenate(
        [rows_ref[:, z].reshape(cols, count) for z in range(planes)], axis=0
    )
    out_ref[...] = fit_rows(rows, high_ref, low_ref).reshape(planes, cols, count)


def early_fit(slab, high, low, total_planes):
    sources, early, col_count, count = slab.shape
    block = 2
    whole = pl.BlockSpec((count, count), lambda i: (0, 0))
    return pl.pallas_call(
        early_fit_kernel,
        grid=(early // block,),
        in_specs=[
            pl.BlockSpec((sources, block, col_count, count), lambda i: (0, i, 0, 0)),
            whole,
            whole,
        ],
        out_specs=pl.BlockSpec((block, sources * col_count, count), lambda i: (i, 0, 0)),
        out_shape=jax.ShapeDtypeStruct((total_planes, sources * col_count, count), BF16),
        compiler_params=pltpu.CompilerParams(vmem_limit_bytes=24 << 20),
        cost_estimate=pl.CostEstimate(
            flops=6 * slab.size * count, bytes_accessed=10 << 20, transcendentals=0
        ),
    )(slab, high, low)


def place_late_kernel(late_ref, _, out_ref):
    planes, cols, count = out_ref.shape
    for z in range(planes):
        out_ref[z] = late_ref[:, z].astype(F32).reshape(cols, count).astype(BF16)


def place_late(late, fitted):
    sources, planes, col_count, count = late.shape
    block = 2
    first = (fitted.shape[0] - planes) // block
    return pl.pallas_call(
        place_late_kernel,
        grid=(planes // block,),
        in_specs=[
            pl.BlockSpec((sources, block, col_count, count), lambda i: (0, i, 0, 0)),
            pl.BlockSpec(memory_space=pl.ANY),
        ],
        out_specs=pl.BlockSpec((block, sources * col_count, count), lambda i: (first + i, 0, 0)),
        out_shape=jax.ShapeDtypeStruct(fitted.shape, BF16),
        input_output_aliases={1: 0},
        compiler_params=pltpu.CompilerParams(vmem_limit_bytes=12 << 20),
        cost_estimate=pl.CostEstimate(flops=0, bytes_accessed=2 * late.size * 2, transcendentals=0),
    )(late, fitted)


def per_device(orbitals, points, coulomb):
    gz_count, gy_count = lax.axis_size("gz"), lax.axis_size("gy")
    planes, columns = coulomb.shape
    col_pencil = columns // gz_count
    count = points.shape[0]
    slab_planes = planes // gz_count
    early = EARLY
    weights = lax.dynamic_slice_in_dim(
        coulomb, lax.axis_index("gz") * col_pencil, col_pencil, 1
    ).T
    pencils, at_points, circulant = exchange(
        orbitals, points, weights, gz_count, gy_count, early
    )
    bands = orbitals.shape[0]
    at_points = jnp.transpose(
        at_points.reshape(gy_count, gz_count, 2, bands // 2, count), (2, 1, 0, 3, 4)
    ).reshape(-1, count)
    pencils = jnp.transpose(pencils.reshape(-1, col_pencil, planes), (1, 0, 2))
    first, second = filtered_products(pencils, at_points, circulant, gz_count * early)
    swap = functools.partial(
        lax.all_to_all, axis_name="gz", split_axis=0, concat_axis=0, tiled=True
    )
    slab = swap(first.reshape(gz_count, early, col_pencil, count))
    late, high, low = inverse_and_late_fit(at_points, second.reshape(-1, count))
    late = swap(late.reshape(gz_count, slab_planes - early, col_pencil, count))
    return place_late(late, early_fit(slab, high, low, slab_planes))


def solution(mesh):
    return jax.shard_map(
        per_device,
        mesh=mesh,
        in_specs=(P(("gz", "gy"), None, None), P(), P(None, "gy")),
        out_specs=P("gz", "gy", None),
        check_vma=False,
    )
```

```python
import functools

import jax
import jax.numpy as jnp
import numpy as np
from jax import lax
from jax.experimental import pallas as pl
from jax.experimental.pallas import tpu as pltpu
from jax.sharding import PartitionSpec as P

FULL = lax.Precision.HIGHEST
F32 = jnp.float32
BF16 = jnp.bfloat16
EARLY = 8


def in_hbm(array):
    return pltpu.with_memory_space_constraint(array, pltpu.HBM)


def pick_points(orbital_ref, points_ref, out_ref):
    bands, planes, columns = orbital_ref.shape
    points = points_ref[...]
    point_planes = points // columns
    point_columns = points - point_planes * columns
    count = points.shape[1]
    column_pick = (
        lax.broadcasted_iota(jnp.int32, (columns, count), 0) == point_columns
    ).astype(BF16)
    plane_pick = lax.broadcasted_iota(jnp.int32, (planes, count), 0) == point_planes
    for band in range(bands):
        picked = jnp.dot(orbital_ref[band], column_pick, preferred_element_type=F32)
        values = jnp.sum(jnp.where(plane_pick, picked, 0.0), axis=0, keepdims=True).astype(BF16)
        out_ref[0, band : band + 1, :] = values[:, : count // 2]
        out_ref[1, band : band + 1, :] = values[:, count // 2 :]


def send(source, target, send_sem, recv_sem, device):
    copy = pltpu.make_async_remote_copy(
        src_ref=source,
        dst_ref=target,
        send_sem=send_sem,
        recv_sem=recv_sem,
        device_id=device,
        device_id_type=pl.DeviceIdType.MESH,
    )
    copy.start()
    return copy


def exchange_kernel(
    gz_count,
    gy_count,
    orbital_hbm,
    points_hbm,
    coulomb_hbm,
    left_wave_hbm,
    right_wave_hbm,
    pencil_ref,
    first_value_ref,
    second_value_ref,
    circulant_ref,
    orbital_ref,
    points_ref,
    coulomb_ref,
    left_wave_ref,
    right_wave_ref,
    own_blocks,
    plane_stage,
    row_stage,
    gz_value_stage,
    gy_value_stage,
    own_values,
    first_value_sems,
    second_value_sems,
    gy_first_sems,
    gz_first_sems,
    gz_second_sems,
    gy_second_sems,
    local_sems,
):
    gz, gy = lax.axis_index("gz"), lax.axis_index("gy")
    gy_peers = [lax.rem(gy + d, gy_count) for d in range(1, gy_count)]
    gz_peers = [lax.rem(gz + d, gz_count) for d in range(1, gz_count)]
    barrier = pltpu.get_barrier_semaphore()
    for device in [(gz, peer) for peer in gy_peers] + [(peer, gy) for peer in gz_peers]:
        pl.semaphore_signal(
            barrier, inc=1, device_id=device, device_id_type=pl.DeviceIdType.MESH
        )
    load = [
        pltpu.make_async_copy(points_hbm, points_ref, local_sems.at[9]),
        pltpu.make_async_copy(orbital_hbm, orbital_ref, local_sems.at[0]),
    ]
    for copy in load:
        copy.start()
    load_waves = [
        pltpu.make_async_copy(coulomb_hbm, coulomb_ref, local_sems.at[10]),
        pltpu.make_async_copy(left_wave_hbm, left_wave_ref, local_sems.at[7]),
        pltpu.make_async_copy(right_wave_hbm, right_wave_ref, local_sems.at[8]),
    ]
    for copy in load_waves:
        copy.start()
    for copy in load:
        copy.wait()
    pick_points(orbital_ref, points_ref, own_values)
    bands, planes, columns = orbital_ref.shape
    half = bands // 2
    cols = own_blocks.shape[3]
    width = 256
    for band in range(bands):
        for first in range(0, columns, width):
            turned = orbital_ref[band, :, first : first + width].astype(F32).T
            at = first // cols
            own_blocks[band, at // gz_count : (at + width // cols) // gz_count] = (
                turned.reshape(width // cols // gz_count, gz_count, cols, planes).astype(BF16)
            )
    pl.semaphore_wait(barrier, gy_count + gz_count - 2)

    own = [
        pltpu.make_async_copy(own_values.at[0], gz_value_stage.at[gz], local_sems.at[1]),
        pltpu.make_async_copy(own_values.at[1], gy_value_stage.at[gy], local_sems.at[11]),
        pltpu.make_async_copy(
            own_blocks.at[pl.ds(0, half), gy], plane_stage.at[gy], local_sems.at[2]
        ),
        pltpu.make_async_copy(
            own_blocks.at[pl.ds(half, half), :, gz], row_stage.at[gz], local_sems.at[3]
        ),
    ]
    for copy in own:
        copy.start()
    values = [
        send(
            own_values.at[0],
            gz_value_stage.at[gz],
            first_value_sems.at[0, 0, i],
            first_value_sems.at[0, 1, i],
            (peer, gy),
        )
        for i, peer in enumerate(gz_peers)
    ] + [
        send(
            own_values.at[1],
            gy_value_stage.at[gy],
            first_value_sems.at[1, 0, i],
            first_value_sems.at[1, 1, i],
            (gz, peer),
        )
        for i, peer in enumerate(gy_peers)
    ]
    lower = [
        send(
            own_blocks.at[pl.ds(0, half), peer],
            plane_stage.at[gy],
            gy_first_sems.at[0, i],
            gy_first_sems.at[1, i],
            (gz, peer),
        )
        for i, peer in enumerate(gy_peers)
    ]
    upper = [
        send(
            own_blocks.at[pl.ds(half, half), :, peer],
            row_stage.at[gz],
            gz_first_sems.at[0, i],
            gz_first_sems.at[1, i],
            (peer, gy),
        )
        for i, peer in enumerate(gz_peers)
    ]
    for copy in own:
        copy.wait()
    for copy in values:
        copy.wait_recv()
    values_on = [
        send(
            gz_value_stage,
            first_value_ref.at[gy],
            second_value_sems.at[0, 0, i],
            second_value_sems.at[0, 1, i],
            (gz, peer),
        )
        for i, peer in enumerate(gy_peers)
    ] + [
        send(
            gy_value_stage,
            second_value_ref.at[gz],
            second_value_sems.at[1, 0, i],
            second_value_sems.at[1, 1, i],
            (peer, gy),
        )
        for i, peer in enumerate(gz_peers)
    ]
    for copy in lower:
        copy.wait_recv()
    lower_on = [
        send(
            plane_stage.at[:, :, peer],
            pencil_ref.at[0, gz],
            gz_second_sems.at[0, i],
            gz_second_sems.at[1, i],
            (peer, gy),
        )
        for i, peer in enumerate(gz_peers)
    ]
    for copy in upper:
        copy.wait_recv()
    upper_on = [
        send(
            row_stage.at[:, :, peer],
            pencil_ref.at[1, :, gy],
            gy_second_sems.at[0, i],
            gy_second_sems.at[1, i],
            (gz, peer),
        )
        for i, peer in enumerate(gy_peers)
    ]
    own_on = [
        pltpu.make_async_copy(gz_value_stage, first_value_ref.at[gy], local_sems.at[4]),
        pltpu.make_async_copy(gy_value_stage, second_value_ref.at[gz], local_sems.at[12]),
        pltpu.make_async_copy(plane_stage.at[:, :, gz], pencil_ref.at[0, gz], local_sems.at[5]),
        pltpu.make_async_copy(row_stage.at[:, :, gy], pencil_ref.at[1, :, gy], local_sems.at[6]),
    ]
    for copy in own_on:
        copy.start()
    for copy in load_waves:
        copy.wait()
    all_cols = coulomb_ref.shape[1]
    own_cols = lax.broadcasted_iota(jnp.int32, (cols, all_cols), 0) + gz * cols
    pick = (lax.broadcasted_iota(jnp.int32, (cols, all_cols), 1) == own_cols).astype(F32)
    weights = lax.dot_general(
        pick,
        coulomb_ref[...],
        (((1,), (1,)), ((), ())),
        precision=FULL,
        preferred_element_type=F32,
    ) * (1.0 / planes)
    weights = jnp.concatenate([weights, weights], axis=1)
    for c in range(cols):
        high, low = split_parts(
            jnp.dot(
                left_wave_ref[...] * weights[c : c + 1, :],
                right_wave_ref[...],
                precision=FULL,
                preferred_element_type=F32,
            ),
            2,
        )
        circulant_ref[c] = jnp.concatenate([high, high, low], axis=1)
    for copy in own_on:
        copy.wait()
    for copy in values + lower + upper:
        copy.wait_send()
    for copy in values_on + lower_on + upper_on:
        copy.wait()


def exchange(orbitals, points, coulomb, gz_count, gy_count, early):
    bands, planes, columns = orbitals.shape
    count = points.shape[0]
    cols = coulomb.shape[1] // gz_count
    half = bands // 2
    slab = planes // gz_count
    z = np.arange(planes)
    order = z.reshape(gz_count, slab)
    order = np.concatenate([order[:, :early].ravel(), order[:, early:].ravel()])
    angles = 2.0 * np.pi / planes * (z[:, None] * z % planes)
    waves = np.concatenate([np.cos(angles), np.sin(angles)], axis=1)
    vmem, hbm = (pl.BlockSpec(memory_space=space) for space in (pltpu.VMEM, pltpu.HBM))
    dma = pltpu.SemaphoreType.DMA
    return pl.pallas_call(
        functools.partial(exchange_kernel, gz_count, gy_count),
        in_specs=[hbm, hbm, hbm, hbm, hbm],
        out_specs=(vmem, vmem, vmem, vmem),
        out_shape=(
            jax.ShapeDtypeStruct((2, gz_count, gy_count, half, cols, planes), BF16),
            jax.ShapeDtypeStruct((gy_count, gz_count, bands, count // 2), BF16),
            jax.ShapeDtypeStruct((gz_count, gy_count, bands, count // 2), BF16),
            jax.ShapeDtypeStruct((cols, planes, 3 * planes), BF16),
        ),
        scratch_shapes=[
            pltpu.VMEM((bands, planes, columns), BF16),
            pltpu.VMEM((1, count), jnp.int32),
            pltpu.VMEM(coulomb.shape, F32),
            pltpu.VMEM((planes, 2 * planes), F32),
            pltpu.VMEM((2 * planes, planes), F32),
            pltpu.VMEM((bands, gy_count, gz_count, cols, planes), BF16),
            pltpu.VMEM((gy_count, half, gz_count, cols, planes), BF16),
            pltpu.VMEM((gz_count, half, gy_count, cols, planes), BF16),
            pltpu.VMEM((gz_count, bands, count // 2), BF16),
            pltpu.VMEM((gy_count, bands, count // 2), BF16),
            pltpu.VMEM((2, bands, count // 2), BF16),
            dma((2, 2, gz_count - 1)),
            dma((2, 2, gz_count - 1)),
            dma((2, gy_count - 1)),
            dma((2, gz_count - 1)),
            dma((2, gz_count - 1)),
            dma((2, gy_count - 1)),
            dma((13,)),
        ],
        compiler_params=pltpu.CompilerParams(
            collective_id=0, has_side_effects=True, vmem_limit_bytes=28 << 20
        ),
    )(
        in_hbm(orbitals),
        in_hbm(points.reshape(1, count)),
        in_hbm(coulomb),
        in_hbm(jnp.asarray(waves[order], F32)),
        in_hbm(jnp.asarray(waves.T, F32)),
    )


def split_parts(values, count):
    parts = []
    for _ in range(count):
        part = values.astype(BF16)
        parts.append(part)
        values = values - part.astype(F32)
    return parts


def full_dot(left, right):
    high, middle, low = split_parts(left, 3)
    wide = jnp.concatenate([high, high, middle, high, low, middle], axis=1)
    return jnp.dot(wide, full_stack(right), preferred_element_type=F32)


def full_stack(right):
    high, middle, low = split_parts(right, 3)
    return jnp.concatenate([high, middle, high, low, high, middle], axis=0)


def tree_sum(terms):
    while len(terms) > 1:
        terms = [sum(terms[i : i + 2][1:], terms[i]) for i in range(0, len(terms), 2)]
    return terms[0]


def eliminate_rows(rows, first, lane, sub):
    shape = rows.shape
    columns = [jnp.broadcast_to(rows[:, first + j : first + j + 1], shape) for j in range(8)]
    cell = {
        (i, j): jnp.broadcast_to(columns[j][i : i + 1, :], shape)
        for j in range(8)
        for i in range(j + 1)
    }
    for k in range(8):
        recip = 1.0 / cell[k, k]
        side = {i: cell[min(i, k), max(i, k)] for i in range(8) if i != k}
        scaled = {i: side[i] * recip for i in side}
        swept = {}
        for i, j in cell:
            if i == k and j == k:
                swept[i, j] = -recip
            elif i == k or j == k:
                swept[i, j] = scaled[j if i == k else i]
            else:
                swept[i, j] = cell[i, j] - side[i] * scaled[j]
        cell = swept
    inside = (lane >= first) & (lane < first + 8)
    source = [
        jnp.where(
            inside,
            jnp.where(lane == first + j, -1.0, 0.0),
            -jnp.broadcast_to(rows[j : j + 1, :], shape),
        )
        for j in range(8)
    ]
    results = [
        tree_sum([cell[min(i, j), max(i, j)] * source[j] for j in range(8)]) for i in range(8)
    ]
    panel = results[0]
    for i in range(1, 8):
        panel = jnp.where(sub == i, results[i], panel)
    return results, panel, inside


def small_inverse(block):
    size = block.shape[0]
    group_rows = 32
    tiles = [block[i : i + 8, :] for i in range(0, size, 8)]
    lane = lax.broadcasted_iota(jnp.int32, (8, size), 1)
    sub = lax.broadcasted_iota(jnp.int32, (8, size), 0)
    per_group = group_rows // 8
    for start in range(0, size, group_rows):
        group = list(range(start // 8, start // 8 + per_group))
        for at in group:
            results, panel, inside = eliminate_rows(tiles[at], at * 8, lane, sub)
            for step in range(1, per_group):
                other = group[(at - group[0] + step) % per_group]
                terms = [
                    jnp.broadcast_to(tiles[other][:, at * 8 + j : at * 8 + j + 1], (8, size))
                    * results[j]
                    for j in range(8)
                ]
                tiles[other] = jnp.where(inside, 0.0, tiles[other]) - tree_sum(terms)
            tiles[at] = panel
        rest = [i for i in range(len(tiles)) if i not in group]
        panel = jnp.concatenate([tiles[i] for i in group], axis=0)
        stack = jnp.concatenate([tiles[i] for i in rest], axis=0)
        change = full_dot(stack[:, start : start + group_rows], panel)
        wide_lane = lax.broadcasted_iota(jnp.int32, stack.shape, 1)
        in_group = (wide_lane >= start) & (wide_lane < start + group_rows)
        stack = jnp.where(in_group, 0.0, stack) - change
        for place, i in enumerate(rest):
            tiles[i] = stack[place * 8 : place * 8 + 8, :]
    return jnp.concatenate(tiles, axis=0)


def inverse_kernel(
    width, point_ref, late_ref, fitted_ref, high_out, low_out, work, high_ref, low_ref
):
    size = work.shape[0]
    block = 256

    @pl.when(pl.program_id(0) == 0)
    def _():
        for first in range(0, size, block):
            base = lax.dot_general(
                point_ref[:, first : first + block],
                point_ref[...],
                (((0,), (0,)), ((), ())),
                preferred_element_type=F32,
            )
            work[first : first + block, :] = base * base

        def eliminate(k, carry):
            at = pl.ds(pl.multiple_of(k * width, width), width)
            pivot = small_inverse(work[at, at])
            work[at, :] = full_dot(pivot, work[at, :])
            work[at, at] = pivot
            panel = work[at, :]
            stacked = full_stack(panel)
            high, middle, low = split_parts(work[:, at], 3)
            wide = jnp.concatenate([high, high, middle, high, low, middle], axis=1)
            work[:, at] = jnp.zeros((size, width), F32)
            for first in range(0, size, block):
                columns = slice(first, first + block)
                change = jnp.dot(wide, stacked[:, columns], preferred_element_type=F32)
                work[:, columns] = work[:, columns] - change
            work[at, :] = panel
            return carry

        lax.fori_loop(0, size // width, eliminate, 0)
        for first in range(0, size, block):
            rows = slice(first, first + block)
            high, low = split_parts(work[rows, :], 2)
            high_ref[rows, :] = high
            low_ref[rows, :] = low

    @pl.when(pl.program_id(0) > 0)
    def _():
        rows = pl.ds(pl.multiple_of((pl.program_id(0) - 1) * block, block), block)
        high_out[...] = high_ref[rows, :]
        low_out[...] = low_ref[rows, :]
        fitted_ref[...] = fit_rows(late_ref[...], high_ref, low_ref)


def inverse_and_late_fit(at_points, late):
    size = at_points.shape[1]
    block = 256
    steps = late.shape[0] // block
    assert steps == size // block
    rows = pl.BlockSpec((block, size), lambda i: (jnp.maximum(i - 1, 0), 0))
    return pl.pallas_call(
        functools.partial(inverse_kernel, 128),
        grid=(1 + steps,),
        in_specs=[pl.BlockSpec(at_points.shape, lambda i: (0, 0)), rows],
        out_specs=(rows, rows, rows),
        out_shape=(
            pltpu.HBM(late.shape, BF16),
            pltpu.HBM((size, size), BF16),
            pltpu.HBM((size, size), BF16),
        ),
        scratch_shapes=[
            pltpu.VMEM((size, size), F32),
            pltpu.VMEM((size, size), BF16),
            pltpu.VMEM((size, size), BF16),
        ],
        compiler_params=pltpu.CompilerParams(vmem_limit_bytes=36 << 20),
        cost_estimate=pl.CostEstimate(
            flops=60 * size**3, bytes_accessed=8 * size * size, transcendentals=0
        ),
    )(at_points, in_hbm(late))


def filter_kernel(pencil_ref, point_ref, circulant_ref, early_ref, late_ref):
    early = early_ref.shape[0]
    col_count = pencil_ref.shape[0]

    def products(c):
        sums = lax.dot_general(
            pencil_ref[c], point_ref[...], (((0,), (0,)), ((), ())), preferred_element_type=F32
        )
        return split_parts(sums * sums, 2)

    following = products(0)
    for c in range(col_count):
        high, low = following
        if c + 1 < col_count:
            following = products(c + 1)
        smooth = jnp.dot(
            circulant_ref[c],
            jnp.concatenate([high, low, high], axis=0),
            preferred_element_type=F32,
        )
        early_ref[:, c, :] = smooth[:early]
        late_ref[:, c, :] = smooth[early:]


def filtered_products(pencils, at_points, circulant, early):
    col_count, bands, planes = pencils.shape
    count = at_points.shape[1]
    late = planes - early
    chunk = 256
    return pl.pallas_call(
        filter_kernel,
        grid=(count // chunk,),
        in_specs=[
            pl.BlockSpec(pencils.shape, lambda i: (0, 0, 0)),
            pl.BlockSpec((bands, chunk), lambda i: (0, i)),
            pl.BlockSpec(circulant.shape, lambda i: (0, 0, 0)),
        ],
        out_specs=[
            pl.BlockSpec((early, col_count, chunk), lambda i: (0, 0, i)),
            pl.BlockSpec((late, col_count, chunk), lambda i: (0, 0, i)),
        ],
        out_shape=[
            pltpu.HBM((early, col_count, count), F32),
            pltpu.HBM((late, col_count, count), F32),
        ],
        compiler_params=pltpu.CompilerParams(vmem_limit_bytes=28 << 20),
        cost_estimate=pl.CostEstimate(
            flops=8 * col_count * planes * bands * count, bytes_accessed=10 << 20, transcendentals=0
        ),
    )(pencils, at_points, circulant)


def fit_rows(rows, high_ref, low_ref):
    high, low = split_parts(rows, 2)
    dot = functools.partial(jnp.dot, preferred_element_type=F32)
    return (
        dot(high, high_ref[...]) + (dot(low, high_ref[...]) + dot(high, low_ref[...]))
    ).astype(BF16)


def early_fit_kernel(rows_ref, high_ref, low_ref, out_ref):
    planes, cols, count = out_ref.shape
    rows = jnp.concatenate(
        [rows_ref[:, z].reshape(cols, count) for z in range(planes)], axis=0
    )
    out_ref[...] = fit_rows(rows, high_ref, low_ref).reshape(planes, cols, count)


def early_fit(slab, high, low, total_planes):
    sources, early, col_count, count = slab.shape
    block = 2
    whole = pl.BlockSpec((count, count), lambda i: (0, 0))
    return pl.pallas_call(
        early_fit_kernel,
        grid=(early // block,),
        in_specs=[
            pl.BlockSpec((sources, block, col_count, count), lambda i: (0, i, 0, 0)),
            whole,
            whole,
        ],
        out_specs=pl.BlockSpec((block, sources * col_count, count), lambda i: (i, 0, 0)),
        out_shape=jax.ShapeDtypeStruct((total_planes, sources * col_count, count), BF16),
        compiler_params=pltpu.CompilerParams(vmem_limit_bytes=24 << 20),
        cost_estimate=pl.CostEstimate(
            flops=6 * slab.size * count, bytes_accessed=10 << 20, transcendentals=0
        ),
    )(slab, high, low)


def place_late_kernel(late_ref, _, out_ref):
    planes, cols, count = out_ref.shape
    for z in range(planes):
        out_ref[z] = late_ref[:, z].astype(F32).reshape(cols, count).astype(BF16)


def place_late(late, fitted):
    sources, planes, col_count, count = late.shape
    block = 2
    first = (fitted.shape[0] - planes) // block
    return pl.pallas_call(
        place_late_kernel,
        grid=(planes // block,),
        in_specs=[
            pl.BlockSpec((sources, block, col_count, count), lambda i: (0, i, 0, 0)),
            pl.BlockSpec(memory_space=pl.ANY),
        ],
        out_specs=pl.BlockSpec((block, sources * col_count, count), lambda i: (first + i, 0, 0)),
        out_shape=jax.ShapeDtypeStruct(fitted.shape, BF16),
        input_output_aliases={1: 0},
        compiler_params=pltpu.CompilerParams(vmem_limit_bytes=12 << 20),
        cost_estimate=pl.CostEstimate(flops=0, bytes_accessed=2 * late.size * 2, transcendentals=0),
    )(late, fitted)


def per_device(orbitals, points, coulomb):
    gz_count, gy_count = lax.axis_size("gz"), lax.axis_size("gy")
    planes, columns = coulomb.shape
    col_pencil = columns // gz_count
    count = points.shape[0]
    slab_planes = planes // gz_count
    early = EARLY
    pencils, first_values, second_values, circulant = exchange(
        orbitals, points, coulomb, gz_count, gy_count, early
    )
    split = (2, orbitals.shape[0] // 2, count // 2)
    at_points = jnp.concatenate(
        [
            jnp.transpose(first_values.reshape(gy_count, gz_count, *split), (2, 1, 0, 3, 4)),
            jnp.transpose(second_values.reshape(gz_count, gy_count, *split), (2, 0, 1, 3, 4)),
        ],
        axis=4,
    ).reshape(-1, count)
    pencils = jnp.transpose(pencils.reshape(-1, col_pencil, planes), (1, 0, 2))
    first, second = filtered_products(pencils, at_points, circulant, gz_count * early)
    swap = functools.partial(
        lax.all_to_all, axis_name="gz", split_axis=0, concat_axis=0, tiled=True
    )
    slab = swap(first.reshape(gz_count, early, col_pencil, count))
    late, high, low = inverse_and_late_fit(at_points, second.reshape(-1, count))
    late = swap(late.reshape(gz_count, slab_planes - early, col_pencil, count))
    return place_late(late, early_fit(slab, high, low, slab_planes))


def solution(mesh):
    return jax.shard_map(
        per_device,
        mesh=mesh,
        in_specs=(P(("gz", "gy"), None, None), P(), P(None, "gy")),
        out_specs=P("gz", "gy", None),
        check_vma=False,
    )
```

```python
import functools

import jax
import jax.numpy as jnp
import numpy as np
from jax import lax
from jax.experimental import pallas as pl
from jax.experimental.pallas import tpu as pltpu
from jax.sharding import PartitionSpec as P

FULL = lax.Precision.HIGHEST
F32 = jnp.float32
BF16 = jnp.bfloat16
EARLY = 8


def in_hbm(array):
    return pltpu.with_memory_space_constraint(array, pltpu.HBM)


def pick_points(orbital_ref, points_ref, out_ref):
    bands, planes, columns = orbital_ref.shape
    points = points_ref[...]
    point_planes = points // columns
    point_columns = points - point_planes * columns
    count = points.shape[1]
    column_pick = (
        lax.broadcasted_iota(jnp.int32, (columns, count), 0) == point_columns
    ).astype(BF16)
    plane_pick = lax.broadcasted_iota(jnp.int32, (planes, count), 0) == point_planes
    for band in range(bands):
        picked = jnp.dot(orbital_ref[band], column_pick, preferred_element_type=F32)
        values = jnp.sum(jnp.where(plane_pick, picked, 0.0), axis=0, keepdims=True).astype(BF16)
        out_ref[0, band : band + 1, :] = values[:, : count // 2]
        out_ref[1, band : band + 1, :] = values[:, count // 2 :]


def send(source, target, send_sem, recv_sem, device):
    copy = pltpu.make_async_remote_copy(
        src_ref=source,
        dst_ref=target,
        send_sem=send_sem,
        recv_sem=recv_sem,
        device_id=device,
        device_id_type=pl.DeviceIdType.MESH,
    )
    copy.start()
    return copy


def exchange_kernel(
    gz_count,
    gy_count,
    orbital_hbm,
    points_hbm,
    coulomb_hbm,
    left_wave_hbm,
    right_wave_hbm,
    pencil_ref,
    first_value_ref,
    second_value_ref,
    circulant_ref,
    orbital_ref,
    points_ref,
    coulomb_ref,
    left_wave_ref,
    right_wave_ref,
    own_blocks,
    plane_stage,
    row_stage,
    gz_value_stage,
    gy_value_stage,
    own_values,
    first_value_sems,
    second_value_sems,
    gy_first_sems,
    gz_first_sems,
    gz_second_sems,
    gy_second_sems,
    local_sems,
):
    gz, gy = lax.axis_index("gz"), lax.axis_index("gy")
    gy_peers = [lax.rem(gy + d, gy_count) for d in range(1, gy_count)]
    gz_peers = [lax.rem(gz + d, gz_count) for d in range(1, gz_count)]
    barrier = pltpu.get_barrier_semaphore()
    for device in [(gz, peer) for peer in gy_peers] + [(peer, gy) for peer in gz_peers]:
        pl.semaphore_signal(
            barrier, inc=1, device_id=device, device_id_type=pl.DeviceIdType.MESH
        )
    load = [
        pltpu.make_async_copy(points_hbm, points_ref, local_sems.at[9]),
        pltpu.make_async_copy(orbital_hbm, orbital_ref, local_sems.at[0]),
    ]
    for copy in load:
        copy.start()
    load_waves = [
        pltpu.make_async_copy(coulomb_hbm, coulomb_ref, local_sems.at[10]),
        pltpu.make_async_copy(left_wave_hbm, left_wave_ref, local_sems.at[7]),
        pltpu.make_async_copy(right_wave_hbm, right_wave_ref, local_sems.at[8]),
    ]
    for copy in load_waves:
        copy.start()
    for copy in load:
        copy.wait()
    pick_points(orbital_ref, points_ref, own_values)
    bands, planes, columns = orbital_ref.shape
    half = bands // 2
    cols = own_blocks.shape[3]
    width = 256
    for band in range(bands):
        for first in range(0, columns, width):
            turned = orbital_ref[band, :, first : first + width].astype(F32).T
            at = first // cols
            own_blocks[band, at // gz_count : (at + width // cols) // gz_count] = (
                turned.reshape(width // cols // gz_count, gz_count, cols, planes).astype(BF16)
            )
    pl.semaphore_wait(barrier, gy_count + gz_count - 2)

    own = [
        pltpu.make_async_copy(own_values.at[0], gz_value_stage.at[gz], local_sems.at[1]),
        pltpu.make_async_copy(own_values.at[1], gy_value_stage.at[gy], local_sems.at[11]),
        pltpu.make_async_copy(
            own_blocks.at[pl.ds(0, half), gy], plane_stage.at[gy], local_sems.at[2]
        ),
        pltpu.make_async_copy(
            own_blocks.at[pl.ds(half, half), :, gz], row_stage.at[gz], local_sems.at[3]
        ),
    ]
    for copy in own:
        copy.start()
    values = [
        send(
            own_values.at[0],
            gz_value_stage.at[gz],
            first_value_sems.at[0, 0, i],
            first_value_sems.at[0, 1, i],
            (peer, gy),
        )
        for i, peer in enumerate(gz_peers)
    ] + [
        send(
            own_values.at[1],
            gy_value_stage.at[gy],
            first_value_sems.at[1, 0, i],
            first_value_sems.at[1, 1, i],
            (gz, peer),
        )
        for i, peer in enumerate(gy_peers)
    ]
    lower = [
        send(
            own_blocks.at[pl.ds(0, half), peer],
            plane_stage.at[gy],
            gy_first_sems.at[0, i],
            gy_first_sems.at[1, i],
            (gz, peer),
        )
        for i, peer in enumerate(gy_peers)
    ]
    upper = [
        send(
            own_blocks.at[pl.ds(half, half), :, peer],
            row_stage.at[gz],
            gz_first_sems.at[0, i],
            gz_first_sems.at[1, i],
            (peer, gy),
        )
        for i, peer in enumerate(gz_peers)
    ]
    for copy in own:
        copy.wait()
    for copy in values:
        copy.wait_recv()
    values_on = [
        send(
            gz_value_stage,
            first_value_ref.at[gy],
            second_value_sems.at[0, 0, i],
            second_value_sems.at[0, 1, i],
            (gz, peer),
        )
        for i, peer in enumerate(gy_peers)
    ] + [
        send(
            gy_value_stage,
            second_value_ref.at[gz],
            second_value_sems.at[1, 0, i],
            second_value_sems.at[1, 1, i],
            (peer, gy),
        )
        for i, peer in enumerate(gz_peers)
    ]
    for copy in lower:
        copy.wait_recv()
    lower_on = [
        send(
            plane_stage.at[:, :, peer],
            pencil_ref.at[0, gz],
            gz_second_sems.at[0, i],
            gz_second_sems.at[1, i],
            (peer, gy),
        )
        for i, peer in enumerate(gz_peers)
    ]
    for copy in upper:
        copy.wait_recv()
    upper_on = [
        send(
            row_stage.at[:, :, peer],
            pencil_ref.at[1, :, gy],
            gy_second_sems.at[0, i],
            gy_second_sems.at[1, i],
            (gz, peer),
        )
        for i, peer in enumerate(gy_peers)
    ]
    own_on = [
        pltpu.make_async_copy(gz_value_stage, first_value_ref.at[gy], local_sems.at[4]),
        pltpu.make_async_copy(gy_value_stage, second_value_ref.at[gz], local_sems.at[12]),
        pltpu.make_async_copy(plane_stage.at[:, :, gz], pencil_ref.at[0, gz], local_sems.at[5]),
        pltpu.make_async_copy(row_stage.at[:, :, gy], pencil_ref.at[1, :, gy], local_sems.at[6]),
    ]
    for copy in own_on:
        copy.start()
    for copy in load_waves:
        copy.wait()
    all_cols = coulomb_ref.shape[1]
    own_cols = lax.broadcasted_iota(jnp.int32, (cols, all_cols), 0) + gz * cols
    pick = (lax.broadcasted_iota(jnp.int32, (cols, all_cols), 1) == own_cols).astype(F32)
    weights = lax.dot_general(
        pick,
        coulomb_ref[...],
        (((1,), (1,)), ((), ())),
        precision=FULL,
        preferred_element_type=F32,
    ) * (1.0 / planes)
    weights = jnp.concatenate([weights, weights], axis=1)
    for c in range(cols):
        high, low = split_parts(
            jnp.dot(
                left_wave_ref[...] * weights[c : c + 1, :],
                right_wave_ref[...],
                precision=FULL,
                preferred_element_type=F32,
            ),
            2,
        )
        circulant_ref[c] = jnp.concatenate([high, high, low], axis=1)
    for copy in own_on:
        copy.wait()
    for copy in values + lower + upper:
        copy.wait_send()
    for copy in values_on + lower_on + upper_on:
        copy.wait()


def exchange(orbitals, points, coulomb, gz_count, gy_count, early):
    bands, planes, columns = orbitals.shape
    count = points.shape[0]
    cols = coulomb.shape[1] // gz_count
    half = bands // 2
    slab = planes // gz_count
    z = np.arange(planes)
    order = z.reshape(gz_count, slab)
    order = np.concatenate([order[:, :early].ravel(), order[:, early:].ravel()])
    angles = 2.0 * np.pi / planes * (z[:, None] * z % planes)
    waves = np.concatenate([np.cos(angles), np.sin(angles)], axis=1)
    vmem, hbm = (pl.BlockSpec(memory_space=space) for space in (pltpu.VMEM, pltpu.HBM))
    dma = pltpu.SemaphoreType.DMA
    return pl.pallas_call(
        functools.partial(exchange_kernel, gz_count, gy_count),
        in_specs=[hbm, hbm, hbm, hbm, hbm],
        out_specs=(vmem, vmem, vmem, vmem),
        out_shape=(
            jax.ShapeDtypeStruct((2, gz_count, gy_count, half, cols, planes), BF16),
            jax.ShapeDtypeStruct((gy_count, gz_count, bands, count // 2), BF16),
            jax.ShapeDtypeStruct((gz_count, gy_count, bands, count // 2), BF16),
            jax.ShapeDtypeStruct((cols, planes, 3 * planes), BF16),
        ),
        scratch_shapes=[
            pltpu.VMEM((bands, planes, columns), BF16),
            pltpu.VMEM((1, count), jnp.int32),
            pltpu.VMEM(coulomb.shape, F32),
            pltpu.VMEM((planes, 2 * planes), F32),
            pltpu.VMEM((2 * planes, planes), F32),
            pltpu.VMEM((bands, gy_count, gz_count, cols, planes), BF16),
            pltpu.VMEM((gy_count, half, gz_count, cols, planes), BF16),
            pltpu.VMEM((gz_count, half, gy_count, cols, planes), BF16),
            pltpu.VMEM((gz_count, bands, count // 2), BF16),
            pltpu.VMEM((gy_count, bands, count // 2), BF16),
            pltpu.VMEM((2, bands, count // 2), BF16),
            dma((2, 2, gz_count - 1)),
            dma((2, 2, gz_count - 1)),
            dma((2, gy_count - 1)),
            dma((2, gz_count - 1)),
            dma((2, gz_count - 1)),
            dma((2, gy_count - 1)),
            dma((13,)),
        ],
        compiler_params=pltpu.CompilerParams(
            collective_id=0, has_side_effects=True, vmem_limit_bytes=28 << 20
        ),
    )(
        in_hbm(orbitals),
        in_hbm(points.reshape(1, count)),
        in_hbm(coulomb),
        in_hbm(jnp.asarray(waves[order], F32)),
        in_hbm(jnp.asarray(waves.T, F32)),
    )


def split_parts(values, count):
    parts = []
    for _ in range(count):
        part = values.astype(BF16)
        parts.append(part)
        values = values - part.astype(F32)
    return parts


def full_dot(left, right):
    return jnp.dot(left_stack(left), right_stack(right), preferred_element_type=F32)


def left_stack(left):
    high, middle, low = split_parts(left, 3)
    return jnp.concatenate([high, high, middle, high, low, middle], axis=1)


def right_stack(right):
    high, middle, low = split_parts(right, 3)
    return jnp.concatenate([high, middle, high, low, high, middle], axis=0)


def tree_sum(terms):
    while len(terms) > 1:
        terms = [sum(terms[i : i + 2][1:], terms[i]) for i in range(0, len(terms), 2)]
    return terms[0]


def eliminate_rows(rows, first, lane, sub):
    shape = rows.shape
    columns = [jnp.broadcast_to(rows[:, first + j : first + j + 1], shape) for j in range(8)]
    cell = {
        (i, j): jnp.broadcast_to(columns[j][i : i + 1, :], shape)
        for j in range(8)
        for i in range(j + 1)
    }
    for k in range(8):
        recip = 1.0 / cell[k, k]
        side = {i: cell[min(i, k), max(i, k)] for i in range(8) if i != k}
        scaled = {i: side[i] * recip for i in side}
        swept = {}
        for i, j in cell:
            if i == k and j == k:
                swept[i, j] = -recip
            elif i == k or j == k:
                swept[i, j] = scaled[j if i == k else i]
            else:
                swept[i, j] = cell[i, j] - side[i] * scaled[j]
        cell = swept
    inside = (lane >= first) & (lane < first + 8)
    source = [
        jnp.where(
            inside,
            jnp.where(lane == first + j, -1.0, 0.0),
            -jnp.broadcast_to(rows[j : j + 1, :], shape),
        )
        for j in range(8)
    ]
    results = [
        tree_sum([cell[min(i, j), max(i, j)] * source[j] for j in range(8)]) for i in range(8)
    ]
    panel = results[0]
    for i in range(1, 8):
        panel = jnp.where(sub == i, results[i], panel)
    return results, panel, inside


def small_inverse(block):
    size = block.shape[0]
    tiles = [block[i : i + 8, :] for i in range(0, size, 8)]
    lane = lax.broadcasted_iota(jnp.int32, (8, size), 1)
    sub = lax.broadcasted_iota(jnp.int32, (8, size), 0)
    for at in range(len(tiles)):
        first = at * 8
        following = [at + 1] if at + 1 < len(tiles) else []
        rest = [i for i in range(len(tiles)) if i != at and i not in following]
        stack = jnp.concatenate([tiles[i] for i in rest], axis=0)
        wide_lane = lax.broadcasted_iota(jnp.int32, stack.shape, 1)
        kept = jnp.where((wide_lane >= first) & (wide_lane < first + 8), 0.0, stack)
        wide = left_stack(stack[:, first : first + 8])
        results, panel, inside = eliminate_rows(tiles[at], first, lane, sub)
        for other in following:
            terms = [
                jnp.broadcast_to(tiles[other][:, first + j : first + j + 1], (8, size)) * results[j]
                for j in range(8)
            ]
            tiles[other] = jnp.where(inside, 0.0, tiles[other]) - tree_sum(terms)
        stack = kept - jnp.dot(wide, right_stack(panel), preferred_element_type=F32)
        for place, i in enumerate(rest):
            tiles[i] = stack[place * 8 : place * 8 + 8, :]
        tiles[at] = panel
    return jnp.concatenate(tiles, axis=0)


def inverse_kernel(
    width, point_ref, late_ref, fitted_ref, high_out, low_out, work, high_ref, low_ref
):
    size = work.shape[0]
    block = 256

    @pl.when(pl.program_id(0) == 0)
    def _():
        for first in range(0, size, block):
            base = lax.dot_general(
                point_ref[:, first : first + block],
                point_ref[...],
                (((0,), (0,)), ((), ())),
                preferred_element_type=F32,
            )
            work[first : first + block, :] = base * base

        def eliminate(k, carry):
            at = pl.ds(pl.multiple_of(k * width, width), width)
            pivot = small_inverse(work[at, at])
            work[at, :] = full_dot(pivot, work[at, :])
            work[at, at] = pivot
            panel = work[at, :]
            stacked = right_stack(panel)
            wide = left_stack(work[:, at])
            work[:, at] = jnp.zeros((size, width), F32)
            for first in range(0, size, block):
                columns = slice(first, first + block)
                change = jnp.dot(wide, stacked[:, columns], preferred_element_type=F32)
                work[:, columns] = work[:, columns] - change
            work[at, :] = panel
            return carry

        lax.fori_loop(0, size // width, eliminate, 0)
        for first in range(0, size, block):
            rows = slice(first, first + block)
            high, low = split_parts(work[rows, :], 2)
            high_ref[rows, :] = high
            low_ref[rows, :] = low

    @pl.when(pl.program_id(0) > 0)
    def _():
        rows = pl.ds(pl.multiple_of((pl.program_id(0) - 1) * block, block), block)
        high_out[...] = high_ref[rows, :]
        low_out[...] = low_ref[rows, :]
        fitted_ref[...] = fit_rows(late_ref[...], high_ref, low_ref)


def inverse_and_late_fit(at_points, late):
    size = at_points.shape[1]
    block = 256
    steps = late.shape[0] // block
    assert steps == size // block
    rows = pl.BlockSpec((block, size), lambda i: (jnp.maximum(i - 1, 0), 0))
    return pl.pallas_call(
        functools.partial(inverse_kernel, 128),
        grid=(1 + steps,),
        in_specs=[pl.BlockSpec(at_points.shape, lambda i: (0, 0)), rows],
        out_specs=(rows, rows, rows),
        out_shape=(
            pltpu.HBM(late.shape, BF16),
            pltpu.HBM((size, size), BF16),
            pltpu.HBM((size, size), BF16),
        ),
        scratch_shapes=[
            pltpu.VMEM((size, size), F32),
            pltpu.VMEM((size, size), BF16),
            pltpu.VMEM((size, size), BF16),
        ],
        compiler_params=pltpu.CompilerParams(vmem_limit_bytes=36 << 20),
        cost_estimate=pl.CostEstimate(
            flops=60 * size**3, bytes_accessed=8 * size * size, transcendentals=0
        ),
    )(at_points, in_hbm(late))


def filter_kernel(pencil_ref, point_ref, circulant_ref, early_ref, late_ref):
    early = early_ref.shape[0]
    col_count = pencil_ref.shape[0]

    def products(c):
        sums = lax.dot_general(
            pencil_ref[c], point_ref[...], (((0,), (0,)), ((), ())), preferred_element_type=F32
        )
        return split_parts(sums * sums, 2)

    following = products(0)
    for c in range(col_count):
        high, low = following
        if c + 1 < col_count:
            following = products(c + 1)
        smooth = jnp.dot(
            circulant_ref[c],
            jnp.concatenate([high, low, high], axis=0),
            preferred_element_type=F32,
        )
        early_ref[:, c, :] = smooth[:early]
        late_ref[:, c, :] = smooth[early:]


def filtered_products(pencils, at_points, circulant, early):
    col_count, bands, planes = pencils.shape
    count = at_points.shape[1]
    late = planes - early
    chunk = 256
    return pl.pallas_call(
        filter_kernel,
        grid=(count // chunk,),
        in_specs=[
            pl.BlockSpec(pencils.shape, lambda i: (0, 0, 0)),
            pl.BlockSpec((bands, chunk), lambda i: (0, i)),
            pl.BlockSpec(circulant.shape, lambda i: (0, 0, 0)),
        ],
        out_specs=[
            pl.BlockSpec((early, col_count, chunk), lambda i: (0, 0, i)),
            pl.BlockSpec((late, col_count, chunk), lambda i: (0, 0, i)),
        ],
        out_shape=[
            pltpu.HBM((early, col_count, count), F32),
            pltpu.HBM((late, col_count, count), F32),
        ],
        compiler_params=pltpu.CompilerParams(vmem_limit_bytes=28 << 20),
        cost_estimate=pl.CostEstimate(
            flops=8 * col_count * planes * bands * count, bytes_accessed=10 << 20, transcendentals=0
        ),
    )(pencils, at_points, circulant)


def fit_rows(rows, high_ref, low_ref):
    high, low = split_parts(rows, 2)
    dot = functools.partial(jnp.dot, preferred_element_type=F32)
    return (
        dot(high, high_ref[...]) + (dot(low, high_ref[...]) + dot(high, low_ref[...]))
    ).astype(BF16)


def early_fit_kernel(rows_ref, high_ref, low_ref, out_ref):
    planes, cols, count = out_ref.shape
    rows = jnp.concatenate(
        [rows_ref[:, z].reshape(cols, count) for z in range(planes)], axis=0
    )
    out_ref[...] = fit_rows(rows, high_ref, low_ref).reshape(planes, cols, count)


def early_fit(slab, high, low, total_planes):
    sources, early, col_count, count = slab.shape
    block = 2
    whole = pl.BlockSpec((count, count), lambda i: (0, 0))
    return pl.pallas_call(
        early_fit_kernel,
        grid=(early // block,),
        in_specs=[
            pl.BlockSpec((sources, block, col_count, count), lambda i: (0, i, 0, 0)),
            whole,
            whole,
        ],
        out_specs=pl.BlockSpec((block, sources * col_count, count), lambda i: (i, 0, 0)),
        out_shape=jax.ShapeDtypeStruct((total_planes, sources * col_count, count), BF16),
        compiler_params=pltpu.CompilerParams(vmem_limit_bytes=24 << 20),
        cost_estimate=pl.CostEstimate(
            flops=6 * slab.size * count, bytes_accessed=10 << 20, transcendentals=0
        ),
    )(slab, high, low)


def place_late_kernel(late_ref, _, out_ref):
    planes, cols, count = out_ref.shape
    for z in range(planes):
        out_ref[z] = late_ref[:, z].astype(F32).reshape(cols, count).astype(BF16)


def place_late(late, fitted):
    sources, planes, col_count, count = late.shape
    block = 2
    first = (fitted.shape[0] - planes) // block
    return pl.pallas_call(
        place_late_kernel,
        grid=(planes // block,),
        in_specs=[
            pl.BlockSpec((sources, block, col_count, count), lambda i: (0, i, 0, 0)),
            pl.BlockSpec(memory_space=pl.ANY),
        ],
        out_specs=pl.BlockSpec((block, sources * col_count, count), lambda i: (first + i, 0, 0)),
        out_shape=jax.ShapeDtypeStruct(fitted.shape, BF16),
        input_output_aliases={1: 0},
        compiler_params=pltpu.CompilerParams(vmem_limit_bytes=12 << 20),
        cost_estimate=pl.CostEstimate(flops=0, bytes_accessed=2 * late.size * 2, transcendentals=0),
    )(late, fitted)


def per_device(orbitals, points, coulomb):
    gz_count, gy_count = lax.axis_size("gz"), lax.axis_size("gy")
    planes, columns = coulomb.shape
    col_pencil = columns // gz_count
    count = points.shape[0]
    slab_planes = planes // gz_count
    early = EARLY
    pencils, first_values, second_values, circulant = exchange(
        orbitals, points, coulomb, gz_count, gy_count, early
    )
    split = (2, orbitals.shape[0] // 2, count // 2)
    at_points = jnp.concatenate(
        [
            jnp.transpose(first_values.reshape(gy_count, gz_count, *split), (2, 1, 0, 3, 4)),
            jnp.transpose(second_values.reshape(gz_count, gy_count, *split), (2, 0, 1, 3, 4)),
        ],
        axis=4,
    ).reshape(-1, count)
    pencils = jnp.transpose(pencils.reshape(-1, col_pencil, planes), (1, 0, 2))
    first, second = filtered_products(pencils, at_points, circulant, gz_count * early)
    swap = functools.partial(
        lax.all_to_all, axis_name="gz", split_axis=0, concat_axis=0, tiled=True
    )
    slab = swap(first.reshape(gz_count, early, col_pencil, count))
    late, high, low = inverse_and_late_fit(at_points, second.reshape(-1, count))
    late = swap(late.reshape(gz_count, slab_planes - early, col_pencil, count))
    return place_late(late, early_fit(slab, high, low, slab_planes))


def solution(mesh):
    return jax.shard_map(
        per_device,
        mesh=mesh,
        in_specs=(P(("gz", "gy"), None, None), P(), P(None, "gy")),
        out_specs=P("gz", "gy", None),
        check_vma=False,
    )
```

```python
import functools

import jax
import jax.numpy as jnp
import numpy as np
from jax import lax
from jax.experimental import pallas as pl
from jax.experimental.pallas import tpu as pltpu
from jax.sharding import PartitionSpec as P

FULL = lax.Precision.HIGHEST
F32 = jnp.float32
BF16 = jnp.bfloat16
EARLY = 8


def in_hbm(array):
    return pltpu.with_memory_space_constraint(array, pltpu.HBM)


def pick_points(orbital_ref, points_ref, out_ref):
    bands, planes, columns = orbital_ref.shape
    points = points_ref[...]
    point_planes = points // columns
    point_columns = points - point_planes * columns
    count = points.shape[1]
    column_pick = (
        lax.broadcasted_iota(jnp.int32, (columns, count), 0) == point_columns
    ).astype(BF16)
    plane_pick = lax.broadcasted_iota(jnp.int32, (planes, count), 0) == point_planes
    for band in range(bands):
        picked = jnp.dot(orbital_ref[band], column_pick, preferred_element_type=F32)
        values = jnp.sum(jnp.where(plane_pick, picked, 0.0), axis=0, keepdims=True).astype(BF16)
        out_ref[0, band : band + 1, :] = values[:, : count // 2]
        out_ref[1, band : band + 1, :] = values[:, count // 2 :]


def send(source, target, send_sem, recv_sem, device):
    copy = pltpu.make_async_remote_copy(
        src_ref=source,
        dst_ref=target,
        send_sem=send_sem,
        recv_sem=recv_sem,
        device_id=device,
        device_id_type=pl.DeviceIdType.MESH,
    )
    copy.start()
    return copy


def exchange_kernel(
    gz_count,
    gy_count,
    orbital_hbm,
    points_hbm,
    coulomb_hbm,
    left_wave_hbm,
    right_wave_hbm,
    pencil_ref,
    first_value_ref,
    second_value_ref,
    circulant_ref,
    orbital_ref,
    points_ref,
    coulomb_ref,
    left_wave_ref,
    right_wave_ref,
    own_blocks,
    plane_stage,
    row_stage,
    gz_value_stage,
    gy_value_stage,
    own_values,
    first_value_sems,
    second_value_sems,
    gy_first_sems,
    gz_first_sems,
    gz_second_sems,
    gy_second_sems,
    local_sems,
):
    gz, gy = lax.axis_index("gz"), lax.axis_index("gy")
    gy_peers = [lax.rem(gy + d, gy_count) for d in range(1, gy_count)]
    gz_peers = [lax.rem(gz + d, gz_count) for d in range(1, gz_count)]
    barrier = pltpu.get_barrier_semaphore()
    for device in [(gz, peer) for peer in gy_peers] + [(peer, gy) for peer in gz_peers]:
        pl.semaphore_signal(
            barrier, inc=1, device_id=device, device_id_type=pl.DeviceIdType.MESH
        )
    load = [
        pltpu.make_async_copy(points_hbm, points_ref, local_sems.at[9]),
        pltpu.make_async_copy(orbital_hbm, orbital_ref, local_sems.at[0]),
    ]
    for copy in load:
        copy.start()
    load_waves = [
        pltpu.make_async_copy(coulomb_hbm, coulomb_ref, local_sems.at[10]),
        pltpu.make_async_copy(left_wave_hbm, left_wave_ref, local_sems.at[7]),
        pltpu.make_async_copy(right_wave_hbm, right_wave_ref, local_sems.at[8]),
    ]
    for copy in load_waves:
        copy.start()
    for copy in load:
        copy.wait()
    pick_points(orbital_ref, points_ref, own_values)
    bands, planes, columns = orbital_ref.shape
    half = bands // 2
    cols = own_blocks.shape[3]
    width = 256
    for band in range(bands):
        for first in range(0, columns, width):
            turned = orbital_ref[band, :, first : first + width].astype(F32).T
            at = first // cols
            own_blocks[band, at // gz_count : (at + width // cols) // gz_count] = (
                turned.reshape(width // cols // gz_count, gz_count, cols, planes).astype(BF16)
            )
    pl.semaphore_wait(barrier, gy_count + gz_count - 2)

    own = [
        pltpu.make_async_copy(own_values.at[0], gz_value_stage.at[gz], local_sems.at[1]),
        pltpu.make_async_copy(own_values.at[1], gy_value_stage.at[gy], local_sems.at[11]),
        pltpu.make_async_copy(
            own_blocks.at[pl.ds(0, half), gy], plane_stage.at[gy], local_sems.at[2]
        ),
        pltpu.make_async_copy(
            own_blocks.at[pl.ds(half, half), :, gz], row_stage.at[gz], local_sems.at[3]
        ),
    ]
    for copy in own:
        copy.start()
    values = [
        send(
            own_values.at[0],
            gz_value_stage.at[gz],
            first_value_sems.at[0, 0, i],
            first_value_sems.at[0, 1, i],
            (peer, gy),
        )
        for i, peer in enumerate(gz_peers)
    ] + [
        send(
            own_values.at[1],
            gy_value_stage.at[gy],
            first_value_sems.at[1, 0, i],
            first_value_sems.at[1, 1, i],
            (gz, peer),
        )
        for i, peer in enumerate(gy_peers)
    ]
    lower = [
        send(
            own_blocks.at[pl.ds(0, half), peer],
            plane_stage.at[gy],
            gy_first_sems.at[0, i],
            gy_first_sems.at[1, i],
            (gz, peer),
        )
        for i, peer in enumerate(gy_peers)
    ]
    upper = [
        send(
            own_blocks.at[pl.ds(half, half), :, peer],
            row_stage.at[gz],
            gz_first_sems.at[0, i],
            gz_first_sems.at[1, i],
            (peer, gy),
        )
        for i, peer in enumerate(gz_peers)
    ]
    for copy in own:
        copy.wait()
    for copy in values:
        copy.wait_recv()
    values_on = [
        send(
            gz_value_stage,
            first_value_ref.at[gy],
            second_value_sems.at[0, 0, i],
            second_value_sems.at[0, 1, i],
            (gz, peer),
        )
        for i, peer in enumerate(gy_peers)
    ] + [
        send(
            gy_value_stage,
            second_value_ref.at[gz],
            second_value_sems.at[1, 0, i],
            second_value_sems.at[1, 1, i],
            (peer, gy),
        )
        for i, peer in enumerate(gz_peers)
    ]
    for copy in lower:
        copy.wait_recv()
    lower_on = [
        send(
            plane_stage.at[:, :, peer],
            pencil_ref.at[0, gz],
            gz_second_sems.at[0, i],
            gz_second_sems.at[1, i],
            (peer, gy),
        )
        for i, peer in enumerate(gz_peers)
    ]
    for copy in upper:
        copy.wait_recv()
    upper_on = [
        send(
            row_stage.at[:, :, peer],
            pencil_ref.at[1, :, gy],
            gy_second_sems.at[0, i],
            gy_second_sems.at[1, i],
            (gz, peer),
        )
        for i, peer in enumerate(gy_peers)
    ]
    own_on = [
        pltpu.make_async_copy(gz_value_stage, first_value_ref.at[gy], local_sems.at[4]),
        pltpu.make_async_copy(gy_value_stage, second_value_ref.at[gz], local_sems.at[12]),
        pltpu.make_async_copy(plane_stage.at[:, :, gz], pencil_ref.at[0, gz], local_sems.at[5]),
        pltpu.make_async_copy(row_stage.at[:, :, gy], pencil_ref.at[1, :, gy], local_sems.at[6]),
    ]
    for copy in own_on:
        copy.start()
    for copy in load_waves:
        copy.wait()
    all_cols = coulomb_ref.shape[1]
    own_cols = lax.broadcasted_iota(jnp.int32, (cols, all_cols), 0) + gz * cols
    pick = (lax.broadcasted_iota(jnp.int32, (cols, all_cols), 1) == own_cols).astype(F32)
    weights = lax.dot_general(
        pick,
        coulomb_ref[...],
        (((1,), (1,)), ((), ())),
        precision=FULL,
        preferred_element_type=F32,
    ) * (1.0 / planes)
    weights = jnp.concatenate([weights, weights], axis=1)
    for c in range(cols):
        high, low = split_parts(
            jnp.dot(
                left_wave_ref[...] * weights[c : c + 1, :],
                right_wave_ref[...],
                precision=FULL,
                preferred_element_type=F32,
            ),
            2,
        )
        circulant_ref[c] = jnp.concatenate([high, high, low], axis=1)
    for copy in own_on:
        copy.wait()
    for copy in values + lower + upper:
        copy.wait_send()
    for copy in values_on + lower_on + upper_on:
        copy.wait()


def exchange(orbitals, points, coulomb, gz_count, gy_count, early):
    bands, planes, columns = orbitals.shape
    count = points.shape[0]
    cols = coulomb.shape[1] // gz_count
    half = bands // 2
    slab = planes // gz_count
    z = np.arange(planes)
    order = z.reshape(gz_count, slab)
    order = np.concatenate([order[:, :early].ravel(), order[:, early:].ravel()])
    angles = 2.0 * np.pi / planes * (z[:, None] * z % planes)
    waves = np.concatenate([np.cos(angles), np.sin(angles)], axis=1)
    vmem, hbm = (pl.BlockSpec(memory_space=space) for space in (pltpu.VMEM, pltpu.HBM))
    dma = pltpu.SemaphoreType.DMA
    return pl.pallas_call(
        functools.partial(exchange_kernel, gz_count, gy_count),
        in_specs=[hbm, hbm, hbm, hbm, hbm],
        out_specs=(vmem, vmem, vmem, vmem),
        out_shape=(
            jax.ShapeDtypeStruct((2, gz_count, gy_count, half, cols, planes), BF16),
            jax.ShapeDtypeStruct((gy_count, gz_count, bands, count // 2), BF16),
            jax.ShapeDtypeStruct((gz_count, gy_count, bands, count // 2), BF16),
            jax.ShapeDtypeStruct((cols, planes, 3 * planes), BF16),
        ),
        scratch_shapes=[
            pltpu.VMEM((bands, planes, columns), BF16),
            pltpu.VMEM((1, count), jnp.int32),
            pltpu.VMEM(coulomb.shape, F32),
            pltpu.VMEM((planes, 2 * planes), F32),
            pltpu.VMEM((2 * planes, planes), F32),
            pltpu.VMEM((bands, gy_count, gz_count, cols, planes), BF16),
            pltpu.VMEM((gy_count, half, gz_count, cols, planes), BF16),
            pltpu.VMEM((gz_count, half, gy_count, cols, planes), BF16),
            pltpu.VMEM((gz_count, bands, count // 2), BF16),
            pltpu.VMEM((gy_count, bands, count // 2), BF16),
            pltpu.VMEM((2, bands, count // 2), BF16),
            dma((2, 2, gz_count - 1)),
            dma((2, 2, gz_count - 1)),
            dma((2, gy_count - 1)),
            dma((2, gz_count - 1)),
            dma((2, gz_count - 1)),
            dma((2, gy_count - 1)),
            dma((13,)),
        ],
        compiler_params=pltpu.CompilerParams(
            collective_id=0, has_side_effects=True, vmem_limit_bytes=28 << 20
        ),
    )(
        in_hbm(orbitals),
        in_hbm(points.reshape(1, count)),
        in_hbm(coulomb),
        in_hbm(jnp.asarray(waves[order], F32)),
        in_hbm(jnp.asarray(waves.T, F32)),
    )


def split_parts(values, count):
    parts = []
    for _ in range(count):
        part = values.astype(BF16)
        parts.append(part)
        values = values - part.astype(F32)
    return parts


def full_dot(left, right):
    return jnp.dot(left_stack(left), right_stack(right), preferred_element_type=F32)


def left_stack(left):
    high, middle, low = split_parts(left, 3)
    return jnp.concatenate([high, high, middle, high, low, middle], axis=1)


def right_stack(right):
    high, middle, low = split_parts(right, 3)
    return jnp.concatenate([high, middle, high, low, high, middle], axis=0)


def tree_sum(terms):
    while len(terms) > 1:
        terms = [sum(terms[i : i + 2][1:], terms[i]) for i in range(0, len(terms), 2)]
    return terms[0]


def eliminate_rows(rows, first, lane, sub):
    shape = rows.shape
    columns = [jnp.broadcast_to(rows[:, first + j : first + j + 1], shape) for j in range(8)]
    cell = {
        (i, j): jnp.broadcast_to(columns[j][i : i + 1, :], shape)
        for j in range(8)
        for i in range(j + 1)
    }
    for k in range(8):
        recip = 1.0 / cell[k, k]
        side = {i: cell[min(i, k), max(i, k)] for i in range(8) if i != k}
        scaled = {i: side[i] * recip for i in side}
        swept = {}
        for i, j in cell:
            if i == k and j == k:
                swept[i, j] = -recip
            elif i == k or j == k:
                swept[i, j] = scaled[j if i == k else i]
            else:
                swept[i, j] = cell[i, j] - side[i] * scaled[j]
        cell = swept
    inside = (lane >= first) & (lane < first + 8)
    source = [
        jnp.where(
            inside,
            jnp.where(lane == first + j, -1.0, 0.0),
            -jnp.broadcast_to(rows[j : j + 1, :], shape),
        )
        for j in range(8)
    ]
    results = [
        tree_sum([cell[min(i, j), max(i, j)] * source[j] for j in range(8)]) for i in range(8)
    ]
    panel = results[0]
    for i in range(1, 8):
        panel = jnp.where(sub == i, results[i], panel)
    return results, panel, inside


def small_inverse(block):
    size = block.shape[0]
    tiles = [block[i : i + 8, :] for i in range(0, size, 8)]
    lane = lax.broadcasted_iota(jnp.int32, (8, size), 1)
    sub = lax.broadcasted_iota(jnp.int32, (8, size), 0)
    for at in range(len(tiles)):
        first = at * 8
        following = [at + 1] if at + 1 < len(tiles) else []
        rest = [i for i in range(len(tiles)) if i != at and i not in following]
        stack = jnp.concatenate([tiles[i] for i in rest], axis=0)
        wide_lane = lax.broadcasted_iota(jnp.int32, stack.shape, 1)
        kept = jnp.where((wide_lane >= first) & (wide_lane < first + 8), 0.0, stack)
        wide = left_stack(stack[:, first : first + 8])
        results, panel, inside = eliminate_rows(tiles[at], first, lane, sub)
        for other in following:
            terms = [
                jnp.broadcast_to(tiles[other][:, first + j : first + j + 1], (8, size)) * results[j]
                for j in range(8)
            ]
            tiles[other] = jnp.where(inside, 0.0, tiles[other]) - tree_sum(terms)
        stack = kept - jnp.dot(wide, right_stack(panel), preferred_element_type=F32)
        for place, i in enumerate(rest):
            tiles[i] = stack[place * 8 : place * 8 + 8, :]
        tiles[at] = panel
    return jnp.concatenate(tiles, axis=0)


def inverse_kernel(
    width, point_ref, late_ref, fitted_ref, high_out, low_out, work, high_ref, low_ref
):
    size = work.shape[0]
    block = 256

    @pl.when(pl.program_id(0) == 0)
    def _():
        for first in range(0, size, block):
            base = lax.dot_general(
                point_ref[:, first : first + block],
                point_ref[...],
                (((0,), (0,)), ((), ())),
                preferred_element_type=F32,
            )
            work[first : first + block, :] = base * base

        def eliminate(k, carry):
            at = pl.ds(pl.multiple_of(k * width, width), width)
            pivot = small_inverse(work[at, at])
            work[at, :] = full_dot(pivot, work[at, :])
            work[at, at] = pivot
            panel = work[at, :]
            stacked = right_stack(panel)
            wide = left_stack(work[:, at])
            work[:, at] = jnp.zeros((size, width), F32)
            for first in range(0, size, block):
                columns = slice(first, first + block)
                change = jnp.dot(wide, stacked[:, columns], preferred_element_type=F32)
                work[:, columns] = work[:, columns] - change
            work[at, :] = panel
            return carry

        lax.fori_loop(0, size // width, eliminate, 0)
        for first in range(0, size, block):
            rows = slice(first, first + block)
            high, low = split_parts(work[rows, :], 2)
            high_ref[rows, :] = high
            low_ref[rows, :] = low

    @pl.when(pl.program_id(0) > 0)
    def _():
        rows = pl.ds(pl.multiple_of((pl.program_id(0) - 1) * block, block), block)
        high_out[...] = high_ref[rows, :]
        low_out[...] = low_ref[rows, :]
        fitted_ref[...] = fit_rows(late_ref[...], high_ref, low_ref)


def inverse_and_late_fit(at_points, late):
    size = at_points.shape[1]
    block = 256
    steps = late.shape[0] // block
    assert steps == size // block
    rows = pl.BlockSpec((block, size), lambda i: (jnp.maximum(i - 1, 0), 0))
    return pl.pallas_call(
        functools.partial(inverse_kernel, 128),
        grid=(1 + steps,),
        in_specs=[pl.BlockSpec(memory_space=pltpu.VMEM), rows],
        out_specs=(rows, rows, rows),
        out_shape=(
            pltpu.HBM(late.shape, BF16),
            pltpu.HBM((size, size), BF16),
            pltpu.HBM((size, size), BF16),
        ),
        scratch_shapes=[
            pltpu.VMEM((size, size), F32),
            pltpu.VMEM((size, size), BF16),
            pltpu.VMEM((size, size), BF16),
        ],
        compiler_params=pltpu.CompilerParams(vmem_limit_bytes=36 << 20),
        cost_estimate=pl.CostEstimate(
            flops=60 * size**3, bytes_accessed=8 * size * size, transcendentals=0
        ),
    )(at_points, in_hbm(late))


def filter_kernel(pencil_ref, point_ref, circulant_ref, early_ref, late_ref):
    early = early_ref.shape[0]
    col_count = pencil_ref.shape[0]

    def products(c):
        sums = lax.dot_general(
            pencil_ref[c], point_ref[...], (((0,), (0,)), ((), ())), preferred_element_type=F32
        )
        return split_parts(sums * sums, 2)

    following = products(0)
    for c in range(col_count):
        high, low = following
        if c + 1 < col_count:
            following = products(c + 1)
        smooth = jnp.dot(
            circulant_ref[c],
            jnp.concatenate([high, low, high], axis=0),
            preferred_element_type=F32,
        )
        early_ref[:, c, :] = smooth[:early]
        late_ref[:, c, :] = smooth[early:]


def filtered_products(pencils, at_points, circulant, early):
    col_count, bands, planes = pencils.shape
    count = at_points.shape[1]
    late = planes - early
    chunk = 256
    return pl.pallas_call(
        filter_kernel,
        grid=(count // chunk,),
        in_specs=[
            pl.BlockSpec(memory_space=pltpu.VMEM),
            pl.BlockSpec((bands, chunk), lambda i: (0, i)),
            pl.BlockSpec(memory_space=pltpu.VMEM),
        ],
        out_specs=[
            pl.BlockSpec((early, col_count, chunk), lambda i: (0, 0, i)),
            pl.BlockSpec((late, col_count, chunk), lambda i: (0, 0, i)),
        ],
        out_shape=[
            pltpu.HBM((early, col_count, count), F32),
            pltpu.HBM((late, col_count, count), F32),
        ],
        compiler_params=pltpu.CompilerParams(vmem_limit_bytes=28 << 20),
        cost_estimate=pl.CostEstimate(
            flops=8 * col_count * planes * bands * count, bytes_accessed=10 << 20, transcendentals=0
        ),
    )(pencils, at_points, circulant)


def fit_rows(rows, high_ref, low_ref):
    high, low = split_parts(rows, 2)
    dot = functools.partial(jnp.dot, preferred_element_type=F32)
    return (
        dot(high, high_ref[...]) + (dot(low, high_ref[...]) + dot(high, low_ref[...]))
    ).astype(BF16)


def early_fit_kernel(rows_ref, high_ref, low_ref, out_ref):
    planes, cols, count = out_ref.shape
    rows = jnp.concatenate(
        [rows_ref[:, z].reshape(cols, count) for z in range(planes)], axis=0
    )
    out_ref[...] = fit_rows(rows, high_ref, low_ref).reshape(planes, cols, count)


def early_fit(slab, high, low, total_planes):
    sources, early, col_count, count = slab.shape
    block = 2
    whole = pl.BlockSpec((count, count), lambda i: (0, 0))
    return pl.pallas_call(
        early_fit_kernel,
        grid=(early // block,),
        in_specs=[
            pl.BlockSpec((sources, block, col_count, count), lambda i: (0, i, 0, 0)),
            whole,
            whole,
        ],
        out_specs=pl.BlockSpec((block, sources * col_count, count), lambda i: (i, 0, 0)),
        out_shape=jax.ShapeDtypeStruct((total_planes, sources * col_count, count), BF16),
        compiler_params=pltpu.CompilerParams(vmem_limit_bytes=24 << 20),
        cost_estimate=pl.CostEstimate(
            flops=6 * slab.size * count, bytes_accessed=10 << 20, transcendentals=0
        ),
    )(slab, high, low)


def place_late_kernel(late_ref, _, out_ref):
    planes, cols, count = out_ref.shape
    first = pl.program_id(0) * planes
    for z in range(planes):
        out_ref[z] = late_ref[:, first + z].astype(F32).reshape(cols, count).astype(BF16)


def place_late(late, fitted):
    sources, planes, col_count, count = late.shape
    block = 2
    first = (fitted.shape[0] - planes) // block
    return pl.pallas_call(
        place_late_kernel,
        grid=(planes // block,),
        in_specs=[
            pl.BlockSpec(memory_space=pltpu.VMEM),
            pl.BlockSpec(memory_space=pl.ANY),
        ],
        out_specs=pl.BlockSpec((block, sources * col_count, count), lambda i: (first + i, 0, 0)),
        out_shape=jax.ShapeDtypeStruct(fitted.shape, BF16),
        input_output_aliases={1: 0},
        compiler_params=pltpu.CompilerParams(vmem_limit_bytes=12 << 20),
        cost_estimate=pl.CostEstimate(flops=0, bytes_accessed=2 * late.size * 2, transcendentals=0),
    )(late, fitted)


def per_device(orbitals, points, coulomb):
    gz_count, gy_count = lax.axis_size("gz"), lax.axis_size("gy")
    planes, columns = coulomb.shape
    col_pencil = columns // gz_count
    count = points.shape[0]
    slab_planes = planes // gz_count
    early = EARLY
    pencils, first_values, second_values, circulant = exchange(
        orbitals, points, coulomb, gz_count, gy_count, early
    )
    split = (2, orbitals.shape[0] // 2, count // 2)
    at_points = jnp.concatenate(
        [
            jnp.transpose(first_values.reshape(gy_count, gz_count, *split), (2, 1, 0, 3, 4)),
            jnp.transpose(second_values.reshape(gz_count, gy_count, *split), (2, 0, 1, 3, 4)),
        ],
        axis=4,
    ).reshape(-1, count)
    pencils = jnp.transpose(pencils.reshape(-1, col_pencil, planes), (1, 0, 2))
    first, second = filtered_products(pencils, at_points, circulant, gz_count * early)
    swap = functools.partial(
        lax.all_to_all, axis_name="gz", split_axis=0, concat_axis=0, tiled=True
    )
    slab = swap(first.reshape(gz_count, early, col_pencil, count))
    late, high, low = inverse_and_late_fit(at_points, second.reshape(-1, count))
    late = swap(late.reshape(gz_count, slab_planes - early, col_pencil, count))
    return place_late(late, early_fit(slab, high, low, slab_planes))


def solution(mesh):
    return jax.shard_map(
        per_device,
        mesh=mesh,
        in_specs=(P(("gz", "gy"), None, None), P(), P(None, "gy")),
        out_specs=P("gz", "gy", None),
        check_vma=False,
    )
```

```python
import functools

import jax
import jax.numpy as jnp
import numpy as np
from jax import lax
from jax.experimental import pallas as pl
from jax.experimental.pallas import tpu as pltpu
from jax.sharding import PartitionSpec as P

FULL = lax.Precision.HIGHEST
F32 = jnp.float32
BF16 = jnp.bfloat16
EARLY = 8


def in_hbm(array):
    return pltpu.with_memory_space_constraint(array, pltpu.HBM)


def pick_points(orbital_ref, points_ref, out_ref):
    bands, planes, columns = orbital_ref.shape
    points = points_ref[...]
    point_planes = points // columns
    point_columns = points - point_planes * columns
    count = points.shape[1]
    column_pick = (
        lax.broadcasted_iota(jnp.int32, (columns, count), 0) == point_columns
    ).astype(BF16)
    plane_pick = lax.broadcasted_iota(jnp.int32, (planes, count), 0) == point_planes
    for band in range(bands):
        picked = jnp.dot(orbital_ref[band], column_pick, preferred_element_type=F32)
        values = jnp.sum(jnp.where(plane_pick, picked, 0.0), axis=0, keepdims=True).astype(BF16)
        out_ref[0, band : band + 1, :] = values[:, : count // 2]
        out_ref[1, band : band + 1, :] = values[:, count // 2 :]


def send(source, target, send_sem, recv_sem, device):
    copy = pltpu.make_async_remote_copy(
        src_ref=source,
        dst_ref=target,
        send_sem=send_sem,
        recv_sem=recv_sem,
        device_id=device,
        device_id_type=pl.DeviceIdType.MESH,
    )
    copy.start()
    return copy


def exchange_kernel(
    gz_count,
    gy_count,
    orbital_hbm,
    points_hbm,
    coulomb_hbm,
    left_wave_hbm,
    right_wave_hbm,
    pencil_ref,
    first_value_ref,
    second_value_ref,
    circulant_ref,
    orbital_ref,
    points_ref,
    coulomb_ref,
    left_wave_ref,
    right_wave_ref,
    own_blocks,
    plane_stage,
    row_stage,
    gz_value_stage,
    gy_value_stage,
    own_values,
    first_value_sems,
    second_value_sems,
    gy_first_sems,
    gz_first_sems,
    gz_second_sems,
    gy_second_sems,
    local_sems,
):
    gz, gy = lax.axis_index("gz"), lax.axis_index("gy")
    gy_peers = [lax.rem(gy + d, gy_count) for d in range(1, gy_count)]
    gz_peers = [lax.rem(gz + d, gz_count) for d in range(1, gz_count)]
    barrier = pltpu.get_barrier_semaphore()
    for device in [(gz, peer) for peer in gy_peers] + [(peer, gy) for peer in gz_peers]:
        pl.semaphore_signal(
            barrier, inc=1, device_id=device, device_id_type=pl.DeviceIdType.MESH
        )
    load = [
        pltpu.make_async_copy(points_hbm, points_ref, local_sems.at[9]),
        pltpu.make_async_copy(orbital_hbm, orbital_ref, local_sems.at[0]),
    ]
    for copy in load:
        copy.start()
    load_waves = [
        pltpu.make_async_copy(coulomb_hbm, coulomb_ref, local_sems.at[10]),
        pltpu.make_async_copy(left_wave_hbm, left_wave_ref, local_sems.at[7]),
        pltpu.make_async_copy(right_wave_hbm, right_wave_ref, local_sems.at[8]),
    ]
    for copy in load_waves:
        copy.start()
    for copy in load:
        copy.wait()
    pick_points(orbital_ref, points_ref, own_values)
    bands, planes, columns = orbital_ref.shape
    half = bands // 2
    cols = own_blocks.shape[3]
    width = 256
    for band in range(bands):
        for first in range(0, columns, width):
            turned = orbital_ref[band, :, first : first + width].astype(F32).T
            at = first // cols
            own_blocks[band, at // gz_count : (at + width // cols) // gz_count] = (
                turned.reshape(width // cols // gz_count, gz_count, cols, planes).astype(BF16)
            )
    pl.semaphore_wait(barrier, gy_count + gz_count - 2)

    own = [
        pltpu.make_async_copy(own_values.at[0], gz_value_stage.at[gz], local_sems.at[1]),
        pltpu.make_async_copy(own_values.at[1], gy_value_stage.at[gy], local_sems.at[11]),
        pltpu.make_async_copy(
            own_blocks.at[pl.ds(0, half), gy], plane_stage.at[gy], local_sems.at[2]
        ),
        pltpu.make_async_copy(
            own_blocks.at[pl.ds(half, half), :, gz], row_stage.at[gz], local_sems.at[3]
        ),
    ]
    for copy in own:
        copy.start()
    values = [
        send(
            own_values.at[0],
            gz_value_stage.at[gz],
            first_value_sems.at[0, 0, i],
            first_value_sems.at[0, 1, i],
            (peer, gy),
        )
        for i, peer in enumerate(gz_peers)
    ] + [
        send(
            own_values.at[1],
            gy_value_stage.at[gy],
            first_value_sems.at[1, 0, i],
            first_value_sems.at[1, 1, i],
            (gz, peer),
        )
        for i, peer in enumerate(gy_peers)
    ]
    lower = [
        send(
            own_blocks.at[pl.ds(0, half), peer],
            plane_stage.at[gy],
            gy_first_sems.at[0, i],
            gy_first_sems.at[1, i],
            (gz, peer),
        )
        for i, peer in enumerate(gy_peers)
    ]
    upper = [
        send(
            own_blocks.at[pl.ds(half, half), :, peer],
            row_stage.at[gz],
            gz_first_sems.at[0, i],
            gz_first_sems.at[1, i],
            (peer, gy),
        )
        for i, peer in enumerate(gz_peers)
    ]
    for copy in own:
        copy.wait()
    for copy in values:
        copy.wait_recv()
    values_on = [
        send(
            gz_value_stage,
            first_value_ref.at[gy],
            second_value_sems.at[0, 0, i],
            second_value_sems.at[0, 1, i],
            (gz, peer),
        )
        for i, peer in enumerate(gy_peers)
    ] + [
        send(
            gy_value_stage,
            second_value_ref.at[gz],
            second_value_sems.at[1, 0, i],
            second_value_sems.at[1, 1, i],
            (peer, gy),
        )
        for i, peer in enumerate(gz_peers)
    ]
    for copy in lower:
        copy.wait_recv()
    lower_on = [
        send(
            plane_stage.at[:, :, peer],
            pencil_ref.at[0, gz],
            gz_second_sems.at[0, i],
            gz_second_sems.at[1, i],
            (peer, gy),
        )
        for i, peer in enumerate(gz_peers)
    ]
    for copy in upper:
        copy.wait_recv()
    upper_on = [
        send(
            row_stage.at[:, :, peer],
            pencil_ref.at[1, :, gy],
            gy_second_sems.at[0, i],
            gy_second_sems.at[1, i],
            (gz, peer),
        )
        for i, peer in enumerate(gy_peers)
    ]
    own_on = [
        pltpu.make_async_copy(gz_value_stage, first_value_ref.at[gy], local_sems.at[4]),
        pltpu.make_async_copy(gy_value_stage, second_value_ref.at[gz], local_sems.at[12]),
        pltpu.make_async_copy(plane_stage.at[:, :, gz], pencil_ref.at[0, gz], local_sems.at[5]),
        pltpu.make_async_copy(row_stage.at[:, :, gy], pencil_ref.at[1, :, gy], local_sems.at[6]),
    ]
    for copy in own_on:
        copy.start()
    for copy in load_waves:
        copy.wait()
    all_cols = coulomb_ref.shape[1]
    own_cols = lax.broadcasted_iota(jnp.int32, (cols, all_cols), 0) + gz * cols
    pick = (lax.broadcasted_iota(jnp.int32, (cols, all_cols), 1) == own_cols).astype(F32)
    weights = lax.dot_general(
        pick,
        coulomb_ref[...],
        (((1,), (1,)), ((), ())),
        precision=FULL,
        preferred_element_type=F32,
    ) * (1.0 / planes)
    weights = jnp.concatenate([weights, weights], axis=1)
    for c in range(cols):
        high, low = split_parts(
            jnp.dot(
                left_wave_ref[...] * weights[c : c + 1, :],
                right_wave_ref[...],
                precision=FULL,
                preferred_element_type=F32,
            ),
            2,
        )
        circulant_ref[c] = jnp.concatenate([high, high, low], axis=1)
    for copy in own_on:
        copy.wait()
    for copy in values + lower + upper:
        copy.wait_send()
    for copy in values_on + lower_on + upper_on:
        copy.wait()


def exchange(orbitals, points, coulomb, gz_count, gy_count, early):
    bands, planes, columns = orbitals.shape
    count = points.shape[0]
    cols = coulomb.shape[1] // gz_count
    half = bands // 2
    slab = planes // gz_count
    z = np.arange(planes)
    order = z.reshape(gz_count, slab)
    order = np.concatenate([order[:, :early].ravel(), order[:, early:].ravel()])
    angles = 2.0 * np.pi / planes * (z[:, None] * z % planes)
    waves = np.concatenate([np.cos(angles), np.sin(angles)], axis=1)
    vmem, hbm = (pl.BlockSpec(memory_space=space) for space in (pltpu.VMEM, pltpu.HBM))
    dma = pltpu.SemaphoreType.DMA
    return pl.pallas_call(
        functools.partial(exchange_kernel, gz_count, gy_count),
        in_specs=[hbm, hbm, hbm, hbm, hbm],
        out_specs=(vmem, vmem, vmem, vmem),
        out_shape=(
            jax.ShapeDtypeStruct((2, gz_count, gy_count, half, cols, planes), BF16),
            jax.ShapeDtypeStruct((gy_count, gz_count, bands, count // 2), BF16),
            jax.ShapeDtypeStruct((gz_count, gy_count, bands, count // 2), BF16),
            jax.ShapeDtypeStruct((cols, planes, 3 * planes), BF16),
        ),
        scratch_shapes=[
            pltpu.VMEM((bands, planes, columns), BF16),
            pltpu.VMEM((1, count), jnp.int32),
            pltpu.VMEM(coulomb.shape, F32),
            pltpu.VMEM((planes, 2 * planes), F32),
            pltpu.VMEM((2 * planes, planes), F32),
            pltpu.VMEM((bands, gy_count, gz_count, cols, planes), BF16),
            pltpu.VMEM((gy_count, half, gz_count, cols, planes), BF16),
            pltpu.VMEM((gz_count, half, gy_count, cols, planes), BF16),
            pltpu.VMEM((gz_count, bands, count // 2), BF16),
            pltpu.VMEM((gy_count, bands, count // 2), BF16),
            pltpu.VMEM((2, bands, count // 2), BF16),
            dma((2, 2, gz_count - 1)),
            dma((2, 2, gz_count - 1)),
            dma((2, gy_count - 1)),
            dma((2, gz_count - 1)),
            dma((2, gz_count - 1)),
            dma((2, gy_count - 1)),
            dma((13,)),
        ],
        compiler_params=pltpu.CompilerParams(
            collective_id=0, has_side_effects=True, vmem_limit_bytes=28 << 20
        ),
    )(
        in_hbm(orbitals),
        in_hbm(points.reshape(1, count)),
        in_hbm(coulomb),
        in_hbm(jnp.asarray(waves[order], F32)),
        in_hbm(jnp.asarray(waves.T, F32)),
    )


def split_parts(values, count):
    parts = []
    for _ in range(count):
        part = values.astype(BF16)
        parts.append(part)
        values = values - part.astype(F32)
    return parts


def full_dot(left, right):
    return jnp.dot(left_stack(left), right_stack(right), preferred_element_type=F32)


def left_stack(left):
    high, middle, low = split_parts(left, 3)
    return jnp.concatenate([high, high, middle, high, low, middle], axis=1)


def right_stack(right):
    high, middle, low = split_parts(right, 3)
    return jnp.concatenate([high, middle, high, low, high, middle], axis=0)


def tree_sum(terms):
    while len(terms) > 1:
        terms = [sum(terms[i : i + 2][1:], terms[i]) for i in range(0, len(terms), 2)]
    return terms[0]


def eliminate_rows(rows, first, lane, sub):
    shape = rows.shape
    columns = [jnp.broadcast_to(rows[:, first + j : first + j + 1], shape) for j in range(8)]
    cell = {
        (i, j): jnp.broadcast_to(columns[j][i : i + 1, :], shape)
        for j in range(8)
        for i in range(j + 1)
    }
    for k in range(8):
        recip = 1.0 / cell[k, k]
        side = {i: cell[min(i, k), max(i, k)] for i in range(8) if i != k}
        scaled = {i: side[i] * recip for i in side}
        swept = {}
        for i, j in cell:
            if i == k and j == k:
                swept[i, j] = -recip
            elif i == k or j == k:
                swept[i, j] = scaled[j if i == k else i]
            else:
                swept[i, j] = cell[i, j] - side[i] * scaled[j]
        cell = swept
    inside = (lane >= first) & (lane < first + 8)
    source = [
        jnp.where(
            inside,
            jnp.where(lane == first + j, -1.0, 0.0),
            -jnp.broadcast_to(rows[j : j + 1, :], shape),
        )
        for j in range(8)
    ]
    results = [
        tree_sum([cell[min(i, j), max(i, j)] * source[j] for j in range(8)]) for i in range(8)
    ]
    panel = results[0]
    for i in range(1, 8):
        panel = jnp.where(sub == i, results[i], panel)
    return results, panel, inside


def small_inverse(block):
    size = block.shape[0]
    tiles = [block[i : i + 8, :] for i in range(0, size, 8)]
    lane = lax.broadcasted_iota(jnp.int32, (8, size), 1)
    sub = lax.broadcasted_iota(jnp.int32, (8, size), 0)
    for at in range(len(tiles)):
        first = at * 8
        following = [i for i in (at + 1, at + 2) if i < len(tiles)]
        rest = [i for i in range(len(tiles)) if i != at and i not in following]
        stack = jnp.concatenate([tiles[i] for i in rest], axis=0)
        wide_lane = lax.broadcasted_iota(jnp.int32, stack.shape, 1)
        kept = jnp.where((wide_lane >= first) & (wide_lane < first + 8), 0.0, stack)
        wide = left_stack(stack[:, first : first + 8])
        results, panel, inside = eliminate_rows(tiles[at], first, lane, sub)
        for other in following:
            terms = [
                jnp.broadcast_to(tiles[other][:, first + j : first + j + 1], (8, size)) * results[j]
                for j in range(8)
            ]
            tiles[other] = jnp.where(inside, 0.0, tiles[other]) - tree_sum(terms)
        stack = kept - jnp.dot(wide, right_stack(panel), preferred_element_type=F32)
        for place, i in enumerate(rest):
            tiles[i] = stack[place * 8 : place * 8 + 8, :]
        tiles[at] = panel
    return jnp.concatenate(tiles, axis=0)


def inverse_kernel(
    width, point_ref, late_ref, fitted_ref, high_out, low_out, work, high_ref, low_ref
):
    size = work.shape[0]
    block = 256

    @pl.when(pl.program_id(0) == 0)
    def _():
        for first in range(0, size, block):
            base = lax.dot_general(
                point_ref[:, first : first + block],
                point_ref[...],
                (((0,), (0,)), ((), ())),
                preferred_element_type=F32,
            )
            work[first : first + block, :] = base * base

        def eliminate(k, carry):
            at = pl.ds(pl.multiple_of(k * width, width), width)
            pivot = small_inverse(work[at, at])
            work[at, :] = full_dot(pivot, work[at, :])
            work[at, at] = pivot
            panel = work[at, :]
            stacked = right_stack(panel)
            wide = left_stack(work[:, at])
            work[:, at] = jnp.zeros((size, width), F32)
            for first in range(0, size, block):
                columns = slice(first, first + block)
                change = jnp.dot(wide, stacked[:, columns], preferred_element_type=F32)
                work[:, columns] = work[:, columns] - change
            work[at, :] = panel
            return carry

        lax.fori_loop(0, size // width, eliminate, 0)
        for first in range(0, size, block):
            rows = slice(first, first + block)
            high, low = split_parts(work[rows, :], 2)
            high_ref[rows, :] = high
            low_ref[rows, :] = low

    @pl.when(pl.program_id(0) > 0)
    def _():
        rows = pl.ds(pl.multiple_of((pl.program_id(0) - 1) * block, block), block)
        high_out[...] = high_ref[rows, :]
        low_out[...] = low_ref[rows, :]
        fitted_ref[...] = fit_rows(late_ref[...], high_ref, low_ref)


def inverse_and_late_fit(at_points, late):
    size = at_points.shape[1]
    block = 256
    steps = late.shape[0] // block
    assert steps == size // block
    rows = pl.BlockSpec((block, size), lambda i: (jnp.maximum(i - 1, 0), 0))
    return pl.pallas_call(
        functools.partial(inverse_kernel, 128),
        grid=(1 + steps,),
        in_specs=[pl.BlockSpec(memory_space=pltpu.VMEM), rows],
        out_specs=(rows, rows, rows),
        out_shape=(
            pltpu.HBM(late.shape, BF16),
            pltpu.HBM((size, size), BF16),
            pltpu.HBM((size, size), BF16),
        ),
        scratch_shapes=[
            pltpu.VMEM((size, size), F32),
            pltpu.VMEM((size, size), BF16),
            pltpu.VMEM((size, size), BF16),
        ],
        compiler_params=pltpu.CompilerParams(vmem_limit_bytes=36 << 20),
        cost_estimate=pl.CostEstimate(
            flops=60 * size**3, bytes_accessed=8 * size * size, transcendentals=0
        ),
    )(at_points, in_hbm(late))


def filter_kernel(pencil_ref, point_ref, circulant_ref, early_ref, late_ref):
    early = early_ref.shape[0]
    col_count = pencil_ref.shape[0]

    def products(c):
        sums = lax.dot_general(
            pencil_ref[c], point_ref[...], (((0,), (0,)), ((), ())), preferred_element_type=F32
        )
        return split_parts(sums * sums, 2)

    ahead = [products(0), products(1)]
    for c in range(col_count):
        high, low = ahead.pop(0)
        if c + 2 < col_count:
            ahead.append(products(c + 2))
        smooth = jnp.dot(
            circulant_ref[c],
            jnp.concatenate([high, low, high], axis=0),
            preferred_element_type=F32,
        )
        early_ref[:, c, :] = smooth[:early]
        late_ref[:, c, :] = smooth[early:]


def filtered_products(pencils, at_points, circulant, early):
    col_count, bands, planes = pencils.shape
    count = at_points.shape[1]
    late = planes - early
    chunk = 256
    return pl.pallas_call(
        filter_kernel,
        grid=(count // chunk,),
        in_specs=[
            pl.BlockSpec(memory_space=pltpu.VMEM),
            pl.BlockSpec((bands, chunk), lambda i: (0, i)),
            pl.BlockSpec(memory_space=pltpu.VMEM),
        ],
        out_specs=[
            pl.BlockSpec((early, col_count, chunk), lambda i: (0, 0, i)),
            pl.BlockSpec((late, col_count, chunk), lambda i: (0, 0, i)),
        ],
        out_shape=[
            pltpu.HBM((early, col_count, count), F32),
            pltpu.HBM((late, col_count, count), F32),
        ],
        compiler_params=pltpu.CompilerParams(vmem_limit_bytes=28 << 20),
        cost_estimate=pl.CostEstimate(
            flops=8 * col_count * planes * bands * count, bytes_accessed=10 << 20, transcendentals=0
        ),
    )(pencils, at_points, circulant)


def fit_rows(rows, high_ref, low_ref):
    high, low = split_parts(rows, 2)
    dot = functools.partial(jnp.dot, preferred_element_type=F32)
    return (
        dot(high, high_ref[...]) + (dot(low, high_ref[...]) + dot(high, low_ref[...]))
    ).astype(BF16)


def early_fit_kernel(rows_ref, high_ref, low_ref, out_ref):
    planes, cols, count = out_ref.shape
    rows = jnp.concatenate(
        [rows_ref[:, z].reshape(cols, count) for z in range(planes)], axis=0
    )
    out_ref[...] = fit_rows(rows, high_ref, low_ref).reshape(planes, cols, count)


def early_fit(slab, high, low, total_planes):
    sources, early, col_count, count = slab.shape
    block = 2
    whole = pl.BlockSpec((count, count), lambda i: (0, 0))
    return pl.pallas_call(
        early_fit_kernel,
        grid=(early // block,),
        in_specs=[
            pl.BlockSpec((sources, block, col_count, count), lambda i: (0, i, 0, 0)),
            whole,
            whole,
        ],
        out_specs=pl.BlockSpec((block, sources * col_count, count), lambda i: (i, 0, 0)),
        out_shape=jax.ShapeDtypeStruct((total_planes, sources * col_count, count), BF16),
        compiler_params=pltpu.CompilerParams(vmem_limit_bytes=24 << 20),
        cost_estimate=pl.CostEstimate(
            flops=6 * slab.size * count, bytes_accessed=10 << 20, transcendentals=0
        ),
    )(slab, high, low)


def place_late_kernel(late_ref, _, out_ref):
    planes, cols, count = out_ref.shape
    first = pl.program_id(0) * planes
    for z in range(planes):
        out_ref[z] = late_ref[:, first + z].astype(F32).reshape(cols, count).astype(BF16)


def place_late(late, fitted):
    sources, planes, col_count, count = late.shape
    block = 2
    first = (fitted.shape[0] - planes) // block
    return pl.pallas_call(
        place_late_kernel,
        grid=(planes // block,),
        in_specs=[
            pl.BlockSpec(memory_space=pltpu.VMEM),
            pl.BlockSpec(memory_space=pl.ANY),
        ],
        out_specs=pl.BlockSpec((block, sources * col_count, count), lambda i: (first + i, 0, 0)),
        out_shape=jax.ShapeDtypeStruct(fitted.shape, BF16),
        input_output_aliases={1: 0},
        compiler_params=pltpu.CompilerParams(vmem_limit_bytes=12 << 20),
        cost_estimate=pl.CostEstimate(flops=0, bytes_accessed=2 * late.size * 2, transcendentals=0),
    )(late, fitted)


def per_device(orbitals, points, coulomb):
    gz_count, gy_count = lax.axis_size("gz"), lax.axis_size("gy")
    planes, columns = coulomb.shape
    col_pencil = columns // gz_count
    count = points.shape[0]
    slab_planes = planes // gz_count
    early = EARLY
    pencils, first_values, second_values, circulant = exchange(
        orbitals, points, coulomb, gz_count, gy_count, early
    )
    split = (2, orbitals.shape[0] // 2, count // 2)
    at_points = jnp.concatenate(
        [
            jnp.transpose(first_values.reshape(gy_count, gz_count, *split), (2, 1, 0, 3, 4)),
            jnp.transpose(second_values.reshape(gz_count, gy_count, *split), (2, 0, 1, 3, 4)),
        ],
        axis=4,
    ).reshape(-1, count)
    pencils = jnp.transpose(pencils.reshape(-1, col_pencil, planes), (1, 0, 2))
    first, second = filtered_products(pencils, at_points, circulant, gz_count * early)
    swap = functools.partial(
        lax.all_to_all, axis_name="gz", split_axis=0, concat_axis=0, tiled=True
    )
    slab = swap(first.reshape(gz_count, early, col_pencil, count))
    late, high, low = inverse_and_late_fit(at_points, second.reshape(-1, count))
    late = swap(late.reshape(gz_count, slab_planes - early, col_pencil, count))
    return place_late(late, early_fit(slab, high, low, slab_planes))


def solution(mesh):
    return jax.shard_map(
        per_device,
        mesh=mesh,
        in_specs=(P(("gz", "gy"), None, None), P(), P(None, "gy")),
        out_specs=P("gz", "gy", None),
        check_vma=False,
    )
```

```python
import functools

import jax
import jax.numpy as jnp
import numpy as np
from jax import lax
from jax.experimental import pallas as pl
from jax.experimental.pallas import tpu as pltpu
from jax.sharding import PartitionSpec as P

FULL = lax.Precision.HIGHEST
F32 = jnp.float32
BF16 = jnp.bfloat16
EARLY = 8


def in_hbm(array):
    return pltpu.with_memory_space_constraint(array, pltpu.HBM)


def pick_points(orbital_ref, points_ref, out_ref):
    bands, planes, columns = orbital_ref.shape
    points = points_ref[...]
    point_planes = points // columns
    point_columns = points - point_planes * columns
    count = points.shape[1]
    column_pick = (
        lax.broadcasted_iota(jnp.int32, (columns, count), 0) == point_columns
    ).astype(BF16)
    plane_pick = lax.broadcasted_iota(jnp.int32, (planes, count), 0) == point_planes
    for band in range(bands):
        picked = jnp.dot(orbital_ref[band], column_pick, preferred_element_type=F32)
        values = jnp.sum(jnp.where(plane_pick, picked, 0.0), axis=0, keepdims=True).astype(BF16)
        out_ref[0, band : band + 1, :] = values[:, : count // 2]
        out_ref[1, band : band + 1, :] = values[:, count // 2 :]


def send(source, target, send_sem, recv_sem, device):
    copy = pltpu.make_async_remote_copy(
        src_ref=source,
        dst_ref=target,
        send_sem=send_sem,
        recv_sem=recv_sem,
        device_id=device,
        device_id_type=pl.DeviceIdType.MESH,
    )
    copy.start()
    return copy


def exchange_kernel(
    gz_count,
    gy_count,
    orbital_hbm,
    points_hbm,
    coulomb_hbm,
    left_wave_hbm,
    right_wave_hbm,
    pencil_ref,
    first_value_ref,
    second_value_ref,
    circulant_ref,
    orbital_ref,
    points_ref,
    coulomb_ref,
    left_wave_ref,
    right_wave_ref,
    own_blocks,
    plane_stage,
    row_stage,
    gz_value_stage,
    gy_value_stage,
    own_values,
    first_value_sems,
    second_value_sems,
    gy_first_sems,
    gz_first_sems,
    gz_second_sems,
    gy_second_sems,
    local_sems,
):
    gz, gy = lax.axis_index("gz"), lax.axis_index("gy")
    gy_peers = [lax.rem(gy + d, gy_count) for d in range(1, gy_count)]
    gz_peers = [lax.rem(gz + d, gz_count) for d in range(1, gz_count)]
    barrier = pltpu.get_barrier_semaphore()
    for device in [(gz, peer) for peer in gy_peers] + [(peer, gy) for peer in gz_peers]:
        pl.semaphore_signal(
            barrier, inc=1, device_id=device, device_id_type=pl.DeviceIdType.MESH
        )
    load = [
        pltpu.make_async_copy(points_hbm, points_ref, local_sems.at[9]),
        pltpu.make_async_copy(orbital_hbm, orbital_ref, local_sems.at[0]),
    ]
    for copy in load:
        copy.start()
    load_waves = [
        pltpu.make_async_copy(coulomb_hbm, coulomb_ref, local_sems.at[10]),
        pltpu.make_async_copy(left_wave_hbm, left_wave_ref, local_sems.at[7]),
        pltpu.make_async_copy(right_wave_hbm, right_wave_ref, local_sems.at[8]),
    ]
    for copy in load_waves:
        copy.start()
    for copy in load:
        copy.wait()
    pick_points(orbital_ref, points_ref, own_values)
    bands, planes, columns = orbital_ref.shape
    half = bands // 2
    cols = own_blocks.shape[3]
    width = 256
    for band in range(bands):
        for first in range(0, columns, width):
            turned = orbital_ref[band, :, first : first + width].astype(F32).T
            at = first // cols
            own_blocks[band, at // gz_count : (at + width // cols) // gz_count] = (
                turned.reshape(width // cols // gz_count, gz_count, cols, planes).astype(BF16)
            )
    pl.semaphore_wait(barrier, gy_count + gz_count - 2)

    own = [
        pltpu.make_async_copy(own_values.at[0], gz_value_stage.at[gz], local_sems.at[1]),
        pltpu.make_async_copy(own_values.at[1], gy_value_stage.at[gy], local_sems.at[11]),
        pltpu.make_async_copy(
            own_blocks.at[pl.ds(0, half), gy], plane_stage.at[gy], local_sems.at[2]
        ),
        pltpu.make_async_copy(
            own_blocks.at[pl.ds(half, half), :, gz], row_stage.at[gz], local_sems.at[3]
        ),
    ]
    for copy in own:
        copy.start()
    values = [
        send(
            own_values.at[0],
            gz_value_stage.at[gz],
            first_value_sems.at[0, 0, i],
            first_value_sems.at[0, 1, i],
            (peer, gy),
        )
        for i, peer in enumerate(gz_peers)
    ] + [
        send(
            own_values.at[1],
            gy_value_stage.at[gy],
            first_value_sems.at[1, 0, i],
            first_value_sems.at[1, 1, i],
            (gz, peer),
        )
        for i, peer in enumerate(gy_peers)
    ]
    lower = [
        send(
            own_blocks.at[pl.ds(0, half), peer],
            plane_stage.at[gy],
            gy_first_sems.at[0, i],
            gy_first_sems.at[1, i],
            (gz, peer),
        )
        for i, peer in enumerate(gy_peers)
    ]
    upper = [
        send(
            own_blocks.at[pl.ds(half, half), :, peer],
            row_stage.at[gz],
            gz_first_sems.at[0, i],
            gz_first_sems.at[1, i],
            (peer, gy),
        )
        for i, peer in enumerate(gz_peers)
    ]
    for copy in own:
        copy.wait()
    for copy in values:
        copy.wait_recv()
    values_on = [
        send(
            gz_value_stage,
            first_value_ref.at[gy],
            second_value_sems.at[0, 0, i],
            second_value_sems.at[0, 1, i],
            (gz, peer),
        )
        for i, peer in enumerate(gy_peers)
    ] + [
        send(
            gy_value_stage,
            second_value_ref.at[gz],
            second_value_sems.at[1, 0, i],
            second_value_sems.at[1, 1, i],
            (peer, gy),
        )
        for i, peer in enumerate(gz_peers)
    ]
    for copy in lower:
        copy.wait_recv()
    lower_on = [
        send(
            plane_stage.at[:, :, peer],
            pencil_ref.at[0, gz],
            gz_second_sems.at[0, i],
            gz_second_sems.at[1, i],
            (peer, gy),
        )
        for i, peer in enumerate(gz_peers)
    ]
    for copy in upper:
        copy.wait_recv()
    upper_on = [
        send(
            row_stage.at[:, :, peer],
            pencil_ref.at[1, :, gy],
            gy_second_sems.at[0, i],
            gy_second_sems.at[1, i],
            (gz, peer),
        )
        for i, peer in enumerate(gy_peers)
    ]
    own_on = [
        pltpu.make_async_copy(gz_value_stage, first_value_ref.at[gy], local_sems.at[4]),
        pltpu.make_async_copy(gy_value_stage, second_value_ref.at[gz], local_sems.at[12]),
        pltpu.make_async_copy(plane_stage.at[:, :, gz], pencil_ref.at[0, gz], local_sems.at[5]),
        pltpu.make_async_copy(row_stage.at[:, :, gy], pencil_ref.at[1, :, gy], local_sems.at[6]),
    ]
    for copy in own_on:
        copy.start()
    for copy in load_waves:
        copy.wait()
    all_cols = coulomb_ref.shape[1]
    own_cols = lax.broadcasted_iota(jnp.int32, (cols, all_cols), 0) + gz * cols
    pick = (lax.broadcasted_iota(jnp.int32, (cols, all_cols), 1) == own_cols).astype(F32)
    weights = lax.dot_general(
        pick,
        coulomb_ref[...],
        (((1,), (1,)), ((), ())),
        precision=FULL,
        preferred_element_type=F32,
    ) * (1.0 / planes)
    weights = jnp.concatenate([weights, weights], axis=1)
    for c in range(cols):
        high, low = split_parts(
            jnp.dot(
                left_wave_ref[...] * weights[c : c + 1, :],
                right_wave_ref[...],
                precision=FULL,
                preferred_element_type=F32,
            ),
            2,
        )
        circulant_ref[c] = jnp.concatenate([high, high, low], axis=1)
    for copy in own_on:
        copy.wait()
    for copy in values + lower + upper:
        copy.wait_send()
    for copy in values_on + lower_on + upper_on:
        copy.wait()


def exchange(orbitals, points, coulomb, gz_count, gy_count, early):
    bands, planes, columns = orbitals.shape
    count = points.shape[0]
    cols = coulomb.shape[1] // gz_count
    half = bands // 2
    slab = planes // gz_count
    z = np.arange(planes)
    order = z.reshape(gz_count, slab)
    order = np.concatenate([order[:, :early].ravel(), order[:, early:].ravel()])
    angles = 2.0 * np.pi / planes * (z[:, None] * z % planes)
    waves = np.concatenate([np.cos(angles), np.sin(angles)], axis=1)
    vmem, hbm = (pl.BlockSpec(memory_space=space) for space in (pltpu.VMEM, pltpu.HBM))
    dma = pltpu.SemaphoreType.DMA
    return pl.pallas_call(
        functools.partial(exchange_kernel, gz_count, gy_count),
        in_specs=[hbm, hbm, hbm, hbm, hbm],
        out_specs=(vmem, vmem, vmem, vmem),
        out_shape=(
            jax.ShapeDtypeStruct((2, gz_count, gy_count, half, cols, planes), BF16),
            jax.ShapeDtypeStruct((gy_count, gz_count, bands, count // 2), BF16),
            jax.ShapeDtypeStruct((gz_count, gy_count, bands, count // 2), BF16),
            jax.ShapeDtypeStruct((cols, planes, 3 * planes), BF16),
        ),
        scratch_shapes=[
            pltpu.VMEM((bands, planes, columns), BF16),
            pltpu.VMEM((1, count), jnp.int32),
            pltpu.VMEM(coulomb.shape, F32),
            pltpu.VMEM((planes, 2 * planes), F32),
            pltpu.VMEM((2 * planes, planes), F32),
            pltpu.VMEM((bands, gy_count, gz_count, cols, planes), BF16),
            pltpu.VMEM((gy_count, half, gz_count, cols, planes), BF16),
            pltpu.VMEM((gz_count, half, gy_count, cols, planes), BF16),
            pltpu.VMEM((gz_count, bands, count // 2), BF16),
            pltpu.VMEM((gy_count, bands, count // 2), BF16),
            pltpu.VMEM((2, bands, count // 2), BF16),
            dma((2, 2, gz_count - 1)),
            dma((2, 2, gz_count - 1)),
            dma((2, gy_count - 1)),
            dma((2, gz_count - 1)),
            dma((2, gz_count - 1)),
            dma((2, gy_count - 1)),
            dma((13,)),
        ],
        compiler_params=pltpu.CompilerParams(
            collective_id=0, has_side_effects=True, vmem_limit_bytes=28 << 20
        ),
    )(
        in_hbm(orbitals),
        in_hbm(points.reshape(1, count)),
        in_hbm(coulomb),
        in_hbm(jnp.asarray(waves[order], F32)),
        in_hbm(jnp.asarray(waves.T, F32)),
    )


def split_parts(values, count):
    parts = []
    for _ in range(count):
        part = values.astype(BF16)
        parts.append(part)
        values = values - part.astype(F32)
    return parts


def full_dot(left, right):
    return jnp.dot(left_stack(left), right_stack(right), preferred_element_type=F32)


def left_stack(left):
    high, middle, low = split_parts(left, 3)
    return jnp.concatenate([high, high, middle, high, low, middle], axis=1)


def right_stack(right):
    high, middle, low = split_parts(right, 3)
    return jnp.concatenate([high, middle, high, low, high, middle], axis=0)


def tree_sum(terms):
    while len(terms) > 1:
        terms = [sum(terms[i : i + 2][1:], terms[i]) for i in range(0, len(terms), 2)]
    return terms[0]


def eliminate_rows(rows, first, lane, sub):
    shape = rows.shape
    columns = [jnp.broadcast_to(rows[:, first + j : first + j + 1], shape) for j in range(8)]
    cell = {
        (i, j): jnp.broadcast_to(columns[j][i : i + 1, :], shape)
        for j in range(8)
        for i in range(j + 1)
    }
    for k in range(8):
        recip = 1.0 / cell[k, k]
        side = {i: cell[min(i, k), max(i, k)] for i in range(8) if i != k}
        scaled = {i: side[i] * recip for i in side}
        swept = {}
        for i, j in cell:
            if i == k and j == k:
                swept[i, j] = -recip
            elif i == k or j == k:
                swept[i, j] = scaled[j if i == k else i]
            else:
                swept[i, j] = cell[i, j] - side[i] * scaled[j]
        cell = swept
    inside = (lane >= first) & (lane < first + 8)
    source = [
        jnp.where(
            inside,
            jnp.where(lane == first + j, -1.0, 0.0),
            -jnp.broadcast_to(rows[j : j + 1, :], shape),
        )
        for j in range(8)
    ]
    results = [
        tree_sum([cell[min(i, j), max(i, j)] * source[j] for j in range(8)]) for i in range(8)
    ]
    panel = results[0]
    for i in range(1, 8):
        panel = jnp.where(sub == i, results[i], panel)
    return results, panel, inside


def small_inverse(block):
    size = block.shape[0]
    tiles = [block[i : i + 8, :] for i in range(0, size, 8)]
    lane = lax.broadcasted_iota(jnp.int32, (8, size), 1)
    sub = lax.broadcasted_iota(jnp.int32, (8, size), 0)
    for at in range(len(tiles)):
        first = at * 8
        following = [i for i in (at + 1, at + 2) if i < len(tiles)]
        rest = [i for i in range(len(tiles)) if i != at and i not in following]
        stack = jnp.concatenate([tiles[i] for i in rest], axis=0)
        wide_lane = lax.broadcasted_iota(jnp.int32, stack.shape, 1)
        kept = jnp.where((wide_lane >= first) & (wide_lane < first + 8), 0.0, stack)
        wide = left_stack(stack[:, first : first + 8])
        results, panel, inside = eliminate_rows(tiles[at], first, lane, sub)
        for other in following:
            terms = [
                jnp.broadcast_to(tiles[other][:, first + j : first + j + 1], (8, size)) * results[j]
                for j in range(8)
            ]
            tiles[other] = jnp.where(inside, 0.0, tiles[other]) - tree_sum(terms)
        stack = kept - jnp.dot(wide, right_stack(panel), preferred_element_type=F32)
        for place, i in enumerate(rest):
            tiles[i] = stack[place * 8 : place * 8 + 8, :]
        tiles[at] = panel
    return jnp.concatenate(tiles, axis=0)


def inverse_kernel(
    width, point_ref, late_ref, fitted_ref, high_out, low_out, work, high_ref, low_ref
):
    size = work.shape[0]
    block = 256

    @pl.when(pl.program_id(0) == 0)
    def _():
        for first in range(0, size, block):
            base = lax.dot_general(
                point_ref[:, first : first + block],
                point_ref[...],
                (((0,), (0,)), ((), ())),
                preferred_element_type=F32,
            )
            work[first : first + block, :] = base * base

        def eliminate(k, carry):
            at = pl.ds(pl.multiple_of(k * width, width), width)
            pivot = small_inverse(work[at, at])
            work[at, :] = full_dot(pivot, work[at, :])
            work[at, at] = pivot
            panel = work[at, :]
            stacked = right_stack(panel)
            wide = left_stack(work[:, at])
            work[:, at] = jnp.zeros((size, width), F32)
            for first in range(0, size, block):
                columns = slice(first, first + block)
                change = jnp.dot(wide, stacked[:, columns], preferred_element_type=F32)
                work[:, columns] = work[:, columns] - change
            work[at, :] = panel
            return carry

        lax.fori_loop(0, size // width, eliminate, 0)
        for first in range(0, size, block):
            rows = slice(first, first + block)
            high, low = split_parts(work[rows, :], 2)
            high_ref[rows, :] = high
            low_ref[rows, :] = low

    @pl.when(pl.program_id(0) > 0)
    def _():
        rows = pl.ds(pl.multiple_of((pl.program_id(0) - 1) * block, block), block)
        high_out[...] = high_ref[rows, :]
        low_out[...] = low_ref[rows, :]
        fitted_ref[...] = fit_rows(late_ref[...], high_ref, low_ref)


def inverse_and_late_fit(at_points, late):
    size = at_points.shape[1]
    block = 256
    steps = late.shape[0] // block
    assert steps == size // block
    rows = pl.BlockSpec((block, size), lambda i: (jnp.maximum(i - 1, 0), 0))
    return pl.pallas_call(
        functools.partial(inverse_kernel, 128),
        grid=(1 + steps,),
        in_specs=[pl.BlockSpec(memory_space=pltpu.VMEM), rows],
        out_specs=(rows, rows, rows),
        out_shape=(
            pltpu.HBM(late.shape, BF16),
            pltpu.HBM((size, size), BF16),
            pltpu.HBM((size, size), BF16),
        ),
        scratch_shapes=[
            pltpu.VMEM((size, size), F32),
            pltpu.VMEM((size, size), BF16),
            pltpu.VMEM((size, size), BF16),
        ],
        compiler_params=pltpu.CompilerParams(vmem_limit_bytes=36 << 20),
        cost_estimate=pl.CostEstimate(
            flops=60 * size**3, bytes_accessed=8 * size * size, transcendentals=0
        ),
    )(at_points, in_hbm(late))


def filter_kernel(pencil_ref, point_ref, circulant_ref, early_ref, late_ref):
    early = early_ref.shape[0]
    col_count = pencil_ref.shape[0]

    def products(c):
        sums = lax.dot_general(
            pencil_ref[c], point_ref[...], (((0,), (0,)), ((), ())), preferred_element_type=F32
        )
        return split_parts(sums * sums, 2)

    ahead = [products(0), products(1)]
    for c in range(col_count):
        high, low = ahead.pop(0)
        if c + 2 < col_count:
            ahead.append(products(c + 2))
        smooth = jnp.dot(
            circulant_ref[c],
            jnp.concatenate([high, low, high], axis=0),
            preferred_element_type=F32,
        )
        early_ref[:, c, :] = smooth[:early]
        late_ref[:, c, :] = smooth[early:]


def filtered_products(pencils, at_points, circulant, early):
    col_count, bands, planes = pencils.shape
    count = at_points.shape[1]
    late = planes - early
    chunk = 256
    return pl.pallas_call(
        filter_kernel,
        grid=(count // chunk,),
        in_specs=[
            pl.BlockSpec(memory_space=pltpu.VMEM),
            pl.BlockSpec((bands, chunk), lambda i: (0, i)),
            pl.BlockSpec(memory_space=pltpu.VMEM),
        ],
        out_specs=[
            pl.BlockSpec((early, col_count, chunk), lambda i: (0, 0, i)),
            pl.BlockSpec((late, col_count, chunk), lambda i: (0, 0, i)),
        ],
        out_shape=[
            pltpu.HBM((early, col_count, count), F32),
            pltpu.HBM((late, col_count, count), F32),
        ],
        compiler_params=pltpu.CompilerParams(vmem_limit_bytes=28 << 20),
        cost_estimate=pl.CostEstimate(
            flops=8 * col_count * planes * bands * count, bytes_accessed=10 << 20, transcendentals=0
        ),
    )(pencils, at_points, circulant)


def fit_rows(rows, high_ref, low_ref):
    high, low = split_parts(rows, 2)
    dot = functools.partial(jnp.dot, preferred_element_type=F32)
    return (
        dot(high, high_ref[...]) + (dot(low, high_ref[...]) + dot(high, low_ref[...]))
    ).astype(BF16)


def early_fit_kernel(rows_ref, high_ref, low_ref, out_ref):
    planes, cols, count = out_ref.shape
    rows = jnp.concatenate(
        [rows_ref[:, z].reshape(cols, count) for z in range(planes)], axis=0
    )
    out_ref[...] = fit_rows(rows, high_ref, low_ref).reshape(planes, cols, count)


def early_fit(slab, high, low, total_planes):
    sources, early, col_count, count = slab.shape
    block = 2
    whole = pl.BlockSpec((count, count), lambda i: (0, 0))
    return pl.pallas_call(
        early_fit_kernel,
        grid=(early // block,),
        in_specs=[
            pl.BlockSpec((sources, block, col_count, count), lambda i: (0, i, 0, 0)),
            whole,
            whole,
        ],
        out_specs=pl.BlockSpec((block, sources * col_count, count), lambda i: (i, 0, 0)),
        out_shape=jax.ShapeDtypeStruct((total_planes, sources * col_count, count), BF16),
        compiler_params=pltpu.CompilerParams(vmem_limit_bytes=24 << 20),
        cost_estimate=pl.CostEstimate(
            flops=6 * slab.size * count, bytes_accessed=10 << 20, transcendentals=0
        ),
    )(slab, high, low)


def place_late_kernel(late_ref, _, out_ref):
    planes, cols, count = out_ref.shape
    first = pl.program_id(0) * planes
    for z in range(planes):
        out_ref[z] = late_ref[:, first + z].astype(F32).reshape(cols, count).astype(BF16)


def place_late(late, fitted):
    sources, planes, col_count, count = late.shape
    block = 1
    first = (fitted.shape[0] - planes) // block
    return pl.pallas_call(
        place_late_kernel,
        grid=(planes // block,),
        in_specs=[
            pl.BlockSpec(memory_space=pltpu.VMEM),
            pl.BlockSpec(memory_space=pl.ANY),
        ],
        out_specs=pl.BlockSpec((block, sources * col_count, count), lambda i: (first + i, 0, 0)),
        out_shape=jax.ShapeDtypeStruct(fitted.shape, BF16),
        input_output_aliases={1: 0},
        compiler_params=pltpu.CompilerParams(vmem_limit_bytes=12 << 20),
        cost_estimate=pl.CostEstimate(flops=0, bytes_accessed=2 * late.size * 2, transcendentals=0),
    )(late, fitted)


def per_device(orbitals, points, coulomb):
    gz_count, gy_count = lax.axis_size("gz"), lax.axis_size("gy")
    planes, columns = coulomb.shape
    col_pencil = columns // gz_count
    count = points.shape[0]
    slab_planes = planes // gz_count
    early = EARLY
    pencils, first_values, second_values, circulant = exchange(
        orbitals, points, coulomb, gz_count, gy_count, early
    )
    split = (2, orbitals.shape[0] // 2, count // 2)
    at_points = jnp.concatenate(
        [
            jnp.transpose(first_values.reshape(gy_count, gz_count, *split), (2, 1, 0, 3, 4)),
            jnp.transpose(second_values.reshape(gz_count, gy_count, *split), (2, 0, 1, 3, 4)),
        ],
        axis=4,
    ).reshape(-1, count)
    pencils = jnp.transpose(pencils.reshape(-1, col_pencil, planes), (1, 0, 2))
    first, second = filtered_products(pencils, at_points, circulant, gz_count * early)
    swap = functools.partial(
        lax.all_to_all, axis_name="gz", split_axis=0, concat_axis=0, tiled=True
    )
    slab = swap(first.reshape(gz_count, early, col_pencil, count))
    late, high, low = inverse_and_late_fit(at_points, second.reshape(-1, count))
    late = swap(late.reshape(gz_count, slab_planes - early, col_pencil, count))
    return place_late(late, early_fit(slab, high, low, slab_planes))


def solution(mesh):
    return jax.shard_map(
        per_device,
        mesh=mesh,
        in_specs=(P(("gz", "gy"), None, None), P(), P(None, "gy")),
        out_specs=P("gz", "gy", None),
        check_vma=False,
    )
```
